256 devices in a mesh: feat: 16 (over z, x_hi), tok: 16 (over x_lo, y, core).
Axes of the slice: x: 4 (x_hi: 2, x_lo: 2; x = x_hi * 2 + x_lo), y: 4, z: 8, core: 2. Of those that a mesh axis runs over, the one named last changes fastest.
Arguments:
- activations: bfloat16 [8192, 32768], P('tok', 'feat'), may hold values from -48 to 48
- pattern: int32 [192, 2], replicated, may hold values from 0 to 63, as said below
- block_slot: int32 [192], replicated, may hold values from 0 to 191
Outputs:
- gram_blocks: float32 [512, 192, 512], P('tok', 'feat')
The draws below stay inside these ranges and needn't reach their ends.
Inputs may be any that keep to these rules, and one draw needn't show every extreme that they name: `pattern`: block_slot is a permutation of the slots. The row block of the listed block stored at slot s lies in the panel of feat index s // 12 (blocks k * 4 to k * 4 + 3 for index k). Among the column blocks of the 12 slots of one feat index, at most 1 lie in any one index's panel, and exactly 1 in some.
All inputs are finite; a program needn't handle non-finite values.
Results may differ from the reference program's by a relative error of at most 0.0003.
Values may be sent and summed in bfloat16 or wider, within the bound.
A program may use at most 128 MiB of HBM per device.

```python
import jax
import jax.numpy as jnp
from jax import lax

F = 32768
BLK = 512
NB_DEV = 12
TOKENS = 8192
NLIST = 192
N_FEAT = 16


def shared_plan(key):
    base = jax.random.fold_in(key, 11)
    perm_key, col_key, row_key, slot_key = jax.random.split(base, 4)
    holder_perms = jax.vmap(lambda one_key: jax.random.permutation(one_key, N_FEAT))(jax.random.split(perm_key, N_FEAT))
    panel_blocks = F // (BLK * N_FEAT)
    needs = jnp.arange(NB_DEV) % N_FEAT
    holders = holder_perms[:, needs]
    columns = holders * panel_blocks + jax.random.randint(col_key, (N_FEAT, NB_DEV), 0, panel_blocks)
    rows = jnp.arange(N_FEAT)[:, None] * panel_blocks + jax.random.randint(row_key, (N_FEAT, NB_DEV), 0, panel_blocks)
    ordered = jnp.stack([rows, columns], -1).reshape(N_FEAT * NB_DEV, 2).astype(jnp.int32)
    block_slot = jax.random.permutation(slot_key, N_FEAT * NB_DEV).astype(jnp.int32)
    return (ordered[block_slot], block_slot)


def draw_pattern(key, part):
    return shared_plan(key)[0]


def draw_block_slot(key, part):
    return shared_plan(key)[1]


def block_levels(rng, dims, pieces, low, largest):
    level, own = 1.0, jax.random.fold_in(rng, 6)
    for axis_at, shards_of in pieces:
        draws = jnp.exp(jax.random.uniform(jax.random.fold_in(own, axis_at), (shards_of,), jnp.float32, low / len(pieces), largest / len(pieces)))
        level = level * jnp.repeat(draws, dims[axis_at] // shards_of).reshape([-1 if axis == axis_at else 1 for axis in range(len(dims))])
    return level


def scatter_about(rng, shape, spread, reach, pieces=(), kind=jnp.bfloat16):
    array = jax.random.normal(rng, shape, jnp.float32) * spread
    if len(pieces) > 0:
        array = block_levels(rng, shape, pieces, -0.22, 0.18) * array
    return jnp.clip(array, min=-reach, max=reach).astype(kind)


def setup_inputs(seed: int = 0) -> dict:
    keys = jax.random.split(jax.random.key(seed), 4)
    return {
        "activations": scatter_about(keys[0], (TOKENS, F), 8.0, 48.0, ((0, 16), (1, 16))),
        "pattern": draw_pattern(jax.random.fold_in(keys[3], 71), 0),
        "block_slot": draw_block_slot(jax.random.fold_in(keys[3], 71), 0),
    }


def reference(activations, pattern, block_slot):
    scale = 1.0 / TOKENS

    def one_block(pair):
        row_part = lax.dynamic_slice_in_dim(activations, (pair[0] * BLK).astype(jnp.int32), BLK, 1)
        col_part = lax.dynamic_slice_in_dim(activations, (pair[1] * BLK).astype(jnp.int32), BLK, 1)
        return jnp.dot(row_part.T, col_part, preferred_element_type=jnp.float32) * scale

    blocks = lax.map(one_block, pattern)
    stored = jnp.zeros((NLIST, BLK, BLK), jnp.float32).at[block_slot].set(blocks)
    return jnp.transpose(stored, (1, 0, 2))
```

```python
import jax
import jax.numpy as jnp
from jax import lax
from jax.sharding import PartitionSpec as P

BLK = 512
CHUNKS = 4


def body(activations, pattern, block_slot):
    tok_rows, width = activations.shape
    feat_count = lax.axis_size("feat")
    tok_count = lax.axis_size("tok")
    my_index = lax.axis_index("feat")
    panel_blocks = width // BLK
    list_length = pattern.shape[0]
    per_device = list_length // feat_count
    scale = 1.0 / (tok_rows * tok_count)
    ordered = jnp.zeros_like(pattern).at[block_slot].set(pattern)
    pairs = ordered.reshape(feat_count, per_device, 2)
    holder = pairs[:, :, 1] // panel_blocks
    local_column = pairs[:, :, 1] % panel_blocks
    match = holder == my_index
    picked = jnp.sum(jnp.where(match, local_column, 0), axis=1)
    my_pairs = lax.dynamic_index_in_dim(pairs, my_index, 0, keepdims=False)
    my_holder = my_pairs[:, 1] // panel_blocks
    blocks_local = activations.reshape(tok_rows, panel_blocks, BLK)
    row_blocks = jnp.take(blocks_local, my_pairs[:, 0] % panel_blocks, axis=1)
    w = BLK // CHUNKS
    outs = []
    for c in range(CHUNKS):
        part = blocks_local[:, :, c * w:(c + 1) * w]
        send = jnp.take(part, picked, axis=1)
        received = lax.all_to_all(send, "feat", split_axis=1, concat_axis=1, tiled=True)
        column_blocks = jnp.take(received, my_holder, axis=1)
        g = jnp.einsum("tki,tkj->ikj", row_blocks, column_blocks, preferred_element_type=jnp.float32) * scale
        outs.append(lax.psum_scatter(g, "tok", scatter_dimension=0, tiled=True))
    return jnp.concatenate(outs, axis=2)


def solution(mesh):
    placed = (P("tok", "feat"), P(), P())
    return jax.shard_map(
        body, mesh=mesh, in_specs=placed, out_specs=P("tok", "feat", None), check_vma=False
    )
```

```python
import functools

import jax
import jax.numpy as jnp
from jax import lax
from jax.experimental import pallas as pl
from jax.experimental.pallas import tpu as pltpu
from jax.sharding import PartitionSpec as P

BLK = 512
MESH = pl.DeviceIdType.MESH


def exchange_kernel(n, send_ref, recv_ref, send_sem, recv_sem, local_sem):
    me = lax.axis_index("feat")
    barrier = pltpu.get_barrier_semaphore()
    for k in range(1, n):
        peer = lax.rem(me + k, n)
        pl.semaphore_signal(barrier, 1, device_id={"feat": peer}, device_id_type=MESH)
    pl.semaphore_wait(barrier, n - 1)
    local = pltpu.make_async_copy(send_ref.at[me], recv_ref.at[me], local_sem)
    local.start()
    copies = []
    for k in range(1, n):
        peer = lax.rem(me + k, n)
        copy = pltpu.make_async_remote_copy(
            src_ref=send_ref.at[peer],
            dst_ref=recv_ref.at[me],
            send_sem=send_sem.at[k],
            recv_sem=recv_sem.at[k],
            device_id={"feat": peer},
            device_id_type=MESH,
        )
        copy.start()
        copies.append(copy)
    for copy in copies:
        copy.wait()
    local.wait()


def exchange(send):
    n = send.shape[0]
    return pl.pallas_call(
        functools.partial(exchange_kernel, n),
        out_shape=jax.ShapeDtypeStruct(send.shape, send.dtype),
        in_specs=[pl.BlockSpec(memory_space=pl.ANY)],
        out_specs=pl.BlockSpec(memory_space=pl.ANY),
        scratch_shapes=[
            pltpu.SemaphoreType.DMA((n,)),
            pltpu.SemaphoreType.DMA((n,)),
            pltpu.SemaphoreType.DMA,
        ],
        compiler_params=pltpu.CompilerParams(collective_id=0, has_side_effects=True),
    )(send)


def body(activations, pattern, block_slot):
    tok_rows, width = activations.shape
    feat_count = lax.axis_size("feat")
    tok_count = lax.axis_size("tok")
    my_index = lax.axis_index("feat")
    panel_blocks = width // BLK
    list_length = pattern.shape[0]
    per_device = list_length // feat_count
    scale = 1.0 / (tok_rows * tok_count)
    ordered = jnp.zeros_like(pattern).at[block_slot].set(pattern)
    pairs = ordered.reshape(feat_count, per_device, 2)
    holder = pairs[:, :, 1] // panel_blocks
    local_column = pairs[:, :, 1] % panel_blocks
    picked = jnp.sum(jnp.where(holder == my_index, local_column, 0), axis=1)
    my_pairs = lax.dynamic_index_in_dim(pairs, my_index, 0, keepdims=False)
    my_holder = my_pairs[:, 1] // panel_blocks
    blocks_local = activations.reshape(tok_rows, panel_blocks, BLK).transpose(1, 0, 2)
    row_blocks = jnp.take(blocks_local, my_pairs[:, 0] % panel_blocks, axis=0)
    send = jnp.take(blocks_local, picked, axis=0)
    received = exchange(send)
    column_blocks = jnp.take(received, my_holder, axis=0)
    g = jnp.einsum("kti,ktj->ikj", row_blocks, column_blocks, preferred_element_type=jnp.float32) * scale
    return lax.psum_scatter(g, "tok", scatter_dimension=0, tiled=True)


def solution(mesh):
    placed = (P("tok", "feat"), P(), P())
    return jax.shard_map(
        body, mesh=mesh, in_specs=placed, out_specs=P("tok", "feat", None), check_vma=False
    )
```

```python
import functools

import jax
import jax.numpy as jnp
from jax import lax
from jax.experimental import pallas as pl
from jax.experimental.pallas import tpu as pltpu
from jax.sharding import PartitionSpec as P

BLK = 512
CHUNKS = 4
MESH = pl.DeviceIdType.MESH


def fused_kernel(n_feat, n_tok, chunks, scale,
                 holder_ref, send_ref, rows_ref, out_ref, *scratch):
    recv = scratch[:chunks]
    gbuf, sta, stb, accbuf, fsend, frecv, flocal, asend, arecv, alocal, bsend, brecv = scratch[chunks:]
    slots, width, tokens = rows_ref.shape
    w = width // chunks
    group = n_tok // 2
    piece = width // n_tok
    me = lax.axis_index("feat")
    t = lax.axis_index("tok")
    x = t // group
    j = t % group
    partner = (1 - x) * group + j

    barrier = pltpu.get_barrier_semaphore()
    for k in range(1, n_feat):
        pl.semaphore_signal(barrier, 1, device_id={"feat": lax.rem(me + k, n_feat)}, device_id_type=MESH)
    for o in range(1, group):
        pl.semaphore_signal(barrier, 1, device_id={"tok": x * group + lax.rem(j + o, group)}, device_id_type=MESH)
    pl.semaphore_signal(barrier, 1, device_id={"tok": partner}, device_id_type=MESH)
    pl.semaphore_wait(barrier, n_feat - 1 + group - 1 + 1)

    def feat_copies(c):
        cols = pl.ds(c * w, w)
        local = pltpu.make_async_copy(send_ref.at[me, :, cols], recv[c].at[me], flocal.at[c])
        copies = [local]
        for k in range(1, n_feat):
            peer = lax.rem(me + k, n_feat)
            copies.append(pltpu.make_async_remote_copy(
                src_ref=send_ref.at[peer, :, cols],
                dst_ref=recv[c].at[me],
                send_sem=fsend.at[c, k],
                recv_sem=frecv.at[c, k],
                device_id={"feat": peer},
                device_id_type=MESH,
            ))
        return copies

    pending = feat_copies(0)
    for cp in pending:
        cp.start()
    for c in range(chunks):
        for cp in pending:
            cp.wait()
        if c + 1 < chunks:
            pending = feat_copies(c + 1)
            for cp in pending:
                cp.start()

        def gram_one(k, carry):
            q = recv[c][holder_ref[k]]
            g = jnp.dot(rows_ref[k], q, preferred_element_type=jnp.float32) * scale
            for xx in range(2):
                for m in range(group):
                    r0 = (xx * group + m) * piece
                    gbuf[m, xx, k] = g[r0:r0 + piece, :]
            return carry

        lax.fori_loop(0, slots, gram_one, 0)

        own = pltpu.make_async_copy(gbuf.at[j], sta.at[c, j], alocal.at[c])
        own.start()
        a_copies = []
        for o in range(1, group):
            dest = lax.rem(j + o, group)
            cp = pltpu.make_async_remote_copy(
                src_ref=gbuf.at[dest],
                dst_ref=sta.at[c, j],
                send_sem=asend.at[c, o],
                recv_sem=arecv.at[c, o],
                device_id={"tok": x * group + dest},
                device_id_type=MESH,
            )
            cp.start()
            a_copies.append(cp)
        own.wait()
        for cp in a_copies:
            cp.wait()
        acc = sta[c, 0]
        for m in range(1, group):
            acc = acc + sta[c, m]
        accbuf[...] = acc
        bcp = pltpu.make_async_remote_copy(
            src_ref=accbuf.at[1 - x],
            dst_ref=stb.at[c],
            send_sem=bsend.at[c],
            recv_sem=brecv.at[c],
            device_id={"tok": partner},
            device_id_type=MESH,
        )
        bcp.start()
        bcp.wait()
        out_ref[:, :, pl.ds(c * w, w)] = accbuf[x] + stb[c]


def fused(holder, send, rows_t, n_feat, n_tok, scale):
    slots, width, tokens = rows_t.shape
    w = width // CHUNKS
    group = n_tok // 2
    piece = width // n_tok
    kernel = functools.partial(fused_kernel, n_feat, n_tok, CHUNKS, scale)
    return pl.pallas_call(
        kernel,
        out_shape=jax.ShapeDtypeStruct((slots, piece, width), jnp.float32),
        in_specs=[
            pl.BlockSpec(memory_space=pltpu.SMEM),
            pl.BlockSpec(memory_space=pl.ANY),
            pl.BlockSpec(memory_space=pltpu.VMEM),
        ],
        out_specs=pl.BlockSpec(memory_space=pltpu.VMEM),
        scratch_shapes=[pltpu.VMEM((n_feat, tokens, w), send.dtype) for _ in range(CHUNKS)] + [
            pltpu.VMEM((group, 2, slots, piece, w), jnp.float32),
            pltpu.VMEM((CHUNKS, group, 2, slots, piece, w), jnp.float32),
            pltpu.VMEM((CHUNKS, slots, piece, w), jnp.float32),
            pltpu.VMEM((2, slots, piece, w), jnp.float32),
            pltpu.SemaphoreType.DMA((CHUNKS, n_feat)),
            pltpu.SemaphoreType.DMA((CHUNKS, n_feat)),
            pltpu.SemaphoreType.DMA((CHUNKS,)),
            pltpu.SemaphoreType.DMA((CHUNKS, group)),
            pltpu.SemaphoreType.DMA((CHUNKS, group)),
            pltpu.SemaphoreType.DMA((CHUNKS,)),
            pltpu.SemaphoreType.DMA((CHUNKS,)),
            pltpu.SemaphoreType.DMA((CHUNKS,)),
        ],
        compiler_params=pltpu.CompilerParams(
            collective_id=0, has_side_effects=True, vmem_limit_bytes=60 * 1024 * 1024
        ),
    )(holder, send, rows_t)


def body(activations, pattern, block_slot):
    tok_rows, width = activations.shape
    feat_count = lax.axis_size("feat")
    tok_count = lax.axis_size("tok")
    my_index = lax.axis_index("feat")
    panel_blocks = width // BLK
    list_length = pattern.shape[0]
    per_device = list_length // feat_count
    scale = 1.0 / (tok_rows * tok_count)
    ordered = jnp.zeros_like(pattern).at[block_slot].set(pattern)
    pairs = ordered.reshape(feat_count, per_device, 2)
    holder = pairs[:, :, 1] // panel_blocks
    local_column = pairs[:, :, 1] % panel_blocks
    picked = jnp.sum(jnp.where(holder == my_index, local_column, 0), axis=1)
    my_pairs = lax.dynamic_index_in_dim(pairs, my_index, 0, keepdims=False)
    my_holder = my_pairs[:, 1] // panel_blocks
    blocks_local = activations.reshape(tok_rows, panel_blocks, BLK).transpose(1, 0, 2)
    rows_t = jnp.take(blocks_local, my_pairs[:, 0] % panel_blocks, axis=0).transpose(0, 2, 1)
    send = jnp.take(blocks_local, picked, axis=0)
    out = fused(my_holder, send, rows_t, feat_count, tok_count, scale)
    return out.transpose(1, 0, 2)


def solution(mesh):
    placed = (P("tok", "feat"), P(), P())
    return jax.shard_map(
        body, mesh=mesh, in_specs=placed, out_specs=P("tok", "feat", None), check_vma=False
    )
```

```python
import functools

import jax
import jax.numpy as jnp
from jax import lax
from jax.experimental import pallas as pl
from jax.experimental.pallas import tpu as pltpu
from jax.sharding import PartitionSpec as P

BLK = 512
CHUNKS = 4
MESH = pl.DeviceIdType.MESH


def fused_kernel(n_feat, n_tok, chunks, scale,
                 holder_ref, rowblk_ref, send_ref, act_ref, out_ref, *scratch):
    recv = scratch[:chunks]
    gbuf, sta, stb, accbuf, fsend, frecv, flocal, asend, arecv, alocal, bsend, brecv = scratch[chunks:]
    slots = holder_ref.shape[0]
    tokens, width = send_ref.shape[1], send_ref.shape[2]
    w = width // chunks
    group = n_tok // 2
    piece = width // n_tok
    me = lax.axis_index("feat")
    t = lax.axis_index("tok")
    x = t // group
    j = t % group
    partner = (1 - x) * group + j

    barrier = pltpu.get_barrier_semaphore()
    for k in range(1, n_feat):
        pl.semaphore_signal(barrier, 1, device_id={"feat": lax.rem(me + k, n_feat)}, device_id_type=MESH)
    for o in range(1, group):
        pl.semaphore_signal(barrier, 1, device_id={"tok": x * group + lax.rem(j + o, group)}, device_id_type=MESH)
    pl.semaphore_signal(barrier, 1, device_id={"tok": partner}, device_id_type=MESH)
    pl.semaphore_wait(barrier, n_feat - 1 + group - 1 + 1)

    def feat_copies(c):
        cols = pl.ds(c * w, w)
        local = pltpu.make_async_copy(send_ref.at[me, :, cols], recv[c].at[me], flocal.at[c])
        copies = [local]
        for k in range(1, n_feat):
            peer = lax.rem(me + k, n_feat)
            copies.append(pltpu.make_async_remote_copy(
                src_ref=send_ref.at[peer, :, cols],
                dst_ref=recv[c].at[me],
                send_sem=fsend.at[c, k],
                recv_sem=frecv.at[c, k],
                device_id={"feat": peer},
                device_id_type=MESH,
            ))
        return copies

    pending = feat_copies(0)
    for cp in pending:
        cp.start()
    for c in range(chunks):
        for cp in pending:
            cp.wait()
        if c + 1 < chunks:
            pending = feat_copies(c + 1)
            for cp in pending:
                cp.start()

        def gram_one(k, carry):
            q = recv[c][holder_ref[k]]
            p = act_ref[rowblk_ref[k]]
            g = lax.dot_general(
                p, q, (((0,), (0,)), ((), ())), preferred_element_type=jnp.float32
            ) * scale
            for xx in range(2):
                for m in range(group):
                    r0 = (xx * group + m) * piece
                    gbuf[m, xx, k] = g[r0:r0 + piece, :]
            return carry

        lax.fori_loop(0, slots, gram_one, 0)

        own = pltpu.make_async_copy(gbuf.at[j], sta.at[c, j], alocal.at[c])
        own.start()
        a_copies = []
        for o in range(1, group):
            dest = lax.rem(j + o, group)
            cp = pltpu.make_async_remote_copy(
                src_ref=gbuf.at[dest],
                dst_ref=sta.at[c, j],
                send_sem=asend.at[c, o],
                recv_sem=arecv.at[c, o],
                device_id={"tok": x * group + dest},
                device_id_type=MESH,
            )
            cp.start()
            a_copies.append(cp)
        own.wait()
        for cp in a_copies:
            cp.wait()
        acc = sta[c, 0]
        for m in range(1, group):
            acc = acc + sta[c, m]
        accbuf[...] = acc
        bcp = pltpu.make_async_remote_copy(
            src_ref=accbuf.at[1 - x],
            dst_ref=stb.at[c],
            send_sem=bsend.at[c],
            recv_sem=brecv.at[c],
            device_id={"tok": partner},
            device_id_type=MESH,
        )
        bcp.start()
        bcp.wait()
        out_ref[:, :, pl.ds(c * w, w)] = accbuf[x] + stb[c]


def fused(holder, rowblk, send, activations, n_feat, n_tok, scale):
    slots = holder.shape[0]
    tokens, width = send.shape[1], send.shape[2]
    w = width // CHUNKS
    group = n_tok // 2
    piece = width // n_tok
    kernel = functools.partial(fused_kernel, n_feat, n_tok, CHUNKS, scale)
    return pl.pallas_call(
        kernel,
        out_shape=jax.ShapeDtypeStruct((slots, piece, width), jnp.float32),
        in_specs=[
            pl.BlockSpec(memory_space=pltpu.SMEM),
            pl.BlockSpec(memory_space=pltpu.SMEM),
            pl.BlockSpec(memory_space=pl.ANY),
            pl.BlockSpec(memory_space=pltpu.VMEM),
        ],
        out_specs=pl.BlockSpec(memory_space=pltpu.VMEM),
        scratch_shapes=[pltpu.VMEM((n_feat, tokens, w), send.dtype) for _ in range(CHUNKS)] + [
            pltpu.VMEM((group, 2, slots, piece, w), jnp.float32),
            pltpu.VMEM((CHUNKS, group, 2, slots, piece, w), jnp.float32),
            pltpu.VMEM((CHUNKS, slots, piece, w), jnp.float32),
            pltpu.VMEM((2, slots, piece, w), jnp.float32),
            pltpu.SemaphoreType.DMA((CHUNKS, n_feat)),
            pltpu.SemaphoreType.DMA((CHUNKS, n_feat)),
            pltpu.SemaphoreType.DMA((CHUNKS,)),
            pltpu.SemaphoreType.DMA((CHUNKS, group)),
            pltpu.SemaphoreType.DMA((CHUNKS, group)),
            pltpu.SemaphoreType.DMA((CHUNKS,)),
            pltpu.SemaphoreType.DMA((CHUNKS,)),
            pltpu.SemaphoreType.DMA((CHUNKS,)),
        ],
        compiler_params=pltpu.CompilerParams(
            collective_id=0, has_side_effects=True, vmem_limit_bytes=60 * 1024 * 1024
        ),
    )(holder, rowblk, send, activations)


def body(activations, pattern, block_slot):
    tok_rows, width = activations.shape
    feat_count = lax.axis_size("feat")
    tok_count = lax.axis_size("tok")
    my_index = lax.axis_index("feat")
    panel_blocks = width // BLK
    list_length = pattern.shape[0]
    per_device = list_length // feat_count
    scale = 1.0 / (tok_rows * tok_count)
    ordered = jnp.zeros_like(pattern).at[block_slot].set(pattern)
    pairs = ordered.reshape(feat_count, per_device, 2)
    holder = pairs[:, :, 1] // panel_blocks
    local_column = pairs[:, :, 1] % panel_blocks
    picked = jnp.sum(jnp.where(holder == my_index, local_column, 0), axis=1)
    my_pairs = lax.dynamic_index_in_dim(pairs, my_index, 0, keepdims=False)
    my_holder = my_pairs[:, 1] // panel_blocks
    send = jnp.stack(
        [lax.dynamic_slice_in_dim(activations, picked[p] * BLK, BLK, axis=1) for p in range(feat_count)]
    )
    rowblk = my_pairs[:, 0] % panel_blocks
    blocks_local = activations.reshape(tok_rows, panel_blocks, BLK).transpose(1, 0, 2)
    out = fused(my_holder, rowblk, send, blocks_local, feat_count, tok_count, scale)
    return out.transpose(1, 0, 2)


def solution(mesh):
    placed = (P("tok", "feat"), P(), P())
    return jax.shard_map(
        body, mesh=mesh, in_specs=placed, out_specs=P("tok", "feat", None), check_vma=False
    )
```

```python
import functools

import jax
import jax.numpy as jnp
from jax import lax
from jax.experimental import pallas as pl
from jax.experimental.pallas import tpu as pltpu
from jax.sharding import PartitionSpec as P

BLK = 512
CHUNKS = 4
MESH = pl.DeviceIdType.MESH


def fused_kernel(n_feat, n_tok, chunks, scale,
                 holder_ref, rowblk_ref, send_ref, act_ref, out_ref, *scratch):
    recv = scratch[:chunks]
    gbuf, sta, stb, accbuf, fsend, frecv, flocal, asend, arecv, alocal, bsend, brecv = scratch[chunks:]
    slots = holder_ref.shape[0]
    tokens, width = send_ref.shape[1], send_ref.shape[2]
    w = width // chunks
    group = n_tok // 2
    piece = width // n_tok
    me = lax.axis_index("feat")
    t = lax.axis_index("tok")
    x = t // group
    j = t % group
    partner = (1 - x) * group + j

    barrier = pltpu.get_barrier_semaphore()
    for k in range(1, n_feat):
        pl.semaphore_signal(barrier, 1, device_id={"feat": lax.rem(me + k, n_feat)}, device_id_type=MESH)
    for o in range(1, group):
        pl.semaphore_signal(barrier, 1, device_id={"tok": x * group + lax.rem(j + o, group)}, device_id_type=MESH)
    pl.semaphore_signal(barrier, 1, device_id={"tok": partner}, device_id_type=MESH)
    pl.semaphore_wait(barrier, n_feat - 1 + group - 1 + 1)

    def feat_copies(c):
        cols = pl.ds(c * w, w)
        local = pltpu.make_async_copy(send_ref.at[me, :, cols], recv[c].at[me], flocal.at[c])
        copies = [local]
        for k in range(1, n_feat):
            peer = lax.rem(me + k, n_feat)
            copies.append(pltpu.make_async_remote_copy(
                src_ref=send_ref.at[peer, :, cols],
                dst_ref=recv[c].at[me],
                send_sem=fsend.at[c, k],
                recv_sem=frecv.at[c, k],
                device_id={"feat": peer},
                device_id_type=MESH,
            ))
        return copies

    pending = feat_copies(0)
    for cp in pending:
        cp.start()
    for c in range(chunks):
        for cp in pending:
            cp.wait()
        if c + 1 < chunks:
            pending = feat_copies(c + 1)
            for cp in pending:
                cp.start()

        def gram_one(k, carry):
            q = recv[c][holder_ref[k]]
            p = act_ref[rowblk_ref[k]]
            g = lax.dot_general(
                p, q, (((0,), (0,)), ((), ())), preferred_element_type=jnp.float32
            ) * scale
            for xx in range(2):
                for m in range(group):
                    r0 = (xx * group + m) * piece
                    gbuf[m, xx, k] = g[r0:r0 + piece, :]
            return carry

        lax.fori_loop(0, slots, gram_one, 0)

        own = pltpu.make_async_copy(gbuf.at[j], sta.at[c, j], alocal.at[c])
        own.start()
        a_copies = []
        for o in range(1, group):
            dest = lax.rem(j + o, group)
            cp = pltpu.make_async_remote_copy(
                src_ref=gbuf.at[dest],
                dst_ref=sta.at[c, j],
                send_sem=asend.at[c, o],
                recv_sem=arecv.at[c, o],
                device_id={"tok": x * group + dest},
                device_id_type=MESH,
            )
            cp.start()
            a_copies.append(cp)
        own.wait()
        for cp in a_copies:
            cp.wait()
        acc = sta[c, 0]
        for m in range(1, group):
            acc = acc + sta[c, m]
        accbuf[...] = acc
        bcp = pltpu.make_async_remote_copy(
            src_ref=accbuf.at[1 - x],
            dst_ref=stb.at[c],
            send_sem=bsend.at[c],
            recv_sem=brecv.at[c],
            device_id={"tok": partner},
            device_id_type=MESH,
        )
        bcp.start()
        bcp.wait()
        out_ref[:, :, pl.ds(c * w, w)] = accbuf[x] + stb[c]


def fused(holder, rowblk, send, activations, n_feat, n_tok, scale):
    slots = holder.shape[0]
    tokens, width = send.shape[1], send.shape[2]
    w = width // CHUNKS
    group = n_tok // 2
    piece = width // n_tok
    kernel = functools.partial(fused_kernel, n_feat, n_tok, CHUNKS, scale)
    return pl.pallas_call(
        kernel,
        out_shape=jax.ShapeDtypeStruct((slots, piece, width), jnp.float32),
        in_specs=[
            pl.BlockSpec(memory_space=pltpu.SMEM),
            pl.BlockSpec(memory_space=pltpu.SMEM),
            pl.BlockSpec(memory_space=pl.ANY),
            pl.BlockSpec(memory_space=pltpu.VMEM),
        ],
        out_specs=pl.BlockSpec(memory_space=pltpu.VMEM),
        scratch_shapes=[pltpu.VMEM((n_feat, tokens, w), send.dtype) for _ in range(CHUNKS)] + [
            pltpu.VMEM((group, 2, slots, piece, w), jnp.float32),
            pltpu.VMEM((CHUNKS, group, 2, slots, piece, w), jnp.float32),
            pltpu.VMEM((CHUNKS, slots, piece, w), jnp.float32),
            pltpu.VMEM((2, slots, piece, w), jnp.float32),
            pltpu.SemaphoreType.DMA((CHUNKS, n_feat)),
            pltpu.SemaphoreType.DMA((CHUNKS, n_feat)),
            pltpu.SemaphoreType.DMA((CHUNKS,)),
            pltpu.SemaphoreType.DMA((CHUNKS, group)),
            pltpu.SemaphoreType.DMA((CHUNKS, group)),
            pltpu.SemaphoreType.DMA((CHUNKS,)),
            pltpu.SemaphoreType.DMA((CHUNKS,)),
            pltpu.SemaphoreType.DMA((CHUNKS,)),
        ],
        compiler_params=pltpu.CompilerParams(
            collective_id=0, has_side_effects=True, vmem_limit_bytes=60 * 1024 * 1024
        ),
    )(holder, rowblk, send, activations)


def gather_kernel(index_ref, src_ref, dst_ref):
    dst_ref[0] = src_ref[...]


def gather_blocks(activations, index):
    tokens = activations.shape[0]
    count = index.shape[0]
    return pl.pallas_call(
        gather_kernel,
        out_shape=jax.ShapeDtypeStruct((count, tokens, BLK), activations.dtype),
        grid_spec=pltpu.PrefetchScalarGridSpec(
            num_scalar_prefetch=1,
            grid=(count,),
            in_specs=[pl.BlockSpec((tokens, BLK), lambda p, index_ref: (0, index_ref[p]))],
            out_specs=pl.BlockSpec((1, tokens, BLK), lambda p, index_ref: (p, 0, 0)),
        ),
    )(index, activations)


def body(activations, pattern, block_slot):
    tok_rows, width = activations.shape
    feat_count = lax.axis_size("feat")
    tok_count = lax.axis_size("tok")
    my_index = lax.axis_index("feat")
    panel_blocks = width // BLK
    list_length = pattern.shape[0]
    per_device = list_length // feat_count
    scale = 1.0 / (tok_rows * tok_count)
    ordered = jnp.zeros_like(pattern).at[block_slot].set(pattern)
    pairs = ordered.reshape(feat_count, per_device, 2)
    holder = pairs[:, :, 1] // panel_blocks
    local_column = pairs[:, :, 1] % panel_blocks
    picked = jnp.sum(jnp.where(holder == my_index, local_column, 0), axis=1)
    my_pairs = lax.dynamic_index_in_dim(pairs, my_index, 0, keepdims=False)
    my_holder = my_pairs[:, 1] // panel_blocks
    send = gather_blocks(activations, picked)
    rowblk = my_pairs[:, 0] % panel_blocks
    blocks_local = gather_blocks(activations, jnp.arange(panel_blocks, dtype=jnp.int32))
    out = fused(my_holder, rowblk, send, blocks_local, feat_count, tok_count, scale)
    return out.transpose(1, 0, 2)


def solution(mesh):
    placed = (P("tok", "feat"), P(), P())
    return jax.shard_map(
        body, mesh=mesh, in_specs=placed, out_specs=P("tok", "feat", None), check_vma=False
    )
```

```python
import functools

import jax
import jax.numpy as jnp
from jax import lax
from jax.experimental import pallas as pl
from jax.experimental.pallas import tpu as pltpu
from jax.sharding import PartitionSpec as P

BLK = 512
CHUNKS = 4
MESH = pl.DeviceIdType.MESH


def fused_kernel(n_feat, n_tok, chunks, scale,
                 holder_ref, rowblk_ref, send_ref, act_ref, out_ref, *scratch):
    recv = scratch[:chunks]
    (gbuf, st0, s1buf, st1, s2buf, st2,
     fsend, frecv, flocal, send0, recv0, send1, recv1, send2, recv2) = scratch[chunks:]
    slots = holder_ref.shape[0]
    tokens, width = send_ref.shape[1], send_ref.shape[2]
    w = width // chunks
    n_y = n_tok // 4
    piece = width // n_tok
    me = lax.axis_index("feat")
    t = lax.axis_index("tok")
    x = t // (2 * n_y)
    y = (t // 2) % n_y
    core = t % 2
    core_peer = t + 1 - 2 * core
    x_peer = t + (1 - 2 * x) * 2 * n_y

    barrier = pltpu.get_barrier_semaphore()
    for k in range(1, n_feat):
        pl.semaphore_signal(barrier, 1, device_id={"feat": lax.rem(me + k, n_feat)}, device_id_type=MESH)
    for o in range(1, n_y):
        dest = x * 2 * n_y + lax.rem(y + o, n_y) * 2 + core
        pl.semaphore_signal(barrier, 1, device_id={"tok": dest}, device_id_type=MESH)
    pl.semaphore_signal(barrier, 1, device_id={"tok": core_peer}, device_id_type=MESH)
    pl.semaphore_signal(barrier, 1, device_id={"tok": x_peer}, device_id_type=MESH)
    pl.semaphore_wait(barrier, n_feat - 1 + n_y - 1 + 2)

    def feat_copies(c):
        cols = pl.ds(c * w, w)
        local = pltpu.make_async_copy(send_ref.at[me, :, cols], recv[c].at[me], flocal.at[c])
        copies = [local]
        for k in range(1, n_feat):
            peer = lax.rem(me + k, n_feat)
            copies.append(pltpu.make_async_remote_copy(
                src_ref=send_ref.at[peer, :, cols],
                dst_ref=recv[c].at[me],
                send_sem=fsend.at[c, k],
                recv_sem=frecv.at[c, k],
                device_id={"feat": peer},
                device_id_type=MESH,
            ))
        return copies

    pending = feat_copies(0)
    for cp in pending:
        cp.start()
    for c in range(chunks):
        for cp in pending:
            cp.wait()
        if c + 1 < chunks:
            pending = feat_copies(c + 1)
            for cp in pending:
                cp.start()

        def gram_one(k, carry):
            q = recv[c][holder_ref[k]]
            p = act_ref[rowblk_ref[k]]
            g = lax.dot_general(
                p, q, (((0,), (0,)), ((), ())), preferred_element_type=jnp.float32
            ) * scale
            for xx in range(2):
                for yy in range(n_y):
                    for cc in range(2):
                        r0 = ((xx * n_y + yy) * 2 + cc) * piece
                        gbuf[cc, yy, xx, k] = g[r0:r0 + piece, :]
            return carry

        lax.fori_loop(0, slots, gram_one, 0)

        cp0 = pltpu.make_async_remote_copy(
            src_ref=gbuf.at[1 - core],
            dst_ref=st0.at[c],
            send_sem=send0.at[c],
            recv_sem=recv0.at[c],
            device_id={"tok": core_peer},
            device_id_type=MESH,
        )
        cp0.start()
        cp0.wait()
        s1buf[...] = gbuf[core] + st0[c]

        copies1 = []
        for o in range(1, n_y):
            dy = lax.rem(y + o, n_y)
            cp = pltpu.make_async_remote_copy(
                src_ref=s1buf.at[dy],
                dst_ref=st1.at[c, y],
                send_sem=send1.at[c, o],
                recv_sem=recv1.at[c, o],
                device_id={"tok": x * 2 * n_y + dy * 2 + core},
                device_id_type=MESH,
            )
            cp.start()
            copies1.append(cp)
        for cp in copies1:
            cp.wait()
        acc = s1buf[y]
        for o in range(1, n_y):
            acc = acc + st1[c, lax.rem(y + o, n_y)]
        s2buf[...] = acc

        cp2 = pltpu.make_async_remote_copy(
            src_ref=s2buf.at[1 - x],
            dst_ref=st2.at[c],
            send_sem=send2.at[c],
            recv_sem=recv2.at[c],
            device_id={"tok": x_peer},
            device_id_type=MESH,
        )
        cp2.start()
        cp2.wait()
        out_ref[:, :, pl.ds(c * w, w)] = s2buf[x] + st2[c]


def fused(holder, rowblk, send, activations, n_feat, n_tok, scale):
    slots = holder.shape[0]
    tokens, width = send.shape[1], send.shape[2]
    w = width // CHUNKS
    n_y = n_tok // 4
    piece = width // n_tok
    kernel = functools.partial(fused_kernel, n_feat, n_tok, CHUNKS, scale)
    blk = (slots, piece, w)
    return pl.pallas_call(
        kernel,
        out_shape=jax.ShapeDtypeStruct((slots, piece, width), jnp.float32),
        in_specs=[
            pl.BlockSpec(memory_space=pltpu.SMEM),
            pl.BlockSpec(memory_space=pltpu.SMEM),
            pl.BlockSpec(memory_space=pl.ANY),
            pl.BlockSpec(memory_space=pltpu.VMEM),
        ],
        out_specs=pl.BlockSpec(memory_space=pltpu.VMEM),
        scratch_shapes=[pltpu.VMEM((n_feat, tokens, w), send.dtype) for _ in range(CHUNKS)] + [
            pltpu.VMEM((2, n_y, 2) + blk, jnp.float32),
            pltpu.VMEM((CHUNKS, n_y, 2) + blk, jnp.float32),
            pltpu.VMEM((n_y, 2) + blk, jnp.float32),
            pltpu.VMEM((CHUNKS, n_y, 2) + blk, jnp.float32),
            pltpu.VMEM((2,) + blk, jnp.float32),
            pltpu.VMEM((CHUNKS,) + blk, jnp.float32),
            pltpu.SemaphoreType.DMA((CHUNKS, n_feat)),
            pltpu.SemaphoreType.DMA((CHUNKS, n_feat)),
            pltpu.SemaphoreType.DMA((CHUNKS,)),
            pltpu.SemaphoreType.DMA((CHUNKS,)),
            pltpu.SemaphoreType.DMA((CHUNKS,)),
            pltpu.SemaphoreType.DMA((CHUNKS, n_y)),
            pltpu.SemaphoreType.DMA((CHUNKS, n_y)),
            pltpu.SemaphoreType.DMA((CHUNKS,)),
            pltpu.SemaphoreType.DMA((CHUNKS,)),
        ],
        compiler_params=pltpu.CompilerParams(
            collective_id=0, has_side_effects=True, vmem_limit_bytes=60 * 1024 * 1024
        ),
    )(holder, rowblk, send, activations)


def gather_kernel(index_ref, src_ref, dst_ref):
    dst_ref[0] = src_ref[...]


def gather_blocks(activations, index):
    tokens = activations.shape[0]
    count = index.shape[0]
    return pl.pallas_call(
        gather_kernel,
        out_shape=jax.ShapeDtypeStruct((count, tokens, BLK), activations.dtype),
        grid_spec=pltpu.PrefetchScalarGridSpec(
            num_scalar_prefetch=1,
            grid=(count,),
            in_specs=[pl.BlockSpec((tokens, BLK), lambda p, index_ref: (0, index_ref[p]))],
            out_specs=pl.BlockSpec((1, tokens, BLK), lambda p, index_ref: (p, 0, 0)),
        ),
    )(index, activations)


def body(activations, pattern, block_slot):
    tok_rows, width = activations.shape
    feat_count = lax.axis_size("feat")
    tok_count = lax.axis_size("tok")
    my_index = lax.axis_index("feat")
    panel_blocks = width // BLK
    list_length = pattern.shape[0]
    per_device = list_length // feat_count
    scale = 1.0 / (tok_rows * tok_count)
    ordered = jnp.zeros_like(pattern).at[block_slot].set(pattern)
    pairs = ordered.reshape(feat_count, per_device, 2)
    holder = pairs[:, :, 1] // panel_blocks
    local_column = pairs[:, :, 1] % panel_blocks
    picked = jnp.sum(jnp.where(holder == my_index, local_column, 0), axis=1)
    my_pairs = lax.dynamic_index_in_dim(pairs, my_index, 0, keepdims=False)
    my_holder = my_pairs[:, 1] // panel_blocks
    send = gather_blocks(activations, picked)
    rowblk = my_pairs[:, 0] % panel_blocks
    blocks_local = gather_blocks(activations, jnp.arange(panel_blocks, dtype=jnp.int32))
    out = fused(my_holder, rowblk, send, blocks_local, feat_count, tok_count, scale)
    return out.transpose(1, 0, 2)


def solution(mesh):
    placed = (P("tok", "feat"), P(), P())
    return jax.shard_map(
        body, mesh=mesh, in_specs=placed, out_specs=P("tok", "feat", None), check_vma=False
    )
```

```python
import functools

import jax
import jax.numpy as jnp
from jax import lax
from jax.experimental import pallas as pl
from jax.experimental.pallas import tpu as pltpu
from jax.sharding import PartitionSpec as P

BLK = 512
CHUNKS = 4
MESH = pl.DeviceIdType.MESH


def fused_kernel(n_feat, n_tok, chunks, scale,
                 holder_ref, rowblk_ref, picked_ref, act_hbm, out_ref, *scratch):
    recv = scratch[:chunks]
    (act_ref, send_ref, gbuf, st0, s1buf, st1, s2buf, st2, panel_sem,
     fsend, frecv, flocal, send0, recv0, send1, recv1, send2, recv2) = scratch[chunks:]
    slots = holder_ref.shape[0]
    tokens, width = send_ref.shape[1], send_ref.shape[2]
    panel_blocks = act_ref.shape[0]
    w = width // chunks
    n_y = n_tok // 4
    piece = width // n_tok
    me = lax.axis_index("feat")
    t = lax.axis_index("tok")
    x = t // (2 * n_y)
    y = (t // 2) % n_y
    core = t % 2
    core_peer = t + 1 - 2 * core
    x_peer = t + (1 - 2 * x) * 2 * n_y

    barrier = pltpu.get_barrier_semaphore()
    for k in range(1, n_feat):
        pl.semaphore_signal(barrier, 1, device_id={"feat": lax.rem(me + k, n_feat)}, device_id_type=MESH)
    for o in range(1, n_y):
        dest = x * 2 * n_y + lax.rem(y + o, n_y) * 2 + core
        pl.semaphore_signal(barrier, 1, device_id={"tok": dest}, device_id_type=MESH)
    pl.semaphore_signal(barrier, 1, device_id={"tok": core_peer}, device_id_type=MESH)
    pl.semaphore_signal(barrier, 1, device_id={"tok": x_peer}, device_id_type=MESH)
    pl.semaphore_wait(barrier, n_feat - 1 + n_y - 1 + 2)

    panel = [
        pltpu.make_async_copy(act_hbm.at[:, pl.ds(b * width, width)], act_ref.at[b], panel_sem.at[b])
        for b in range(panel_blocks)
    ]
    for cp in panel:
        cp.start()
    for cp in panel:
        cp.wait()
    for p in range(n_feat):
        send_ref[p] = act_ref[picked_ref[p]]

    def feat_copies(c):
        cols = pl.ds(c * w, w)
        local = pltpu.make_async_copy(send_ref.at[me, :, cols], recv[c].at[me], flocal.at[c])
        copies = [local]
        for k in range(1, n_feat):
            peer = lax.rem(me + k, n_feat)
            copies.append(pltpu.make_async_remote_copy(
                src_ref=send_ref.at[peer, :, cols],
                dst_ref=recv[c].at[me],
                send_sem=fsend.at[c, k],
                recv_sem=frecv.at[c, k],
                device_id={"feat": peer},
                device_id_type=MESH,
            ))
        return copies

    pending = feat_copies(0)
    for cp in pending:
        cp.start()
    for c in range(chunks):
        for cp in pending:
            cp.wait()
        if c + 1 < chunks:
            pending = feat_copies(c + 1)
            for cp in pending:
                cp.start()

        def gram_one(k, carry):
            q = recv[c][holder_ref[k]]
            p = act_ref[rowblk_ref[k]]
            g = lax.dot_general(
                p, q, (((0,), (0,)), ((), ())), preferred_element_type=jnp.float32
            ) * scale
            for xx in range(2):
                for yy in range(n_y):
                    for cc in range(2):
                        r0 = ((xx * n_y + yy) * 2 + cc) * piece
                        gbuf[cc, yy, xx, k] = g[r0:r0 + piece, :]
            return carry

        lax.fori_loop(0, slots, gram_one, 0)

        cp0 = pltpu.make_async_remote_copy(
            src_ref=gbuf.at[1 - core],
            dst_ref=st0.at[c],
            send_sem=send0.at[c],
            recv_sem=recv0.at[c],
            device_id={"tok": core_peer},
            device_id_type=MESH,
        )
        cp0.start()
        cp0.wait()
        s1buf[...] = gbuf[core] + st0[c]

        copies1 = []
        for o in range(1, n_y):
            dy = lax.rem(y + o, n_y)
            cp = pltpu.make_async_remote_copy(
                src_ref=s1buf.at[dy],
                dst_ref=st1.at[c, y],
                send_sem=send1.at[c, o],
                recv_sem=recv1.at[c, o],
                device_id={"tok": x * 2 * n_y + dy * 2 + core},
                device_id_type=MESH,
            )
            cp.start()
            copies1.append(cp)
        for cp in copies1:
            cp.wait()
        acc = s1buf[y]
        for o in range(1, n_y):
            acc = acc + st1[c, lax.rem(y + o, n_y)]
        s2buf[...] = acc

        cp2 = pltpu.make_async_remote_copy(
            src_ref=s2buf.at[1 - x],
            dst_ref=st2.at[c],
            send_sem=send2.at[c],
            recv_sem=recv2.at[c],
            device_id={"tok": x_peer},
            device_id_type=MESH,
        )
        cp2.start()
        cp2.wait()
        out_ref[:, :, pl.ds(c * w, w)] = s2buf[x] + st2[c]


def fused(holder, rowblk, picked, activations, n_feat, n_tok, scale):
    slots = holder.shape[0]
    tokens, width = activations.shape[0], BLK
    panel_blocks = activations.shape[1] // BLK
    w = width // CHUNKS
    n_y = n_tok // 4
    piece = width // n_tok
    kernel = functools.partial(fused_kernel, n_feat, n_tok, CHUNKS, scale)
    blk = (slots, piece, w)
    return pl.pallas_call(
        kernel,
        out_shape=jax.ShapeDtypeStruct((slots, piece, width), jnp.float32),
        in_specs=[
            pl.BlockSpec(memory_space=pltpu.SMEM),
            pl.BlockSpec(memory_space=pltpu.SMEM),
            pl.BlockSpec(memory_space=pltpu.SMEM),
            pl.BlockSpec(memory_space=pl.ANY),
        ],
        out_specs=pl.BlockSpec(memory_space=pltpu.VMEM),
        scratch_shapes=[pltpu.VMEM((n_feat, tokens, w), activations.dtype) for _ in range(CHUNKS)] + [
            pltpu.VMEM((panel_blocks, tokens, width), activations.dtype),
            pltpu.VMEM((n_feat, tokens, width), activations.dtype),
            pltpu.VMEM((2, n_y, 2) + blk, jnp.float32),
            pltpu.VMEM((CHUNKS, n_y, 2) + blk, jnp.float32),
            pltpu.VMEM((n_y, 2) + blk, jnp.float32),
            pltpu.VMEM((CHUNKS, n_y, 2) + blk, jnp.float32),
            pltpu.VMEM((2,) + blk, jnp.float32),
            pltpu.VMEM((CHUNKS,) + blk, jnp.float32),
            pltpu.SemaphoreType.DMA((panel_blocks,)),
            pltpu.SemaphoreType.DMA((CHUNKS, n_feat)),
            pltpu.SemaphoreType.DMA((CHUNKS, n_feat)),
            pltpu.SemaphoreType.DMA((CHUNKS,)),
            pltpu.SemaphoreType.DMA((CHUNKS,)),
            pltpu.SemaphoreType.DMA((CHUNKS,)),
            pltpu.SemaphoreType.DMA((CHUNKS, n_y)),
            pltpu.SemaphoreType.DMA((CHUNKS, n_y)),
            pltpu.SemaphoreType.DMA((CHUNKS,)),
            pltpu.SemaphoreType.DMA((CHUNKS,)),
        ],
        compiler_params=pltpu.CompilerParams(
            collective_id=0, has_side_effects=True, vmem_limit_bytes=60 * 1024 * 1024
        ),
    )(holder, rowblk, picked, activations)


def body(activations, pattern, block_slot):
    tok_rows, width = activations.shape
    feat_count = lax.axis_size("feat")
    tok_count = lax.axis_size("tok")
    my_index = lax.axis_index("feat")
    panel_blocks = width // BLK
    list_length = pattern.shape[0]
    per_device = list_length // feat_count
    scale = 1.0 / (tok_rows * tok_count)
    ordered = jnp.zeros_like(pattern).at[block_slot].set(pattern)
    pairs = ordered.reshape(feat_count, per_device, 2)
    holder = pairs[:, :, 1] // panel_blocks
    local_column = pairs[:, :, 1] % panel_blocks
    picked = jnp.sum(jnp.where(holder == my_index, local_column, 0), axis=1)
    my_pairs = lax.dynamic_index_in_dim(pairs, my_index, 0, keepdims=False)
    my_holder = my_pairs[:, 1] // panel_blocks
    rowblk = my_pairs[:, 0] % panel_blocks
    out = fused(my_holder, rowblk, picked, activations, feat_count, tok_count, scale)
    return out.transpose(1, 0, 2)


def solution(mesh):
    placed = (P("tok", "feat"), P(), P())
    return jax.shard_map(
        body, mesh=mesh, in_specs=placed, out_specs=P("tok", "feat", None), check_vma=False
    )
```

```python
import functools

import jax
import jax.numpy as jnp
from jax import lax
from jax.experimental import pallas as pl
from jax.experimental.pallas import tpu as pltpu
from jax.sharding import PartitionSpec as P

BLK = 512
CHUNKS = 4
MESH = pl.DeviceIdType.MESH


def fused_kernel(n_feat, n_tok, chunks, scale,
                 holder_ref, rowblk_ref, picked_ref, act_hbm, out_ref, *scratch):
    recv = scratch[:chunks]
    (act_ref, send_ref, gbuf, st0, s1buf, st1, s2buf, st2, panel_sem,
     fsend, frecv, flocal, send0, recv0, send1, recv1, send2, recv2) = scratch[chunks:]
    slots = holder_ref.shape[0]
    tokens, width = send_ref.shape[1], send_ref.shape[2]
    panel_blocks = act_ref.shape[0]
    w = width // chunks
    n_y = n_tok // 4
    piece = width // n_tok
    me = lax.axis_index("feat")
    t = lax.axis_index("tok")
    x = t // (2 * n_y)
    y = (t // 2) % n_y
    core = t % 2
    core_peer = t + 1 - 2 * core
    x_peer = t + (1 - 2 * x) * 2 * n_y

    barrier = pltpu.get_barrier_semaphore()
    for k in range(1, n_feat):
        pl.semaphore_signal(barrier, 1, device_id={"feat": lax.rem(me + k, n_feat)}, device_id_type=MESH)
    for o in range(1, n_y):
        dest = x * 2 * n_y + lax.rem(y + o, n_y) * 2 + core
        pl.semaphore_signal(barrier, 1, device_id={"tok": dest}, device_id_type=MESH)
    pl.semaphore_signal(barrier, 1, device_id={"tok": core_peer}, device_id_type=MESH)
    pl.semaphore_signal(barrier, 1, device_id={"tok": x_peer}, device_id_type=MESH)
    pl.semaphore_wait(barrier, n_feat - 1 + n_y - 1 + 2)

    panel = [
        pltpu.make_async_copy(act_hbm.at[:, pl.ds(b * width, width)], act_ref.at[b], panel_sem.at[b])
        for b in range(panel_blocks)
    ]
    for cp in panel:
        cp.start()
    for cp in panel:
        cp.wait()
    for p in range(n_feat):
        send_ref[p] = act_ref[picked_ref[p]]

    def feat_copies(c):
        cols = pl.ds(c * w, w)
        local = pltpu.make_async_copy(send_ref.at[me, :, cols], recv[c].at[me], flocal.at[c])
        copies = [local]
        for k in range(1, n_feat):
            peer = lax.rem(me + k, n_feat)
            copies.append(pltpu.make_async_remote_copy(
                src_ref=send_ref.at[peer, :, cols],
                dst_ref=recv[c].at[me],
                send_sem=fsend.at[c, k],
                recv_sem=frecv.at[c, k],
                device_id={"feat": peer},
                device_id_type=MESH,
            ))
        return copies

    in_flight = []
    for c in range(min(2, chunks)):
        in_flight.append(feat_copies(c))
        for cp in in_flight[-1]:
            cp.start()
    for c in range(chunks):
        for cp in in_flight[c]:
            cp.wait()
        if c + 2 < chunks:
            in_flight.append(feat_copies(c + 2))
            for cp in in_flight[-1]:
                cp.start()

        def gram_one(k, carry):
            q = recv[c][holder_ref[k]]
            p = act_ref[rowblk_ref[k]]
            g = lax.dot_general(
                p, q, (((0,), (0,)), ((), ())), preferred_element_type=jnp.float32
            ) * scale
            for xx in range(2):
                for yy in range(n_y):
                    for cc in range(2):
                        r0 = ((xx * n_y + yy) * 2 + cc) * piece
                        gbuf[cc, yy, xx, k] = g[r0:r0 + piece, :]
            return carry

        lax.fori_loop(0, slots, gram_one, 0)

        cp0 = pltpu.make_async_remote_copy(
            src_ref=gbuf.at[1 - core],
            dst_ref=st0.at[c],
            send_sem=send0.at[c],
            recv_sem=recv0.at[c],
            device_id={"tok": core_peer},
            device_id_type=MESH,
        )
        cp0.start()
        cp0.wait()
        s1buf[...] = gbuf[core] + st0[c]

        copies1 = []
        for o in range(1, n_y):
            dy = lax.rem(y + o, n_y)
            cp = pltpu.make_async_remote_copy(
                src_ref=s1buf.at[dy],
                dst_ref=st1.at[c, y],
                send_sem=send1.at[c, o],
                recv_sem=recv1.at[c, o],
                device_id={"tok": x * 2 * n_y + dy * 2 + core},
                device_id_type=MESH,
            )
            cp.start()
            copies1.append(cp)
        for cp in copies1:
            cp.wait()
        acc = s1buf[y]
        for o in range(1, n_y):
            acc = acc + st1[c, lax.rem(y + o, n_y)]
        s2buf[...] = acc

        cp2 = pltpu.make_async_remote_copy(
            src_ref=s2buf.at[1 - x],
            dst_ref=st2.at[c],
            send_sem=send2.at[c],
            recv_sem=recv2.at[c],
            device_id={"tok": x_peer},
            device_id_type=MESH,
        )
        cp2.start()
        cp2.wait()
        out_ref[:, :, pl.ds(c * w, w)] = s2buf[x] + st2[c]


def fused(holder, rowblk, picked, activations, n_feat, n_tok, scale):
    slots = holder.shape[0]
    tokens, width = activations.shape[0], BLK
    panel_blocks = activations.shape[1] // BLK
    w = width // CHUNKS
    n_y = n_tok // 4
    piece = width // n_tok
    kernel = functools.partial(fused_kernel, n_feat, n_tok, CHUNKS, scale)
    blk = (slots, piece, w)
    return pl.pallas_call(
        kernel,
        out_shape=jax.ShapeDtypeStruct((slots, piece, width), jnp.float32),
        in_specs=[
            pl.BlockSpec(memory_space=pltpu.SMEM),
            pl.BlockSpec(memory_space=pltpu.SMEM),
            pl.BlockSpec(memory_space=pltpu.SMEM),
            pl.BlockSpec(memory_space=pl.ANY),
        ],
        out_specs=pl.BlockSpec(memory_space=pltpu.VMEM),
        scratch_shapes=[pltpu.VMEM((n_feat, tokens, w), activations.dtype) for _ in range(CHUNKS)] + [
            pltpu.VMEM((panel_blocks, tokens, width), activations.dtype),
            pltpu.VMEM((n_feat, tokens, width), activations.dtype),
            pltpu.VMEM((2, n_y, 2) + blk, jnp.float32),
            pltpu.VMEM((CHUNKS, n_y, 2) + blk, jnp.float32),
            pltpu.VMEM((n_y, 2) + blk, jnp.float32),
            pltpu.VMEM((CHUNKS, n_y, 2) + blk, jnp.float32),
            pltpu.VMEM((2,) + blk, jnp.float32),
            pltpu.VMEM((CHUNKS,) + blk, jnp.float32),
            pltpu.SemaphoreType.DMA((panel_blocks,)),
            pltpu.SemaphoreType.DMA((CHUNKS, n_feat)),
            pltpu.SemaphoreType.DMA((CHUNKS, n_feat)),
            pltpu.SemaphoreType.DMA((CHUNKS,)),
            pltpu.SemaphoreType.DMA((CHUNKS,)),
            pltpu.SemaphoreType.DMA((CHUNKS,)),
            pltpu.SemaphoreType.DMA((CHUNKS, n_y)),
            pltpu.SemaphoreType.DMA((CHUNKS, n_y)),
            pltpu.SemaphoreType.DMA((CHUNKS,)),
            pltpu.SemaphoreType.DMA((CHUNKS,)),
        ],
        compiler_params=pltpu.CompilerParams(
            collective_id=0, has_side_effects=True, vmem_limit_bytes=60 * 1024 * 1024
        ),
    )(holder, rowblk, picked, activations)


def body(activations, pattern, block_slot):
    tok_rows, width = activations.shape
    feat_count = lax.axis_size("feat")
    tok_count = lax.axis_size("tok")
    my_index = lax.axis_index("feat")
    panel_blocks = width // BLK
    list_length = pattern.shape[0]
    per_device = list_length // feat_count
    scale = 1.0 / (tok_rows * tok_count)
    ordered = jnp.zeros_like(pattern).at[block_slot].set(pattern)
    pairs = ordered.reshape(feat_count, per_device, 2)
    holder = pairs[:, :, 1] // panel_blocks
    local_column = pairs[:, :, 1] % panel_blocks
    picked = jnp.sum(jnp.where(holder == my_index, local_column, 0), axis=1)
    my_pairs = lax.dynamic_index_in_dim(pairs, my_index, 0, keepdims=False)
    my_holder = my_pairs[:, 1] // panel_blocks
    rowblk = my_pairs[:, 0] % panel_blocks
    out = fused(my_holder, rowblk, picked, activations, feat_count, tok_count, scale)
    return out.transpose(1, 0, 2)


def solution(mesh):
    placed = (P("tok", "feat"), P(), P())
    return jax.shard_map(
        body, mesh=mesh, in_specs=placed, out_specs=P("tok", "feat", None), check_vma=False
    )
```

```python
import functools

import jax
import jax.numpy as jnp
from jax import lax
from jax.experimental import pallas as pl
from jax.experimental.pallas import tpu as pltpu
from jax.sharding import PartitionSpec as P

BLK = 512
CHUNKS = 4
DEPTH = 4
MESH = pl.DeviceIdType.MESH


def fused_kernel(n_feat, n_tok, chunks, scale,
                 holder_ref, rowblk_ref, picked_ref, act_hbm, out_ref, *scratch):
    recv = scratch[:chunks]
    (act_ref, send_ref, gbuf, st0, s1buf, st1, s2buf, st2, panel_sem,
     fsend, frecv, flocal, send0, recv0, send1, recv1, send2, recv2) = scratch[chunks:]
    slots = holder_ref.shape[0]
    tokens, width = send_ref.shape[1], send_ref.shape[2]
    panel_blocks = act_ref.shape[0]
    w = width // chunks
    n_y = n_tok // 4
    piece = width // n_tok
    me = lax.axis_index("feat")
    t = lax.axis_index("tok")
    x = t // (2 * n_y)
    y = (t // 2) % n_y
    core = t % 2
    core_peer = t + 1 - 2 * core
    x_peer = t + (1 - 2 * x) * 2 * n_y

    barrier = pltpu.get_barrier_semaphore()
    for k in range(1, n_feat):
        pl.semaphore_signal(barrier, 1, device_id={"feat": lax.rem(me + k, n_feat)}, device_id_type=MESH)
    for o in range(1, n_y):
        dest = x * 2 * n_y + lax.rem(y + o, n_y) * 2 + core
        pl.semaphore_signal(barrier, 1, device_id={"tok": dest}, device_id_type=MESH)
    pl.semaphore_signal(barrier, 1, device_id={"tok": core_peer}, device_id_type=MESH)
    pl.semaphore_signal(barrier, 1, device_id={"tok": x_peer}, device_id_type=MESH)
    pl.semaphore_wait(barrier, n_feat - 1 + n_y - 1 + 2)

    panel = [
        pltpu.make_async_copy(act_hbm.at[:, pl.ds(b * width, width)], act_ref.at[b], panel_sem.at[b])
        for b in range(panel_blocks)
    ]
    for cp in panel:
        cp.start()
    for cp in panel:
        cp.wait()
    for p in range(n_feat):
        send_ref[p] = act_ref[picked_ref[p]]

    def feat_copies(c):
        cols = pl.ds(c * w, w)
        local = pltpu.make_async_copy(send_ref.at[me, :, cols], recv[c].at[me], flocal.at[c])
        copies = [local]
        for k in range(1, n_feat):
            peer = lax.rem(me + k, n_feat)
            copies.append(pltpu.make_async_remote_copy(
                src_ref=send_ref.at[peer, :, cols],
                dst_ref=recv[c].at[me],
                send_sem=fsend.at[c, k],
                recv_sem=frecv.at[c, k],
                device_id={"feat": peer},
                device_id_type=MESH,
            ))
        return copies

    in_flight = []
    for c in range(min(DEPTH, chunks)):
        in_flight.append(feat_copies(c))
        for cp in in_flight[-1]:
            cp.start()
    for c in range(chunks):
        for cp in in_flight[c]:
            cp.wait()
        if c + DEPTH < chunks:
            in_flight.append(feat_copies(c + DEPTH))
            for cp in in_flight[-1]:
                cp.start()

        def gram_one(k, carry):
            q = recv[c][holder_ref[k]]
            p = act_ref[rowblk_ref[k]]
            g = lax.dot_general(
                p, q, (((0,), (0,)), ((), ())), preferred_element_type=jnp.float32
            ) * scale
            for xx in range(2):
                for yy in range(n_y):
                    for cc in range(2):
                        r0 = ((xx * n_y + yy) * 2 + cc) * piece
                        gbuf[cc, yy, xx, k] = g[r0:r0 + piece, :]
            return carry

        lax.fori_loop(0, slots, gram_one, 0)

        cp0 = pltpu.make_async_remote_copy(
            src_ref=gbuf.at[1 - core],
            dst_ref=st0.at[c],
            send_sem=send0.at[c],
            recv_sem=recv0.at[c],
            device_id={"tok": core_peer},
            device_id_type=MESH,
        )
        cp0.start()
        cp0.wait()
        s1buf[...] = gbuf[core] + st0[c]

        copies1 = []
        for o in range(1, n_y):
            dy = lax.rem(y + o, n_y)
            cp = pltpu.make_async_remote_copy(
                src_ref=s1buf.at[dy],
                dst_ref=st1.at[c, y],
                send_sem=send1.at[c, o],
                recv_sem=recv1.at[c, o],
                device_id={"tok": x * 2 * n_y + dy * 2 + core},
                device_id_type=MESH,
            )
            cp.start()
            copies1.append(cp)
        for cp in copies1:
            cp.wait()
        acc = s1buf[y]
        for o in range(1, n_y):
            acc = acc + st1[c, lax.rem(y + o, n_y)]
        s2buf[...] = acc

        cp2 = pltpu.make_async_remote_copy(
            src_ref=s2buf.at[1 - x],
            dst_ref=st2.at[c],
            send_sem=send2.at[c],
            recv_sem=recv2.at[c],
            device_id={"tok": x_peer},
            device_id_type=MESH,
        )
        cp2.start()
        cp2.wait()
        out_ref[:, :, pl.ds(c * w, w)] = s2buf[x] + st2[c]


def fused(holder, rowblk, picked, activations, n_feat, n_tok, scale):
    slots = holder.shape[0]
    tokens, width = activations.shape[0], BLK
    panel_blocks = activations.shape[1] // BLK
    w = width // CHUNKS
    n_y = n_tok // 4
    piece = width // n_tok
    kernel = functools.partial(fused_kernel, n_feat, n_tok, CHUNKS, scale)
    blk = (slots, piece, w)
    return pl.pallas_call(
        kernel,
        out_shape=jax.ShapeDtypeStruct((slots, piece, width), jnp.float32),
        in_specs=[
            pl.BlockSpec(memory_space=pltpu.SMEM),
            pl.BlockSpec(memory_space=pltpu.SMEM),
            pl.BlockSpec(memory_space=pltpu.SMEM),
            pl.BlockSpec(memory_space=pl.ANY),
        ],
        out_specs=pl.BlockSpec(memory_space=pltpu.VMEM),
        scratch_shapes=[pltpu.VMEM((n_feat, tokens, w), activations.dtype) for _ in range(CHUNKS)] + [
            pltpu.VMEM((panel_blocks, tokens, width), activations.dtype),
            pltpu.VMEM((n_feat, tokens, width), activations.dtype),
            pltpu.VMEM((2, n_y, 2) + blk, jnp.float32),
            pltpu.VMEM((CHUNKS, n_y, 2) + blk, jnp.float32),
            pltpu.VMEM((n_y, 2) + blk, jnp.float32),
            pltpu.VMEM((CHUNKS, n_y, 2) + blk, jnp.float32),
            pltpu.VMEM((2,) + blk, jnp.float32),
            pltpu.VMEM((CHUNKS,) + blk, jnp.float32),
            pltpu.SemaphoreType.DMA((panel_blocks,)),
            pltpu.SemaphoreType.DMA((CHUNKS, n_feat)),
            pltpu.SemaphoreType.DMA((CHUNKS, n_feat)),
            pltpu.SemaphoreType.DMA((CHUNKS,)),
            pltpu.SemaphoreType.DMA((CHUNKS,)),
            pltpu.SemaphoreType.DMA((CHUNKS,)),
            pltpu.SemaphoreType.DMA((CHUNKS, n_y)),
            pltpu.SemaphoreType.DMA((CHUNKS, n_y)),
            pltpu.SemaphoreType.DMA((CHUNKS,)),
            pltpu.SemaphoreType.DMA((CHUNKS,)),
        ],
        compiler_params=pltpu.CompilerParams(
            collective_id=0, has_side_effects=True, vmem_limit_bytes=60 * 1024 * 1024
        ),
    )(holder, rowblk, picked, activations)


def body(activations, pattern, block_slot):
    tok_rows, width = activations.shape
    feat_count = lax.axis_size("feat")
    tok_count = lax.axis_size("tok")
    my_index = lax.axis_index("feat")
    panel_blocks = width // BLK
    list_length = pattern.shape[0]
    per_device = list_length // feat_count
    scale = 1.0 / (tok_rows * tok_count)
    ordered = jnp.zeros_like(pattern).at[block_slot].set(pattern)
    pairs = ordered.reshape(feat_count, per_device, 2)
    holder = pairs[:, :, 1] // panel_blocks
    local_column = pairs[:, :, 1] % panel_blocks
    picked = jnp.sum(jnp.where(holder == my_index, local_column, 0), axis=1)
    my_pairs = lax.dynamic_index_in_dim(pairs, my_index, 0, keepdims=False)
    my_holder = my_pairs[:, 1] // panel_blocks
    rowblk = my_pairs[:, 0] % panel_blocks
    out = fused(my_holder, rowblk, picked, activations, feat_count, tok_count, scale)
    return out.transpose(1, 0, 2)


def solution(mesh):
    placed = (P("tok", "feat"), P(), P())
    return jax.shard_map(
        body, mesh=mesh, in_specs=placed, out_specs=P("tok", "feat", None), check_vma=False
    )
```

```python
import functools

import jax
import jax.numpy as jnp
from jax import lax
from jax.experimental import pallas as pl
from jax.experimental.pallas import tpu as pltpu
from jax.sharding import PartitionSpec as P

BLK = 512
CHUNKS = 4
MESH = pl.DeviceIdType.MESH


def fused_kernel(n_feat, n_tok, chunks, scale,
                 holder_ref, rowblk_ref, picked_ref, act_hbm, out_ref, *scratch):
    recv = scratch[:chunks]
    (act_ref, send_ref, gbuf, st0, s1buf, st1, s2buf, st2, panel_sem,
     fsend, frecv, flocal, send0, recv0, send1, recv1, send2, recv2) = scratch[chunks:]
    slots = holder_ref.shape[0]
    tokens, width = send_ref.shape[1], send_ref.shape[2]
    panel_blocks = act_ref.shape[0]
    w = width // chunks
    n_y = n_tok // 4
    piece = width // n_tok
    me = lax.axis_index("feat")
    t = lax.axis_index("tok")
    x = t // (2 * n_y)
    y = (t // 2) % n_y
    core = t % 2
    core_peer = t + 1 - 2 * core
    x_peer = t + (1 - 2 * x) * 2 * n_y

    barrier = pltpu.get_barrier_semaphore()
    for k in range(1, n_feat):
        pl.semaphore_signal(barrier, 1, device_id={"feat": lax.rem(me + k, n_feat)}, device_id_type=MESH)
    for o in range(1, n_y):
        dest = x * 2 * n_y + lax.rem(y + o, n_y) * 2 + core
        pl.semaphore_signal(barrier, 1, device_id={"tok": dest}, device_id_type=MESH)
    pl.semaphore_signal(barrier, 1, device_id={"tok": core_peer}, device_id_type=MESH)
    pl.semaphore_signal(barrier, 1, device_id={"tok": x_peer}, device_id_type=MESH)
    pl.semaphore_wait(barrier, n_feat - 1 + n_y - 1 + 2)

    panel = [
        pltpu.make_async_copy(act_hbm.at[:, pl.ds(b * width, width)], act_ref.at[b], panel_sem.at[b])
        for b in range(panel_blocks)
    ]
    for cp in panel:
        cp.start()
    for cp in panel:
        cp.wait()

    def feat_copies(c):
        cols = pl.ds(c * w, w)
        local = pltpu.make_async_copy(send_ref.at[me, :, cols], recv[c].at[me], flocal.at[c])
        copies = [local]
        for k in range(1, n_feat):
            peer = lax.rem(me + k, n_feat)
            copies.append(pltpu.make_async_remote_copy(
                src_ref=send_ref.at[peer, :, cols],
                dst_ref=recv[c].at[me],
                send_sem=fsend.at[c, k],
                recv_sem=frecv.at[c, k],
                device_id={"feat": peer},
                device_id_type=MESH,
            ))
        return copies

    in_flight = [feat_copies(c) for c in range(min(2, chunks))]
    for k in list(range(1, n_feat)) + [0]:
        peer = lax.rem(me + k, n_feat)
        send_ref[peer] = act_ref[picked_ref[peer]]
        for copies in in_flight:
            copies[k].start()
    for c in range(chunks):
        for cp in in_flight[c]:
            cp.wait()
        if c + 2 < chunks:
            in_flight.append(feat_copies(c + 2))
            for cp in in_flight[-1]:
                cp.start()

        def gram_one(k, carry):
            q = recv[c][holder_ref[k]]
            p = act_ref[rowblk_ref[k]]
            g = lax.dot_general(
                p, q, (((0,), (0,)), ((), ())), preferred_element_type=jnp.float32
            ) * scale
            for xx in range(2):
                for yy in range(n_y):
                    for cc in range(2):
                        r0 = ((xx * n_y + yy) * 2 + cc) * piece
                        gbuf[cc, yy, xx, k] = g[r0:r0 + piece, :]
            return carry

        lax.fori_loop(0, slots, gram_one, 0)

        cp0 = pltpu.make_async_remote_copy(
            src_ref=gbuf.at[1 - core],
            dst_ref=st0.at[c],
            send_sem=send0.at[c],
            recv_sem=recv0.at[c],
            device_id={"tok": core_peer},
            device_id_type=MESH,
        )
        cp0.start()
        cp0.wait()
        s1buf[...] = gbuf[core] + st0[c]

        copies1 = []
        for o in range(1, n_y):
            dy = lax.rem(y + o, n_y)
            cp = pltpu.make_async_remote_copy(
                src_ref=s1buf.at[dy],
                dst_ref=st1.at[c, y],
                send_sem=send1.at[c, o],
                recv_sem=recv1.at[c, o],
                device_id={"tok": x * 2 * n_y + dy * 2 + core},
                device_id_type=MESH,
            )
            cp.start()
            copies1.append(cp)
        for cp in copies1:
            cp.wait()
        acc = s1buf[y]
        for o in range(1, n_y):
            acc = acc + st1[c, lax.rem(y + o, n_y)]
        s2buf[...] = acc

        cp2 = pltpu.make_async_remote_copy(
            src_ref=s2buf.at[1 - x],
            dst_ref=st2.at[c],
            send_sem=send2.at[c],
            recv_sem=recv2.at[c],
            device_id={"tok": x_peer},
            device_id_type=MESH,
        )
        cp2.start()
        cp2.wait()
        out_ref[:, :, pl.ds(c * w, w)] = s2buf[x] + st2[c]


def fused(holder, rowblk, picked, activations, n_feat, n_tok, scale):
    slots = holder.shape[0]
    tokens, width = activations.shape[0], BLK
    panel_blocks = activations.shape[1] // BLK
    w = width // CHUNKS
    n_y = n_tok // 4
    piece = width // n_tok
    kernel = functools.partial(fused_kernel, n_feat, n_tok, CHUNKS, scale)
    blk = (slots, piece, w)
    return pl.pallas_call(
        kernel,
        out_shape=jax.ShapeDtypeStruct((slots, piece, width), jnp.float32),
        in_specs=[
            pl.BlockSpec(memory_space=pltpu.SMEM),
            pl.BlockSpec(memory_space=pltpu.SMEM),
            pl.BlockSpec(memory_space=pltpu.SMEM),
            pl.BlockSpec(memory_space=pl.ANY),
        ],
        out_specs=pl.BlockSpec(memory_space=pltpu.VMEM),
        scratch_shapes=[pltpu.VMEM((n_feat, tokens, w), activations.dtype) for _ in range(CHUNKS)] + [
            pltpu.VMEM((panel_blocks, tokens, width), activations.dtype),
            pltpu.VMEM((n_feat, tokens, width), activations.dtype),
            pltpu.VMEM((2, n_y, 2) + blk, jnp.float32),
            pltpu.VMEM((CHUNKS, n_y, 2) + blk, jnp.float32),
            pltpu.VMEM((n_y, 2) + blk, jnp.float32),
            pltpu.VMEM((CHUNKS, n_y, 2) + blk, jnp.float32),
            pltpu.VMEM((2,) + blk, jnp.float32),
            pltpu.VMEM((CHUNKS,) + blk, jnp.float32),
            pltpu.SemaphoreType.DMA((panel_blocks,)),
            pltpu.SemaphoreType.DMA((CHUNKS, n_feat)),
            pltpu.SemaphoreType.DMA((CHUNKS, n_feat)),
            pltpu.SemaphoreType.DMA((CHUNKS,)),
            pltpu.SemaphoreType.DMA((CHUNKS,)),
            pltpu.SemaphoreType.DMA((CHUNKS,)),
            pltpu.SemaphoreType.DMA((CHUNKS, n_y)),
            pltpu.SemaphoreType.DMA((CHUNKS, n_y)),
            pltpu.SemaphoreType.DMA((CHUNKS,)),
            pltpu.SemaphoreType.DMA((CHUNKS,)),
        ],
        compiler_params=pltpu.CompilerParams(
            collective_id=0, has_side_effects=True, vmem_limit_bytes=60 * 1024 * 1024
        ),
    )(holder, rowblk, picked, activations)


def body(activations, pattern, block_slot):
    tok_rows, width = activations.shape
    feat_count = lax.axis_size("feat")
    tok_count = lax.axis_size("tok")
    my_index = lax.axis_index("feat")
    panel_blocks = width // BLK
    list_length = pattern.shape[0]
    per_device = list_length // feat_count
    scale = 1.0 / (tok_rows * tok_count)
    ordered = jnp.zeros_like(pattern).at[block_slot].set(pattern)
    pairs = ordered.reshape(feat_count, per_device, 2)
    holder = pairs[:, :, 1] // panel_blocks
    local_column = pairs[:, :, 1] % panel_blocks
    picked = jnp.sum(jnp.where(holder == my_index, local_column, 0), axis=1)
    my_pairs = lax.dynamic_index_in_dim(pairs, my_index, 0, keepdims=False)
    my_holder = my_pairs[:, 1] // panel_blocks
    rowblk = my_pairs[:, 0] % panel_blocks
    out = fused(my_holder, rowblk, picked, activations, feat_count, tok_count, scale)
    return out.transpose(1, 0, 2)


def solution(mesh):
    placed = (P("tok", "feat"), P(), P())
    return jax.shard_map(
        body, mesh=mesh, in_specs=placed, out_specs=P("tok", "feat", None), check_vma=False
    )
```

```python
import functools

import jax
import jax.numpy as jnp
from jax import lax
from jax.experimental import pallas as pl
from jax.experimental.pallas import tpu as pltpu
from jax.sharding import PartitionSpec as P

BLK = 512
CHUNKS = 4
MESH = pl.DeviceIdType.MESH


def fused_kernel(n_feat, n_tok, chunks, scale,
                 holder_ref, rowblk_ref, picked_ref, act_hbm, out_ref, *scratch):
    recv = scratch[:chunks]
    (act_ref, send_ref, gbuf, st0, s1buf, st1, s2buf, st2, stz, panel_sem,
     fsend, frecv, flocal, send0, recv0, send1, recv1, send2, recv2, zsend, zrecv) = scratch[chunks:]
    slots = holder_ref.shape[0]
    tokens, width = send_ref.shape[1], send_ref.shape[2]
    panel_blocks = act_ref.shape[0]
    w = width // chunks
    n_y = n_tok // 4
    piece = width // n_tok
    me = lax.axis_index("feat")
    t = lax.axis_index("tok")
    x = t // (2 * n_y)
    y = (t // 2) % n_y
    core = t % 2
    core_peer = t + 1 - 2 * core
    x_peer = t + (1 - 2 * x) * 2 * n_y

    barrier = pltpu.get_barrier_semaphore()
    for k in range(1, n_feat):
        pl.semaphore_signal(barrier, 1, device_id={"feat": lax.rem(me + k, n_feat)}, device_id_type=MESH)
    for o in range(1, n_tok):
        pl.semaphore_signal(barrier, 1, device_id={"tok": lax.rem(t + o, n_tok)}, device_id_type=MESH)
    pl.semaphore_wait(barrier, n_feat - 1 + n_tok - 1)

    panel = [
        pltpu.make_async_copy(act_hbm.at[:, pl.ds(b * width, width)], act_ref.at[b], panel_sem.at[b])
        for b in range(panel_blocks)
    ]
    for cp in panel:
        cp.start()
    for cp in panel:
        cp.wait()
    for p in range(n_feat):
        send_ref[p] = act_ref[picked_ref[p]]

    def feat_copies(c):
        cols = pl.ds(c * w, w)
        local = pltpu.make_async_copy(send_ref.at[me, :, cols], recv[c].at[me], flocal.at[c])
        copies = [local]
        for k in range(1, n_feat):
            peer = lax.rem(me + k, n_feat)
            copies.append(pltpu.make_async_remote_copy(
                src_ref=send_ref.at[peer, :, cols],
                dst_ref=recv[c].at[me],
                send_sem=fsend.at[c, k],
                recv_sem=frecv.at[c, k],
                device_id={"feat": peer},
                device_id_type=MESH,
            ))
        return copies

    in_flight = []
    for c in range(min(2, chunks)):
        in_flight.append(feat_copies(c))
        for cp in in_flight[-1]:
            cp.start()
    for c in range(chunks):
        for cp in in_flight[c]:
            cp.wait()
        if c + 2 < chunks:
            in_flight.append(feat_copies(c + 2))
            for cp in in_flight[-1]:
                cp.start()

        def gram_one(k, carry):
            q = recv[c][holder_ref[k]]
            p = act_ref[rowblk_ref[k]]
            g = lax.dot_general(
                p, q, (((0,), (0,)), ((), ())), preferred_element_type=jnp.float32
            ) * scale
            for xx in range(2):
                for yy in range(n_y):
                    for cc in range(2):
                        r0 = ((xx * n_y + yy) * 2 + cc) * piece
                        gbuf[cc, yy, xx, k] = g[r0:r0 + piece, :]
            return carry

        lax.fori_loop(0, slots, gram_one, 0)

        if c == chunks - 1:
            last = []
            for o in range(1, n_tok):
                dest = lax.rem(t + o, n_tok)
                cp = pltpu.make_async_remote_copy(
                    src_ref=gbuf.at[dest % 2, (dest // 2) % n_y, dest // (2 * n_y)],
                    dst_ref=stz.at[o],
                    send_sem=zsend.at[o],
                    recv_sem=zrecv.at[o],
                    device_id={"tok": dest},
                    device_id_type=MESH,
                )
                cp.start()
                last.append(cp)
            for cp in last:
                cp.wait()
            acc = gbuf[core, y, x]
            for o in range(1, n_tok):
                acc = acc + stz[o]
            out_ref[:, :, pl.ds(c * w, w)] = acc
            continue

        cp0 = pltpu.make_async_remote_copy(
            src_ref=gbuf.at[1 - core],
            dst_ref=st0.at[c],
            send_sem=send0.at[c],
            recv_sem=recv0.at[c],
            device_id={"tok": core_peer},
            device_id_type=MESH,
        )
        cp0.start()
        cp0.wait()
        s1buf[...] = gbuf[core] + st0[c]

        copies1 = []
        for o in range(1, n_y):
            dy = lax.rem(y + o, n_y)
            cp = pltpu.make_async_remote_copy(
                src_ref=s1buf.at[dy],
                dst_ref=st1.at[c, y],
                send_sem=send1.at[c, o],
                recv_sem=recv1.at[c, o],
                device_id={"tok": x * 2 * n_y + dy * 2 + core},
                device_id_type=MESH,
            )
            cp.start()
            copies1.append(cp)
        for cp in copies1:
            cp.wait()
        acc = s1buf[y]
        for o in range(1, n_y):
            acc = acc + st1[c, lax.rem(y + o, n_y)]
        s2buf[...] = acc

        cp2 = pltpu.make_async_remote_copy(
            src_ref=s2buf.at[1 - x],
            dst_ref=st2.at[c],
            send_sem=send2.at[c],
            recv_sem=recv2.at[c],
            device_id={"tok": x_peer},
            device_id_type=MESH,
        )
        cp2.start()
        cp2.wait()
        out_ref[:, :, pl.ds(c * w, w)] = s2buf[x] + st2[c]


def fused(holder, rowblk, picked, activations, n_feat, n_tok, scale):
    slots = holder.shape[0]
    tokens, width = activations.shape[0], BLK
    panel_blocks = activations.shape[1] // BLK
    w = width // CHUNKS
    n_y = n_tok // 4
    piece = width // n_tok
    kernel = functools.partial(fused_kernel, n_feat, n_tok, CHUNKS, scale)
    blk = (slots, piece, w)
    return pl.pallas_call(
        kernel,
        out_shape=jax.ShapeDtypeStruct((slots, piece, width), jnp.float32),
        in_specs=[
            pl.BlockSpec(memory_space=pltpu.SMEM),
            pl.BlockSpec(memory_space=pltpu.SMEM),
            pl.BlockSpec(memory_space=pltpu.SMEM),
            pl.BlockSpec(memory_space=pl.ANY),
        ],
        out_specs=pl.BlockSpec(memory_space=pltpu.VMEM),
        scratch_shapes=[pltpu.VMEM((n_feat, tokens, w), activations.dtype) for _ in range(CHUNKS)] + [
            pltpu.VMEM((panel_blocks, tokens, width), activations.dtype),
            pltpu.VMEM((n_feat, tokens, width), activations.dtype),
            pltpu.VMEM((2, n_y, 2) + blk, jnp.float32),
            pltpu.VMEM((CHUNKS, n_y, 2) + blk, jnp.float32),
            pltpu.VMEM((n_y, 2) + blk, jnp.float32),
            pltpu.VMEM((CHUNKS, n_y, 2) + blk, jnp.float32),
            pltpu.VMEM((2,) + blk, jnp.float32),
            pltpu.VMEM((CHUNKS,) + blk, jnp.float32),
            pltpu.VMEM((n_tok,) + blk, jnp.float32),
            pltpu.SemaphoreType.DMA((panel_blocks,)),
            pltpu.SemaphoreType.DMA((CHUNKS, n_feat)),
            pltpu.SemaphoreType.DMA((CHUNKS, n_feat)),
            pltpu.SemaphoreType.DMA((CHUNKS,)),
            pltpu.SemaphoreType.DMA((CHUNKS,)),
            pltpu.SemaphoreType.DMA((CHUNKS,)),
            pltpu.SemaphoreType.DMA((CHUNKS, n_y)),
            pltpu.SemaphoreType.DMA((CHUNKS, n_y)),
            pltpu.SemaphoreType.DMA((CHUNKS,)),
            pltpu.SemaphoreType.DMA((CHUNKS,)),
            pltpu.SemaphoreType.DMA((n_tok,)),
            pltpu.SemaphoreType.DMA((n_tok,)),
        ],
        compiler_params=pltpu.CompilerParams(
            collective_id=0, has_side_effects=True, vmem_limit_bytes=60 * 1024 * 1024
        ),
    )(holder, rowblk, picked, activations)


def body(activations, pattern, block_slot):
    tok_rows, width = activations.shape
    feat_count = lax.axis_size("feat")
    tok_count = lax.axis_size("tok")
    my_index = lax.axis_index("feat")
    panel_blocks = width // BLK
    list_length = pattern.shape[0]
    per_device = list_length // feat_count
    scale = 1.0 / (tok_rows * tok_count)
    ordered = jnp.zeros_like(pattern).at[block_slot].set(pattern)
    pairs = ordered.reshape(feat_count, per_device, 2)
    holder = pairs[:, :, 1] // panel_blocks
    local_column = pairs[:, :, 1] % panel_blocks
    picked = jnp.sum(jnp.where(holder == my_index, local_column, 0), axis=1)
    my_pairs = lax.dynamic_index_in_dim(pairs, my_index, 0, keepdims=False)
    my_holder = my_pairs[:, 1] // panel_blocks
    rowblk = my_pairs[:, 0] % panel_blocks
    out = fused(my_holder, rowblk, picked, activations, feat_count, tok_count, scale)
    return out.transpose(1, 0, 2)


def solution(mesh):
    placed = (P("tok", "feat"), P(), P())
    return jax.shard_map(
        body, mesh=mesh, in_specs=placed, out_specs=P("tok", "feat", None), check_vma=False
    )
```

```python
import functools

import jax
import jax.numpy as jnp
from jax import lax
from jax.experimental import pallas as pl
from jax.experimental.pallas import tpu as pltpu
from jax.sharding import PartitionSpec as P

BLK = 512
CHUNKS = 4
MESH = pl.DeviceIdType.MESH


def fused_kernel(n_feat, n_tok, chunks, scale,
                 holder_ref, rowblk_ref, picked_ref, act_hbm, out_ref, *scratch):
    recv = scratch[:chunks]
    (act_ref, send_ref, gbuf, st0, s1buf, st1, s2buf, st2, panel_sem,
     fsend, frecv, flocal, send0, recv0, send1, recv1, send2, recv2) = scratch[chunks:]
    slots = holder_ref.shape[0]
    tokens, width = send_ref.shape[1], send_ref.shape[2]
    panel_blocks = act_ref.shape[0]
    w = width // chunks
    n_y = n_tok // 4
    piece = width // n_tok
    me = lax.axis_index("feat")
    t = lax.axis_index("tok")
    x = t // (2 * n_y)
    y = (t // 2) % n_y
    core = t % 2
    core_peer = t + 1 - 2 * core
    x_peer = t + (1 - 2 * x) * 2 * n_y

    barrier = pltpu.get_barrier_semaphore()
    for k in range(1, n_feat):
        pl.semaphore_signal(barrier, 1, device_id={"feat": lax.rem(me + k, n_feat)}, device_id_type=MESH)
    for o in range(1, n_y):
        dest = x * 2 * n_y + lax.rem(y + o, n_y) * 2 + core
        pl.semaphore_signal(barrier, 1, device_id={"tok": dest}, device_id_type=MESH)
    pl.semaphore_signal(barrier, 1, device_id={"tok": core_peer}, device_id_type=MESH)
    pl.semaphore_signal(barrier, 1, device_id={"tok": x_peer}, device_id_type=MESH)

    panel = [
        pltpu.make_async_copy(act_hbm.at[:, pl.ds(b * width, width)], act_ref.at[b], panel_sem.at[b])
        for b in range(panel_blocks)
    ]
    for cp in panel:
        cp.start()
    for cp in panel:
        cp.wait()
    for p in range(n_feat):
        send_ref[p] = act_ref[picked_ref[p]]

    pl.semaphore_wait(barrier, n_feat - 1 + n_y - 1 + 2)

    def feat_copies(c):
        cols = pl.ds(c * w, w)
        local = pltpu.make_async_copy(send_ref.at[me, :, cols], recv[c].at[me], flocal.at[c])
        copies = [local]
        for k in range(1, n_feat):
            peer = lax.rem(me + k, n_feat)
            copies.append(pltpu.make_async_remote_copy(
                src_ref=send_ref.at[peer, :, cols],
                dst_ref=recv[c].at[me],
                send_sem=fsend.at[c, k],
                recv_sem=frecv.at[c, k],
                device_id={"feat": peer},
                device_id_type=MESH,
            ))
        return copies

    in_flight = []
    for c in range(min(2, chunks)):
        in_flight.append(feat_copies(c))
        for cp in in_flight[-1]:
            cp.start()
    for c in range(chunks):
        for cp in in_flight[c]:
            cp.wait()
        if c + 2 < chunks:
            in_flight.append(feat_copies(c + 2))
            for cp in in_flight[-1]:
                cp.start()

        def gram_one(k, carry):
            q = recv[c][holder_ref[k]]
            p = act_ref[rowblk_ref[k]]
            g = lax.dot_general(
                p, q, (((0,), (0,)), ((), ())), preferred_element_type=jnp.float32
            ) * scale
            for xx in range(2):
                for yy in range(n_y):
                    for cc in range(2):
                        r0 = ((xx * n_y + yy) * 2 + cc) * piece
                        gbuf[cc, yy, xx, k] = g[r0:r0 + piece, :]
            return carry

        lax.fori_loop(0, slots, gram_one, 0)

        cp0 = pltpu.make_async_remote_copy(
            src_ref=gbuf.at[1 - core],
            dst_ref=st0.at[c],
            send_sem=send0.at[c],
            recv_sem=recv0.at[c],
            device_id={"tok": core_peer},
            device_id_type=MESH,
        )
        cp0.start()
        cp0.wait()
        s1buf[...] = gbuf[core] + st0[c]

        copies1 = []
        for o in range(1, n_y):
            dy = lax.rem(y + o, n_y)
            cp = pltpu.make_async_remote_copy(
                src_ref=s1buf.at[dy],
                dst_ref=st1.at[c, y],
                send_sem=send1.at[c, o],
                recv_sem=recv1.at[c, o],
                device_id={"tok": x * 2 * n_y + dy * 2 + core},
                device_id_type=MESH,
            )
            cp.start()
            copies1.append(cp)
        for cp in copies1:
            cp.wait()
        acc = s1buf[y]
        for o in range(1, n_y):
            acc = acc + st1[c, lax.rem(y + o, n_y)]
        s2buf[...] = acc

        cp2 = pltpu.make_async_remote_copy(
            src_ref=s2buf.at[1 - x],
            dst_ref=st2.at[c],
            send_sem=send2.at[c],
            recv_sem=recv2.at[c],
            device_id={"tok": x_peer},
            device_id_type=MESH,
        )
        cp2.start()
        cp2.wait()
        out_ref[:, :, pl.ds(c * w, w)] = s2buf[x] + st2[c]


def fused(holder, rowblk, picked, activations, n_feat, n_tok, scale):
    slots = holder.shape[0]
    tokens, width = activations.shape[0], BLK
    panel_blocks = activations.shape[1] // BLK
    w = width // CHUNKS
    n_y = n_tok // 4
    piece = width // n_tok
    kernel = functools.partial(fused_kernel, n_feat, n_tok, CHUNKS, scale)
    blk = (slots, piece, w)
    return pl.pallas_call(
        kernel,
        out_shape=jax.ShapeDtypeStruct((slots, piece, width), jnp.float32),
        in_specs=[
            pl.BlockSpec(memory_space=pltpu.SMEM),
            pl.BlockSpec(memory_space=pltpu.SMEM),
            pl.BlockSpec(memory_space=pltpu.SMEM),
            pl.BlockSpec(memory_space=pl.ANY),
        ],
        out_specs=pl.BlockSpec(memory_space=pltpu.VMEM),
        scratch_shapes=[pltpu.VMEM((n_feat, tokens, w), activations.dtype) for _ in range(CHUNKS)] + [
            pltpu.VMEM((panel_blocks, tokens, width), activations.dtype),
            pltpu.VMEM((n_feat, tokens, width), activations.dtype),
            pltpu.VMEM((2, n_y, 2) + blk, jnp.float32),
            pltpu.VMEM((CHUNKS, n_y, 2) + blk, jnp.float32),
            pltpu.VMEM((n_y, 2) + blk, jnp.float32),
            pltpu.VMEM((CHUNKS, n_y, 2) + blk, jnp.float32),
            pltpu.VMEM((2,) + blk, jnp.float32),
            pltpu.VMEM((CHUNKS,) + blk, jnp.float32),
            pltpu.SemaphoreType.DMA((panel_blocks,)),
            pltpu.SemaphoreType.DMA((CHUNKS, n_feat)),
            pltpu.SemaphoreType.DMA((CHUNKS, n_feat)),
            pltpu.SemaphoreType.DMA((CHUNKS,)),
            pltpu.SemaphoreType.DMA((CHUNKS,)),
            pltpu.SemaphoreType.DMA((CHUNKS,)),
            pltpu.SemaphoreType.DMA((CHUNKS, n_y)),
            pltpu.SemaphoreType.DMA((CHUNKS, n_y)),
            pltpu.SemaphoreType.DMA((CHUNKS,)),
            pltpu.SemaphoreType.DMA((CHUNKS,)),
        ],
        compiler_params=pltpu.CompilerParams(
            collective_id=0, has_side_effects=True, vmem_limit_bytes=60 * 1024 * 1024
        ),
    )(holder, rowblk, picked, activations)


def body(activations, pattern, block_slot):
    tok_rows, width = activations.shape
    feat_count = lax.axis_size("feat")
    tok_count = lax.axis_size("tok")
    my_index = lax.axis_index("feat")
    panel_blocks = width // BLK
    list_length = pattern.shape[0]
    per_device = list_length // feat_count
    scale = 1.0 / (tok_rows * tok_count)
    ordered = jnp.zeros_like(pattern).at[block_slot].set(pattern)
    pairs = ordered.reshape(feat_count, per_device, 2)
    holder = pairs[:, :, 1] // panel_blocks
    local_column = pairs[:, :, 1] % panel_blocks
    picked = jnp.sum(jnp.where(holder == my_index, local_column, 0), axis=1)
    my_pairs = lax.dynamic_index_in_dim(pairs, my_index, 0, keepdims=False)
    my_holder = my_pairs[:, 1] // panel_blocks
    rowblk = my_pairs[:, 0] % panel_blocks
    out = fused(my_holder, rowblk, picked, activations, feat_count, tok_count, scale)
    return out.transpose(1, 0, 2)


def solution(mesh):
    placed = (P("tok", "feat"), P(), P())
    return jax.shard_map(
        body, mesh=mesh, in_specs=placed, out_specs=P("tok", "feat", None), check_vma=False
    )
```

```python
import functools

import jax
import jax.numpy as jnp
from jax import lax
from jax.experimental import pallas as pl
from jax.experimental.pallas import tpu as pltpu
from jax.sharding import PartitionSpec as P

BLK = 512
CHUNKS = 4
MESH = pl.DeviceIdType.MESH


def fused_kernel(n_feat, n_tok, chunks, scale,
                 holder_ref, rowblk_ref, picked_ref, act_hbm, out_ref, *scratch):
    recv = scratch[:chunks]
    (act_ref, actt_ref, send_ref, gbuf, st0, s1buf, st1, s2buf, st2, panel_sem,
     fsend, frecv, flocal, send0, recv0, send1, recv1, send2, recv2) = scratch[chunks:]
    slots = holder_ref.shape[0]
    tokens, width = send_ref.shape[1], send_ref.shape[2]
    panel_blocks = act_ref.shape[0]
    w = width // chunks
    n_y = n_tok // 4
    piece = width // n_tok
    me = lax.axis_index("feat")
    t = lax.axis_index("tok")
    x = t // (2 * n_y)
    y = (t // 2) % n_y
    core = t % 2
    core_peer = t + 1 - 2 * core
    x_peer = t + (1 - 2 * x) * 2 * n_y

    barrier = pltpu.get_barrier_semaphore()
    for k in range(1, n_feat):
        pl.semaphore_signal(barrier, 1, device_id={"feat": lax.rem(me + k, n_feat)}, device_id_type=MESH)
    for o in range(1, n_y):
        dest = x * 2 * n_y + lax.rem(y + o, n_y) * 2 + core
        pl.semaphore_signal(barrier, 1, device_id={"tok": dest}, device_id_type=MESH)
    pl.semaphore_signal(barrier, 1, device_id={"tok": core_peer}, device_id_type=MESH)
    pl.semaphore_signal(barrier, 1, device_id={"tok": x_peer}, device_id_type=MESH)

    panel = [
        pltpu.make_async_copy(act_hbm.at[:, pl.ds(b * width, width)], act_ref.at[b], panel_sem.at[b])
        for b in range(panel_blocks)
    ]
    for cp in panel:
        cp.start()
    for cp in panel:
        cp.wait()
    for p in range(n_feat):
        send_ref[p] = act_ref[picked_ref[p]]
    for b in range(panel_blocks):
        actt_ref[b] = act_ref[b].T

    pl.semaphore_wait(barrier, n_feat - 1 + n_y - 1 + 2)

    def feat_copies(c):
        cols = pl.ds(c * w, w)
        local = pltpu.make_async_copy(send_ref.at[me, :, cols], recv[c].at[me], flocal.at[c])
        copies = [local]
        for k in range(1, n_feat):
            peer = lax.rem(me + k, n_feat)
            copies.append(pltpu.make_async_remote_copy(
                src_ref=send_ref.at[peer, :, cols],
                dst_ref=recv[c].at[me],
                send_sem=fsend.at[c, k],
                recv_sem=frecv.at[c, k],
                device_id={"feat": peer},
                device_id_type=MESH,
            ))
        return copies

    in_flight = []
    for c in range(min(2, chunks)):
        in_flight.append(feat_copies(c))
        for cp in in_flight[-1]:
            cp.start()
    for c in range(chunks):
        for cp in in_flight[c]:
            cp.wait()
        if c + 2 < chunks:
            in_flight.append(feat_copies(c + 2))
            for cp in in_flight[-1]:
                cp.start()

        def gram_one(k, carry):
            q = recv[c][holder_ref[k]]
            p = actt_ref[rowblk_ref[k]]
            g = jnp.dot(p, q, preferred_element_type=jnp.float32) * scale
            for xx in range(2):
                for yy in range(n_y):
                    for cc in range(2):
                        r0 = ((xx * n_y + yy) * 2 + cc) * piece
                        gbuf[cc, yy, xx, k] = g[r0:r0 + piece, :]
            return carry

        lax.fori_loop(0, slots, gram_one, 0)

        cp0 = pltpu.make_async_remote_copy(
            src_ref=gbuf.at[1 - core],
            dst_ref=st0.at[c],
            send_sem=send0.at[c],
            recv_sem=recv0.at[c],
            device_id={"tok": core_peer},
            device_id_type=MESH,
        )
        cp0.start()
        cp0.wait()
        s1buf[...] = gbuf[core] + st0[c]

        copies1 = []
        for o in range(1, n_y):
            dy = lax.rem(y + o, n_y)
            cp = pltpu.make_async_remote_copy(
                src_ref=s1buf.at[dy],
                dst_ref=st1.at[c, y],
                send_sem=send1.at[c, o],
                recv_sem=recv1.at[c, o],
                device_id={"tok": x * 2 * n_y + dy * 2 + core},
                device_id_type=MESH,
            )
            cp.start()
            copies1.append(cp)
        for cp in copies1:
            cp.wait()
        acc = s1buf[y]
        for o in range(1, n_y):
            acc = acc + st1[c, lax.rem(y + o, n_y)]
        s2buf[...] = acc

        cp2 = pltpu.make_async_remote_copy(
            src_ref=s2buf.at[1 - x],
            dst_ref=st2.at[c],
            send_sem=send2.at[c],
            recv_sem=recv2.at[c],
            device_id={"tok": x_peer},
            device_id_type=MESH,
        )
        cp2.start()
        cp2.wait()
        out_ref[:, :, pl.ds(c * w, w)] = s2buf[x] + st2[c]


def fused(holder, rowblk, picked, activations, n_feat, n_tok, scale):
    slots = holder.shape[0]
    tokens, width = activations.shape[0], BLK
    panel_blocks = activations.shape[1] // BLK
    w = width // CHUNKS
    n_y = n_tok // 4
    piece = width // n_tok
    kernel = functools.partial(fused_kernel, n_feat, n_tok, CHUNKS, scale)
    blk = (slots, piece, w)
    return pl.pallas_call(
        kernel,
        out_shape=jax.ShapeDtypeStruct((slots, piece, width), jnp.float32),
        in_specs=[
            pl.BlockSpec(memory_space=pltpu.SMEM),
            pl.BlockSpec(memory_space=pltpu.SMEM),
            pl.BlockSpec(memory_space=pltpu.SMEM),
            pl.BlockSpec(memory_space=pl.ANY),
        ],
        out_specs=pl.BlockSpec(memory_space=pltpu.VMEM),
        scratch_shapes=[pltpu.VMEM((n_feat, tokens, w), activations.dtype) for _ in range(CHUNKS)] + [
            pltpu.VMEM((panel_blocks, tokens, width), activations.dtype),
            pltpu.VMEM((panel_blocks, width, tokens), activations.dtype),
            pltpu.VMEM((n_feat, tokens, width), activations.dtype),
            pltpu.VMEM((2, n_y, 2) + blk, jnp.float32),
            pltpu.VMEM((CHUNKS, n_y, 2) + blk, jnp.float32),
            pltpu.VMEM((n_y, 2) + blk, jnp.float32),
            pltpu.VMEM((CHUNKS, n_y, 2) + blk, jnp.float32),
            pltpu.VMEM((2,) + blk, jnp.float32),
            pltpu.VMEM((CHUNKS,) + blk, jnp.float32),
            pltpu.SemaphoreType.DMA((panel_blocks,)),
            pltpu.SemaphoreType.DMA((CHUNKS, n_feat)),
            pltpu.SemaphoreType.DMA((CHUNKS, n_feat)),
            pltpu.SemaphoreType.DMA((CHUNKS,)),
            pltpu.SemaphoreType.DMA((CHUNKS,)),
            pltpu.SemaphoreType.DMA((CHUNKS,)),
            pltpu.SemaphoreType.DMA((CHUNKS, n_y)),
            pltpu.SemaphoreType.DMA((CHUNKS, n_y)),
            pltpu.SemaphoreType.DMA((CHUNKS,)),
            pltpu.SemaphoreType.DMA((CHUNKS,)),
        ],
        compiler_params=pltpu.CompilerParams(
            collective_id=0, has_side_effects=True, vmem_limit_bytes=60 * 1024 * 1024
        ),
    )(holder, rowblk, picked, activations)


def body(activations, pattern, block_slot):
    tok_rows, width = activations.shape
    feat_count = lax.axis_size("feat")
    tok_count = lax.axis_size("tok")
    my_index = lax.axis_index("feat")
    panel_blocks = width // BLK
    list_length = pattern.shape[0]
    per_device = list_length // feat_count
    scale = 1.0 / (tok_rows * tok_count)
    ordered = jnp.zeros_like(pattern).at[block_slot].set(pattern)
    pairs = ordered.reshape(feat_count, per_device, 2)
    holder = pairs[:, :, 1] // panel_blocks
    local_column = pairs[:, :, 1] % panel_blocks
    picked = jnp.sum(jnp.where(holder == my_index, local_column, 0), axis=1)
    my_pairs = lax.dynamic_index_in_dim(pairs, my_index, 0, keepdims=False)
    my_holder = my_pairs[:, 1] // panel_blocks
    rowblk = my_pairs[:, 0] % panel_blocks
    out = fused(my_holder, rowblk, picked, activations, feat_count, tok_count, scale)
    return out.transpose(1, 0, 2)


def solution(mesh):
    placed = (P("tok", "feat"), P(), P())
    return jax.shard_map(
        body, mesh=mesh, in_specs=placed, out_specs=P("tok", "feat", None), check_vma=False
    )
```

```python
import functools

import jax
import jax.numpy as jnp
from jax import lax
from jax.experimental import pallas as pl
from jax.experimental.pallas import tpu as pltpu
from jax.sharding import PartitionSpec as P

BLK = 512
CHUNKS = 4
MESH = pl.DeviceIdType.MESH


def fused_kernel(n_feat, n_tok, chunks, scale,
                 holder_ref, rowblk_ref, picked_ref, act_hbm, out_ref, *scratch):
    recv = scratch[:chunks]
    (act_ref, send_ref, gbuf, st0, s1buf, st1, s2buf, st2, panel_sem,
     fsend, frecv, flocal, send0, recv0, send1, recv1, send2, recv2,
     bxbuf, bsum, bybuf, bsem, bysend, byrecv) = scratch[chunks:]
    slots = holder_ref.shape[0]
    tokens, width = send_ref.shape[1], send_ref.shape[2]
    panel_blocks = act_ref.shape[0]
    w = width // chunks
    n_y = n_tok // 4
    piece = width // n_tok
    me = lax.axis_index("feat")
    t = lax.axis_index("tok")
    x = t // (2 * n_y)
    y = (t // 2) % n_y
    core = t % 2
    core_peer = t + 1 - 2 * core
    x_peer = t + (1 - 2 * x) * 2 * n_y

    barrier = pltpu.get_barrier_semaphore()
    for k in range(1, n_feat):
        pl.semaphore_signal(barrier, 1, device_id={"feat": lax.rem(me + k, n_feat)}, device_id_type=MESH)
    for o in range(1, n_y):
        dest = x * 2 * n_y + lax.rem(y + o, n_y) * 2 + core
        pl.semaphore_signal(barrier, 1, device_id={"tok": dest}, device_id_type=MESH)
    pl.semaphore_signal(barrier, 1, device_id={"tok": core_peer}, device_id_type=MESH)
    pl.semaphore_signal(barrier, 1, device_id={"tok": x_peer}, device_id_type=MESH)

    panel = [
        pltpu.make_async_copy(act_hbm.at[:, pl.ds(b * width, width)], act_ref.at[b], panel_sem.at[b])
        for b in range(panel_blocks)
    ]
    for cp in panel:
        cp.start()
    for cp in panel:
        cp.wait()
    for p in range(n_feat):
        send_ref[p] = act_ref[picked_ref[p]]

    pl.semaphore_wait(barrier, n_feat - 1 + n_y - 1 + 2)

    def feat_copies(c):
        cols = pl.ds(c * w, w)
        local = pltpu.make_async_copy(send_ref.at[me, :, cols], recv[c].at[me], flocal.at[c])
        copies = [local]
        for k in range(1, n_feat):
            peer = lax.rem(me + k, n_feat)
            copies.append(pltpu.make_async_remote_copy(
                src_ref=send_ref.at[peer, :, cols],
                dst_ref=recv[c].at[me],
                send_sem=fsend.at[c, k],
                recv_sem=frecv.at[c, k],
                device_id={"feat": peer},
                device_id_type=MESH,
            ))
        return copies

    def reduce_last(c):
        h = slots // 2
        cols = pl.ds(c * w, w)
        cp0 = pltpu.make_async_remote_copy(
            src_ref=gbuf.at[1 - core], dst_ref=st0.at[c], send_sem=send0.at[c],
            recv_sem=recv0.at[c], device_id={"tok": core_peer}, device_id_type=MESH,
        )
        cp0.start()
        cp0.wait()
        s1buf[...] = gbuf[core] + st0[c]
        a_y = []
        for o in range(1, n_y):
            dy = lax.rem(y + o, n_y)
            cp = pltpu.make_async_remote_copy(
                src_ref=s1buf.at[dy, :, pl.ds(0, h)], dst_ref=st1.at[c, y, :, pl.ds(0, h)],
                send_sem=send1.at[c, o], recv_sem=recv1.at[c, o],
                device_id={"tok": x * 2 * n_y + dy * 2 + core}, device_id_type=MESH,
            )
            cp.start()
            a_y.append(cp)
        b_x = pltpu.make_async_remote_copy(
            src_ref=s1buf.at[:, 1 - x, pl.ds(h, slots - h)], dst_ref=bxbuf,
            send_sem=bsem.at[0], recv_sem=bsem.at[1], device_id={"tok": x_peer}, device_id_type=MESH,
        )
        b_x.start()
        b_x.wait()
        bsum[...] = s1buf[:, x, h:] + bxbuf[...]
        b_y = []
        for o in range(1, n_y):
            dy = lax.rem(y + o, n_y)
            cp = pltpu.make_async_remote_copy(
                src_ref=bsum.at[dy], dst_ref=bybuf.at[y],
                send_sem=bysend.at[o], recv_sem=byrecv.at[o],
                device_id={"tok": x * 2 * n_y + dy * 2 + core}, device_id_type=MESH,
            )
            cp.start()
            b_y.append(cp)
        for cp in a_y:
            cp.wait()
        acc = s1buf[y, :, :h]
        for o in range(1, n_y):
            acc = acc + st1[c, lax.rem(y + o, n_y), :, :h]
        s2buf[:, :h] = acc
        a_x = pltpu.make_async_remote_copy(
            src_ref=s2buf.at[1 - x, pl.ds(0, h)], dst_ref=st2.at[c, pl.ds(0, h)],
            send_sem=send2.at[c], recv_sem=recv2.at[c], device_id={"tok": x_peer}, device_id_type=MESH,
        )
        a_x.start()
        for cp in b_y:
            cp.wait()
        accb = bsum[y]
        for o in range(1, n_y):
            accb = accb + bybuf[lax.rem(y + o, n_y)]
        out_ref[h:, :, cols] = accb
        a_x.wait()
        out_ref[:h, :, cols] = s2buf[x, :h] + st2[c, :h]

    in_flight = []
    for c in range(min(2, chunks)):
        in_flight.append(feat_copies(c))
        for cp in in_flight[-1]:
            cp.start()
    for c in range(chunks):
        for cp in in_flight[c]:
            cp.wait()
        if c + 2 < chunks:
            in_flight.append(feat_copies(c + 2))
            for cp in in_flight[-1]:
                cp.start()

        def gram_one(k, carry):
            q = recv[c][holder_ref[k]]
            p = act_ref[rowblk_ref[k]]
            g = lax.dot_general(
                p, q, (((0,), (0,)), ((), ())), preferred_element_type=jnp.float32
            ) * scale
            for xx in range(2):
                for yy in range(n_y):
                    for cc in range(2):
                        r0 = ((xx * n_y + yy) * 2 + cc) * piece
                        gbuf[cc, yy, xx, k] = g[r0:r0 + piece, :]
            return carry

        lax.fori_loop(0, slots, gram_one, 0)

        if c == chunks - 1 and slots > 1:
            reduce_last(c)
            continue

        cp0 = pltpu.make_async_remote_copy(
            src_ref=gbuf.at[1 - core],
            dst_ref=st0.at[c],
            send_sem=send0.at[c],
            recv_sem=recv0.at[c],
            device_id={"tok": core_peer},
            device_id_type=MESH,
        )
        cp0.start()
        cp0.wait()
        s1buf[...] = gbuf[core] + st0[c]

        copies1 = []
        for o in range(1, n_y):
            dy = lax.rem(y + o, n_y)
            cp = pltpu.make_async_remote_copy(
                src_ref=s1buf.at[dy],
                dst_ref=st1.at[c, y],
                send_sem=send1.at[c, o],
                recv_sem=recv1.at[c, o],
                device_id={"tok": x * 2 * n_y + dy * 2 + core},
                device_id_type=MESH,
            )
            cp.start()
            copies1.append(cp)
        for cp in copies1:
            cp.wait()
        acc = s1buf[y]
        for o in range(1, n_y):
            acc = acc + st1[c, lax.rem(y + o, n_y)]
        s2buf[...] = acc

        cp2 = pltpu.make_async_remote_copy(
            src_ref=s2buf.at[1 - x],
            dst_ref=st2.at[c],
            send_sem=send2.at[c],
            recv_sem=recv2.at[c],
            device_id={"tok": x_peer},
            device_id_type=MESH,
        )
        cp2.start()
        cp2.wait()
        out_ref[:, :, pl.ds(c * w, w)] = s2buf[x] + st2[c]


def fused(holder, rowblk, picked, activations, n_feat, n_tok, scale):
    slots = holder.shape[0]
    tokens, width = activations.shape[0], BLK
    panel_blocks = activations.shape[1] // BLK
    w = width // CHUNKS
    n_y = n_tok // 4
    piece = width // n_tok
    kernel = functools.partial(fused_kernel, n_feat, n_tok, CHUNKS, scale)
    blk = (slots, piece, w)
    return pl.pallas_call(
        kernel,
        out_shape=jax.ShapeDtypeStruct((slots, piece, width), jnp.float32),
        in_specs=[
            pl.BlockSpec(memory_space=pltpu.SMEM),
            pl.BlockSpec(memory_space=pltpu.SMEM),
            pl.BlockSpec(memory_space=pltpu.SMEM),
            pl.BlockSpec(memory_space=pl.ANY),
        ],
        out_specs=pl.BlockSpec(memory_space=pltpu.VMEM),
        scratch_shapes=[pltpu.VMEM((n_feat, tokens, w), activations.dtype) for _ in range(CHUNKS)] + [
            pltpu.VMEM((panel_blocks, tokens, width), activations.dtype),
            pltpu.VMEM((n_feat, tokens, width), activations.dtype),
            pltpu.VMEM((2, n_y, 2) + blk, jnp.float32),
            pltpu.VMEM((CHUNKS, n_y, 2) + blk, jnp.float32),
            pltpu.VMEM((n_y, 2) + blk, jnp.float32),
            pltpu.VMEM((CHUNKS, n_y, 2) + blk, jnp.float32),
            pltpu.VMEM((2,) + blk, jnp.float32),
            pltpu.VMEM((CHUNKS,) + blk, jnp.float32),
            pltpu.SemaphoreType.DMA((panel_blocks,)),
            pltpu.SemaphoreType.DMA((CHUNKS, n_feat)),
            pltpu.SemaphoreType.DMA((CHUNKS, n_feat)),
            pltpu.SemaphoreType.DMA((CHUNKS,)),
            pltpu.SemaphoreType.DMA((CHUNKS,)),
            pltpu.SemaphoreType.DMA((CHUNKS,)),
            pltpu.SemaphoreType.DMA((CHUNKS, n_y)),
            pltpu.SemaphoreType.DMA((CHUNKS, n_y)),
            pltpu.SemaphoreType.DMA((CHUNKS,)),
            pltpu.SemaphoreType.DMA((CHUNKS,)),
            pltpu.VMEM((n_y, slots - slots // 2, piece, w), jnp.float32),
            pltpu.VMEM((n_y, slots - slots // 2, piece, w), jnp.float32),
            pltpu.VMEM((n_y, slots - slots // 2, piece, w), jnp.float32),
            pltpu.SemaphoreType.DMA((2,)),
            pltpu.SemaphoreType.DMA((n_y,)),
            pltpu.SemaphoreType.DMA((n_y,)),
        ],
        compiler_params=pltpu.CompilerParams(
            collective_id=0, has_side_effects=True, vmem_limit_bytes=60 * 1024 * 1024
        ),
    )(holder, rowblk, picked, activations)


def body(activations, pattern, block_slot):
    tok_rows, width = activations.shape
    feat_count = lax.axis_size("feat")
    tok_count = lax.axis_size("tok")
    my_index = lax.axis_index("feat")
    panel_blocks = width // BLK
    list_length = pattern.shape[0]
    per_device = list_length // feat_count
    scale = 1.0 / (tok_rows * tok_count)
    ordered = jnp.zeros_like(pattern).at[block_slot].set(pattern)
    pairs = ordered.reshape(feat_count, per_device, 2)
    holder = pairs[:, :, 1] // panel_blocks
    local_column = pairs[:, :, 1] % panel_blocks
    picked = jnp.sum(jnp.where(holder == my_index, local_column, 0), axis=1)
    my_pairs = lax.dynamic_index_in_dim(pairs, my_index, 0, keepdims=False)
    my_holder = my_pairs[:, 1] // panel_blocks
    rowblk = my_pairs[:, 0] % panel_blocks
    out = fused(my_holder, rowblk, picked, activations, feat_count, tok_count, scale)
    return out.transpose(1, 0, 2)


def solution(mesh):
    placed = (P("tok", "feat"), P(), P())
    return jax.shard_map(
        body, mesh=mesh, in_specs=placed, out_specs=P("tok", "feat", None), check_vma=False
    )
```

```python
import functools

import jax
import jax.numpy as jnp
from jax import lax
from jax.experimental import pallas as pl
from jax.experimental.pallas import tpu as pltpu
from jax.sharding import PartitionSpec as P

BLK = 512
CHUNKS = 4
MESH = pl.DeviceIdType.MESH


def fused_kernel(n_feat, n_tok, chunks, scale,
                 holder_ref, rowblk_ref, picked_ref, act_hbm, out_ref, *scratch):
    recv = scratch[:chunks]
    (act_ref, send_ref, gbuf, st0, s1buf, st1, s2buf, st2, panel_sem,
     fsend, frecv, flocal, send0, recv0, send1, recv1, send2, recv2,
     bxbuf, bsum, bybuf, bsem, bysend, byrecv) = scratch[chunks:]
    slots = holder_ref.shape[0]
    tokens, width = send_ref.shape[1], send_ref.shape[2]
    panel_blocks = act_ref.shape[0]
    w = width // chunks
    n_y = n_tok // 4
    piece = width // n_tok
    me = lax.axis_index("feat")
    t = lax.axis_index("tok")
    x = t // (2 * n_y)
    y = (t // 2) % n_y
    core = t % 2
    core_peer = t + 1 - 2 * core
    x_peer = t + (1 - 2 * x) * 2 * n_y

    barrier = pltpu.get_barrier_semaphore()
    for k in range(1, n_feat):
        pl.semaphore_signal(barrier, 1, device_id={"feat": lax.rem(me + k, n_feat)}, device_id_type=MESH)
    for o in range(1, n_y):
        dest = x * 2 * n_y + lax.rem(y + o, n_y) * 2 + core
        pl.semaphore_signal(barrier, 1, device_id={"tok": dest}, device_id_type=MESH)
    pl.semaphore_signal(barrier, 1, device_id={"tok": core_peer}, device_id_type=MESH)
    pl.semaphore_signal(barrier, 1, device_id={"tok": x_peer}, device_id_type=MESH)

    panel = [
        pltpu.make_async_copy(act_hbm.at[:, pl.ds(b * width, width)], act_ref.at[b], panel_sem.at[b])
        for b in range(panel_blocks)
    ]
    for cp in panel:
        cp.start()
    for cp in panel:
        cp.wait()
    for p in range(n_feat):
        send_ref[p] = act_ref[picked_ref[p]]

    pl.semaphore_wait(barrier, n_feat - 1 + n_y - 1 + 2)

    def feat_copies(c):
        cols = pl.ds(c * w, w)
        local = pltpu.make_async_copy(send_ref.at[me, :, cols], recv[c].at[me], flocal.at[c])
        copies = [local]
        for k in range(1, n_feat):
            peer = lax.rem(me + k, n_feat)
            copies.append(pltpu.make_async_remote_copy(
                src_ref=send_ref.at[peer, :, cols],
                dst_ref=recv[c].at[me],
                send_sem=fsend.at[c, k],
                recv_sem=frecv.at[c, k],
                device_id={"feat": peer},
                device_id_type=MESH,
            ))
        return copies

    def reduce_last(c):
        h = slots // 2
        cols = pl.ds(c * w, w)
        cp0a = pltpu.make_async_remote_copy(
            src_ref=gbuf.at[1 - core, :, :, pl.ds(0, h)], dst_ref=st0.at[c, :, :, pl.ds(0, h)],
            send_sem=send0.at[c], recv_sem=recv0.at[c], device_id={"tok": core_peer}, device_id_type=MESH,
        )
        cp0b = pltpu.make_async_remote_copy(
            src_ref=gbuf.at[1 - core, :, :, pl.ds(h, slots - h)],
            dst_ref=st0.at[c, :, :, pl.ds(h, slots - h)],
            send_sem=bsem.at[2], recv_sem=bsem.at[3], device_id={"tok": core_peer}, device_id_type=MESH,
        )
        cp0a.start()
        cp0b.start()
        cp0a.wait()
        s1buf[:, :, :h] = gbuf[core, :, :, :h] + st0[c, :, :, :h]
        a_y = []
        for o in range(1, n_y):
            dy = lax.rem(y + o, n_y)
            cp = pltpu.make_async_remote_copy(
                src_ref=s1buf.at[dy, :, pl.ds(0, h)], dst_ref=st1.at[c, y, :, pl.ds(0, h)],
                send_sem=send1.at[c, o], recv_sem=recv1.at[c, o],
                device_id={"tok": x * 2 * n_y + dy * 2 + core}, device_id_type=MESH,
            )
            cp.start()
            a_y.append(cp)
        cp0b.wait()
        s1buf[:, :, h:] = gbuf[core, :, :, h:] + st0[c, :, :, h:]
        b_x = pltpu.make_async_remote_copy(
            src_ref=s1buf.at[:, 1 - x, pl.ds(h, slots - h)], dst_ref=bxbuf,
            send_sem=bsem.at[0], recv_sem=bsem.at[1], device_id={"tok": x_peer}, device_id_type=MESH,
        )
        b_x.start()
        b_x.wait()
        bsum[...] = s1buf[:, x, h:] + bxbuf[...]
        b_y = []
        for o in range(1, n_y):
            dy = lax.rem(y + o, n_y)
            cp = pltpu.make_async_remote_copy(
                src_ref=bsum.at[dy], dst_ref=bybuf.at[y],
                send_sem=bysend.at[o], recv_sem=byrecv.at[o],
                device_id={"tok": x * 2 * n_y + dy * 2 + core}, device_id_type=MESH,
            )
            cp.start()
            b_y.append(cp)
        for cp in a_y:
            cp.wait()
        acc = s1buf[y, :, :h]
        for o in range(1, n_y):
            acc = acc + st1[c, lax.rem(y + o, n_y), :, :h]
        s2buf[:, :h] = acc
        a_x = pltpu.make_async_remote_copy(
            src_ref=s2buf.at[1 - x, pl.ds(0, h)], dst_ref=st2.at[c, pl.ds(0, h)],
            send_sem=send2.at[c], recv_sem=recv2.at[c], device_id={"tok": x_peer}, device_id_type=MESH,
        )
        a_x.start()
        for cp in b_y:
            cp.wait()
        accb = bsum[y]
        for o in range(1, n_y):
            accb = accb + bybuf[lax.rem(y + o, n_y)]
        out_ref[h:, :, cols] = accb
        a_x.wait()
        out_ref[:h, :, cols] = s2buf[x, :h] + st2[c, :h]

    in_flight = []
    for c in range(min(2, chunks)):
        in_flight.append(feat_copies(c))
        for cp in in_flight[-1]:
            cp.start()
    for c in range(chunks):
        for cp in in_flight[c]:
            cp.wait()
        if c + 2 < chunks:
            in_flight.append(feat_copies(c + 2))
            for cp in in_flight[-1]:
                cp.start()

        def gram_one(k, carry):
            q = recv[c][holder_ref[k]]
            p = act_ref[rowblk_ref[k]]
            g = lax.dot_general(
                p, q, (((0,), (0,)), ((), ())), preferred_element_type=jnp.float32
            ) * scale
            for xx in range(2):
                for yy in range(n_y):
                    for cc in range(2):
                        r0 = ((xx * n_y + yy) * 2 + cc) * piece
                        gbuf[cc, yy, xx, k] = g[r0:r0 + piece, :]
            return carry

        lax.fori_loop(0, slots, gram_one, 0)

        if c == chunks - 1 and slots > 1:
            reduce_last(c)
            continue

        cp0 = pltpu.make_async_remote_copy(
            src_ref=gbuf.at[1 - core],
            dst_ref=st0.at[c],
            send_sem=send0.at[c],
            recv_sem=recv0.at[c],
            device_id={"tok": core_peer},
            device_id_type=MESH,
        )
        cp0.start()
        cp0.wait()
        s1buf[...] = gbuf[core] + st0[c]

        copies1 = []
        for o in range(1, n_y):
            dy = lax.rem(y + o, n_y)
            cp = pltpu.make_async_remote_copy(
                src_ref=s1buf.at[dy],
                dst_ref=st1.at[c, y],
                send_sem=send1.at[c, o],
                recv_sem=recv1.at[c, o],
                device_id={"tok": x * 2 * n_y + dy * 2 + core},
                device_id_type=MESH,
            )
            cp.start()
            copies1.append(cp)
        for cp in copies1:
            cp.wait()
        acc = s1buf[y]
        for o in range(1, n_y):
            acc = acc + st1[c, lax.rem(y + o, n_y)]
        s2buf[...] = acc

        cp2 = pltpu.make_async_remote_copy(
            src_ref=s2buf.at[1 - x],
            dst_ref=st2.at[c],
            send_sem=send2.at[c],
            recv_sem=recv2.at[c],
            device_id={"tok": x_peer},
            device_id_type=MESH,
        )
        cp2.start()
        cp2.wait()
        out_ref[:, :, pl.ds(c * w, w)] = s2buf[x] + st2[c]


def fused(holder, rowblk, picked, activations, n_feat, n_tok, scale):
    slots = holder.shape[0]
    tokens, width = activations.shape[0], BLK
    panel_blocks = activations.shape[1] // BLK
    w = width // CHUNKS
    n_y = n_tok // 4
    piece = width // n_tok
    kernel = functools.partial(fused_kernel, n_feat, n_tok, CHUNKS, scale)
    blk = (slots, piece, w)
    return pl.pallas_call(
        kernel,
        out_shape=jax.ShapeDtypeStruct((slots, piece, width), jnp.float32),
        in_specs=[
            pl.BlockSpec(memory_space=pltpu.SMEM),
            pl.BlockSpec(memory_space=pltpu.SMEM),
            pl.BlockSpec(memory_space=pltpu.SMEM),
            pl.BlockSpec(memory_space=pl.ANY),
        ],
        out_specs=pl.BlockSpec(memory_space=pltpu.VMEM),
        scratch_shapes=[pltpu.VMEM((n_feat, tokens, w), activations.dtype) for _ in range(CHUNKS)] + [
            pltpu.VMEM((panel_blocks, tokens, width), activations.dtype),
            pltpu.VMEM((n_feat, tokens, width), activations.dtype),
            pltpu.VMEM((2, n_y, 2) + blk, jnp.float32),
            pltpu.VMEM((CHUNKS, n_y, 2) + blk, jnp.float32),
            pltpu.VMEM((n_y, 2) + blk, jnp.float32),
            pltpu.VMEM((CHUNKS, n_y, 2) + blk, jnp.float32),
            pltpu.VMEM((2,) + blk, jnp.float32),
            pltpu.VMEM((CHUNKS,) + blk, jnp.float32),
            pltpu.SemaphoreType.DMA((panel_blocks,)),
            pltpu.SemaphoreType.DMA((CHUNKS, n_feat)),
            pltpu.SemaphoreType.DMA((CHUNKS, n_feat)),
            pltpu.SemaphoreType.DMA((CHUNKS,)),
            pltpu.SemaphoreType.DMA((CHUNKS,)),
            pltpu.SemaphoreType.DMA((CHUNKS,)),
            pltpu.SemaphoreType.DMA((CHUNKS, n_y)),
            pltpu.SemaphoreType.DMA((CHUNKS, n_y)),
            pltpu.SemaphoreType.DMA((CHUNKS,)),
            pltpu.SemaphoreType.DMA((CHUNKS,)),
            pltpu.VMEM((n_y, slots - slots // 2, piece, w), jnp.float32),
            pltpu.VMEM((n_y, slots - slots // 2, piece, w), jnp.float32),
            pltpu.VMEM((n_y, slots - slots // 2, piece, w), jnp.float32),
            pltpu.SemaphoreType.DMA((4,)),
            pltpu.SemaphoreType.DMA((n_y,)),
            pltpu.SemaphoreType.DMA((n_y,)),
        ],
        compiler_params=pltpu.CompilerParams(
            collective_id=0, has_side_effects=True, vmem_limit_bytes=60 * 1024 * 1024
        ),
    )(holder, rowblk, picked, activations)


def body(activations, pattern, block_slot):
    tok_rows, width = activations.shape
    feat_count = lax.axis_size("feat")
    tok_count = lax.axis_size("tok")
    my_index = lax.axis_index("feat")
    panel_blocks = width // BLK
    list_length = pattern.shape[0]
    per_device = list_length // feat_count
    scale = 1.0 / (tok_rows * tok_count)
    ordered = jnp.zeros_like(pattern).at[block_slot].set(pattern)
    pairs = ordered.reshape(feat_count, per_device, 2)
    holder = pairs[:, :, 1] // panel_blocks
    local_column = pairs[:, :, 1] % panel_blocks
    picked = jnp.sum(jnp.where(holder == my_index, local_column, 0), axis=1)
    my_pairs = lax.dynamic_index_in_dim(pairs, my_index, 0, keepdims=False)
    my_holder = my_pairs[:, 1] // panel_blocks
    rowblk = my_pairs[:, 0] % panel_blocks
    out = fused(my_holder, rowblk, picked, activations, feat_count, tok_count, scale)
    return out.transpose(1, 0, 2)


def solution(mesh):
    placed = (P("tok", "feat"), P(), P())
    return jax.shard_map(
        body, mesh=mesh, in_specs=placed, out_specs=P("tok", "feat", None), check_vma=False
    )
```

```python
import functools

import jax
import jax.numpy as jnp
from jax import lax
from jax.experimental import pallas as pl
from jax.experimental.pallas import tpu as pltpu
from jax.sharding import PartitionSpec as P

BLK = 512
CHUNKS = 4
MESH = pl.DeviceIdType.MESH


def fused_kernel(n_feat, n_tok, chunks, scale,
                 holder_ref, rowblk_ref, picked_ref, act_hbm, out_ref, *scratch):
    recv = scratch[:chunks]
    (act_ref, send_ref, gbuf, st0, s1buf, st1, s2buf, st2, panel_sem,
     fsend, frecv, flocal, send0, recv0, send1, recv1, send2, recv2,
     bxbuf, bsum, bybuf, bsem, bysend, byrecv) = scratch[chunks:]
    slots = holder_ref.shape[0]
    tokens, width = send_ref.shape[1], send_ref.shape[2]
    panel_blocks = act_ref.shape[0]
    w = width // chunks
    n_y = n_tok // 4
    piece = width // n_tok
    me = lax.axis_index("feat")
    t = lax.axis_index("tok")
    x = t // (2 * n_y)
    y = (t // 2) % n_y
    core = t % 2
    core_peer = t + 1 - 2 * core
    x_peer = t + (1 - 2 * x) * 2 * n_y

    barrier = pltpu.get_barrier_semaphore()
    for k in range(1, n_feat):
        pl.semaphore_signal(barrier, 1, device_id={"feat": lax.rem(me + k, n_feat)}, device_id_type=MESH)
    for o in range(1, n_y):
        dest = x * 2 * n_y + lax.rem(y + o, n_y) * 2 + core
        pl.semaphore_signal(barrier, 1, device_id={"tok": dest}, device_id_type=MESH)
    pl.semaphore_signal(barrier, 1, device_id={"tok": core_peer}, device_id_type=MESH)
    pl.semaphore_signal(barrier, 1, device_id={"tok": x_peer}, device_id_type=MESH)

    panel = [
        pltpu.make_async_copy(act_hbm.at[:, pl.ds(b * width, width)], act_ref.at[b], panel_sem.at[b])
        for b in range(panel_blocks)
    ]
    for cp in panel:
        cp.start()
    for cp in panel:
        cp.wait()
    for p in range(n_feat):
        send_ref[p] = act_ref[picked_ref[p]]

    pl.semaphore_wait(barrier, n_feat - 1 + n_y - 1 + 2)

    def feat_copies(c):
        cols = pl.ds(c * w, w)
        local = pltpu.make_async_copy(send_ref.at[me, :, cols], recv[c].at[me], flocal.at[c])
        copies = [local]
        for k in sorted(range(1, n_feat), key=lambda k: -min(k, n_feat - k)):
            peer = lax.rem(me + k, n_feat)
            copies.append(pltpu.make_async_remote_copy(
                src_ref=send_ref.at[peer, :, cols],
                dst_ref=recv[c].at[me],
                send_sem=fsend.at[c, k],
                recv_sem=frecv.at[c, k],
                device_id={"feat": peer},
                device_id_type=MESH,
            ))
        return copies

    def reduce_last(c):
        h = slots // 2
        cols = pl.ds(c * w, w)
        cp0 = pltpu.make_async_remote_copy(
            src_ref=gbuf.at[1 - core], dst_ref=st0.at[c], send_sem=send0.at[c],
            recv_sem=recv0.at[c], device_id={"tok": core_peer}, device_id_type=MESH,
        )
        cp0.start()
        cp0.wait()
        s1buf[...] = gbuf[core] + st0[c]
        a_y = []
        for o in range(1, n_y):
            dy = lax.rem(y + o, n_y)
            cp = pltpu.make_async_remote_copy(
                src_ref=s1buf.at[dy, :, pl.ds(0, h)], dst_ref=st1.at[c, y, :, pl.ds(0, h)],
                send_sem=send1.at[c, o], recv_sem=recv1.at[c, o],
                device_id={"tok": x * 2 * n_y + dy * 2 + core}, device_id_type=MESH,
            )
            cp.start()
            a_y.append(cp)
        b_x = pltpu.make_async_remote_copy(
            src_ref=s1buf.at[:, 1 - x, pl.ds(h, slots - h)], dst_ref=bxbuf,
            send_sem=bsem.at[0], recv_sem=bsem.at[1], device_id={"tok": x_peer}, device_id_type=MESH,
        )
        b_x.start()
        b_x.wait()
        bsum[...] = s1buf[:, x, h:] + bxbuf[...]
        b_y = []
        for o in range(1, n_y):
            dy = lax.rem(y + o, n_y)
            cp = pltpu.make_async_remote_copy(
                src_ref=bsum.at[dy], dst_ref=bybuf.at[y],
                send_sem=bysend.at[o], recv_sem=byrecv.at[o],
                device_id={"tok": x * 2 * n_y + dy * 2 + core}, device_id_type=MESH,
            )
            cp.start()
            b_y.append(cp)
        for cp in a_y:
            cp.wait()
        acc = s1buf[y, :, :h]
        for o in range(1, n_y):
            acc = acc + st1[c, lax.rem(y + o, n_y), :, :h]
        s2buf[:, :h] = acc
        a_x = pltpu.make_async_remote_copy(
            src_ref=s2buf.at[1 - x, pl.ds(0, h)], dst_ref=st2.at[c, pl.ds(0, h)],
            send_sem=send2.at[c], recv_sem=recv2.at[c], device_id={"tok": x_peer}, device_id_type=MESH,
        )
        a_x.start()
        for cp in b_y:
            cp.wait()
        accb = bsum[y]
        for o in range(1, n_y):
            accb = accb + bybuf[lax.rem(y + o, n_y)]
        out_ref[h:, :, cols] = accb
        a_x.wait()
        out_ref[:h, :, cols] = s2buf[x, :h] + st2[c, :h]

    in_flight = []
    for c in range(min(2, chunks)):
        in_flight.append(feat_copies(c))
        for cp in in_flight[-1]:
            cp.start()
    for c in range(chunks):
        for cp in in_flight[c]:
            cp.wait()
        if c + 2 < chunks:
            in_flight.append(feat_copies(c + 2))
            for cp in in_flight[-1]:
                cp.start()

        def gram_one(k, carry):
            q = recv[c][holder_ref[k]]
            p = act_ref[rowblk_ref[k]]
            g = lax.dot_general(
                p, q, (((0,), (0,)), ((), ())), preferred_element_type=jnp.float32
            ) * scale
            for xx in range(2):
                for yy in range(n_y):
                    for cc in range(2):
                        r0 = ((xx * n_y + yy) * 2 + cc) * piece
                        gbuf[cc, yy, xx, k] = g[r0:r0 + piece, :]
            return carry

        lax.fori_loop(0, slots, gram_one, 0)

        if c == chunks - 1 and slots > 1:
            reduce_last(c)
            continue

        cp0 = pltpu.make_async_remote_copy(
            src_ref=gbuf.at[1 - core],
            dst_ref=st0.at[c],
            send_sem=send0.at[c],
            recv_sem=recv0.at[c],
            device_id={"tok": core_peer},
            device_id_type=MESH,
        )
        cp0.start()
        cp0.wait()
        s1buf[...] = gbuf[core] + st0[c]

        copies1 = []
        for o in range(1, n_y):
            dy = lax.rem(y + o, n_y)
            cp = pltpu.make_async_remote_copy(
                src_ref=s1buf.at[dy],
                dst_ref=st1.at[c, y],
                send_sem=send1.at[c, o],
                recv_sem=recv1.at[c, o],
                device_id={"tok": x * 2 * n_y + dy * 2 + core},
                device_id_type=MESH,
            )
            cp.start()
            copies1.append(cp)
        for cp in copies1:
            cp.wait()
        acc = s1buf[y]
        for o in range(1, n_y):
            acc = acc + st1[c, lax.rem(y + o, n_y)]
        s2buf[...] = acc

        cp2 = pltpu.make_async_remote_copy(
            src_ref=s2buf.at[1 - x],
            dst_ref=st2.at[c],
            send_sem=send2.at[c],
            recv_sem=recv2.at[c],
            device_id={"tok": x_peer},
            device_id_type=MESH,
        )
        cp2.start()
        cp2.wait()
        out_ref[:, :, pl.ds(c * w, w)] = s2buf[x] + st2[c]


def fused(holder, rowblk, picked, activations, n_feat, n_tok, scale):
    slots = holder.shape[0]
    tokens, width = activations.shape[0], BLK
    panel_blocks = activations.shape[1] // BLK
    w = width // CHUNKS
    n_y = n_tok // 4
    piece = width // n_tok
    kernel = functools.partial(fused_kernel, n_feat, n_tok, CHUNKS, scale)
    blk = (slots, piece, w)
    return pl.pallas_call(
        kernel,
        out_shape=jax.ShapeDtypeStruct((slots, piece, width), jnp.float32),
        in_specs=[
            pl.BlockSpec(memory_space=pltpu.SMEM),
            pl.BlockSpec(memory_space=pltpu.SMEM),
            pl.BlockSpec(memory_space=pltpu.SMEM),
            pl.BlockSpec(memory_space=pl.ANY),
        ],
        out_specs=pl.BlockSpec(memory_space=pltpu.VMEM),
        scratch_shapes=[pltpu.VMEM((n_feat, tokens, w), activations.dtype) for _ in range(CHUNKS)] + [
            pltpu.VMEM((panel_blocks, tokens, width), activations.dtype),
            pltpu.VMEM((n_feat, tokens, width), activations.dtype),
            pltpu.VMEM((2, n_y, 2) + blk, jnp.float32),
            pltpu.VMEM((CHUNKS, n_y, 2) + blk, jnp.float32),
            pltpu.VMEM((n_y, 2) + blk, jnp.float32),
            pltpu.VMEM((CHUNKS, n_y, 2) + blk, jnp.float32),
            pltpu.VMEM((2,) + blk, jnp.float32),
            pltpu.VMEM((CHUNKS,) + blk, jnp.float32),
            pltpu.SemaphoreType.DMA((panel_blocks,)),
            pltpu.SemaphoreType.DMA((CHUNKS, n_feat)),
            pltpu.SemaphoreType.DMA((CHUNKS, n_feat)),
            pltpu.SemaphoreType.DMA((CHUNKS,)),
            pltpu.SemaphoreType.DMA((CHUNKS,)),
            pltpu.SemaphoreType.DMA((CHUNKS,)),
            pltpu.SemaphoreType.DMA((CHUNKS, n_y)),
            pltpu.SemaphoreType.DMA((CHUNKS, n_y)),
            pltpu.SemaphoreType.DMA((CHUNKS,)),
            pltpu.SemaphoreType.DMA((CHUNKS,)),
            pltpu.VMEM((n_y, slots - slots // 2, piece, w), jnp.float32),
            pltpu.VMEM((n_y, slots - slots // 2, piece, w), jnp.float32),
            pltpu.VMEM((n_y, slots - slots // 2, piece, w), jnp.float32),
            pltpu.SemaphoreType.DMA((2,)),
            pltpu.SemaphoreType.DMA((n_y,)),
            pltpu.SemaphoreType.DMA((n_y,)),
        ],
        compiler_params=pltpu.CompilerParams(
            collective_id=0, has_side_effects=True, vmem_limit_bytes=60 * 1024 * 1024
        ),
    )(holder, rowblk, picked, activations)


def body(activations, pattern, block_slot):
    tok_rows, width = activations.shape
    feat_count = lax.axis_size("feat")
    tok_count = lax.axis_size("tok")
    my_index = lax.axis_index("feat")
    panel_blocks = width // BLK
    list_length = pattern.shape[0]
    per_device = list_length // feat_count
    scale = 1.0 / (tok_rows * tok_count)
    ordered = jnp.zeros_like(pattern).at[block_slot].set(pattern)
    pairs = ordered.reshape(feat_count, per_device, 2)
    holder = pairs[:, :, 1] // panel_blocks
    local_column = pairs[:, :, 1] % panel_blocks
    picked = jnp.sum(jnp.where(holder == my_index, local_column, 0), axis=1)
    my_pairs = lax.dynamic_index_in_dim(pairs, my_index, 0, keepdims=False)
    my_holder = my_pairs[:, 1] // panel_blocks
    rowblk = my_pairs[:, 0] % panel_blocks
    out = fused(my_holder, rowblk, picked, activations, feat_count, tok_count, scale)
    return out.transpose(1, 0, 2)


def solution(mesh):
    placed = (P("tok", "feat"), P(), P())
    return jax.shard_map(
        body, mesh=mesh, in_specs=placed, out_specs=P("tok", "feat", None), check_vma=False
    )
```

```python
import functools

import jax
import jax.numpy as jnp
from jax import lax
from jax.experimental import pallas as pl
from jax.experimental.pallas import tpu as pltpu
from jax.sharding import PartitionSpec as P

BLK = 512
CHUNKS = 4
MESH = pl.DeviceIdType.MESH


def fused_kernel(n_feat, n_tok, chunks, scale,
                 holder_ref, rowblk_ref, picked_ref, act_hbm, out_ref, *scratch):
    recv = scratch[:chunks]
    (act_ref, send_ref, gbuf, st0, s1buf, st1, s2buf, st2, panel_sem,
     fsend, frecv, flocal, send0, recv0, send1, recv1, send2, recv2,
     bxbuf, bsum, bybuf, bsem, bysend, byrecv) = scratch[chunks:]
    slots = holder_ref.shape[0]
    tokens, width = send_ref.shape[1], send_ref.shape[2]
    panel_blocks = act_ref.shape[0]
    w = width // chunks
    n_y = n_tok // 4
    piece = width // n_tok
    me = lax.axis_index("feat")
    t = lax.axis_index("tok")
    x = t // (2 * n_y)
    y = (t // 2) % n_y
    core = t % 2
    core_peer = t + 1 - 2 * core
    x_peer = t + (1 - 2 * x) * 2 * n_y

    barrier = pltpu.get_barrier_semaphore()
    for k in range(1, n_feat):
        pl.semaphore_signal(barrier, 1, device_id={"feat": lax.rem(me + k, n_feat)}, device_id_type=MESH)
    for o in range(1, n_y):
        dest = x * 2 * n_y + lax.rem(y + o, n_y) * 2 + core
        pl.semaphore_signal(barrier, 1, device_id={"tok": dest}, device_id_type=MESH)
    pl.semaphore_signal(barrier, 1, device_id={"tok": core_peer}, device_id_type=MESH)
    pl.semaphore_signal(barrier, 1, device_id={"tok": x_peer}, device_id_type=MESH)

    panel = [
        pltpu.make_async_copy(act_hbm.at[:, pl.ds(b * width, width)], act_ref.at[b], panel_sem.at[b])
        for b in range(panel_blocks)
    ]
    for cp in panel:
        cp.start()
    for cp in panel:
        cp.wait()
    for p in range(n_feat):
        send_ref[p] = act_ref[picked_ref[p]]

    pl.semaphore_wait(barrier, n_feat - 1 + n_y - 1 + 2)

    def feat_copies(c):
        cols = pl.ds(c * w, w)
        local = pltpu.make_async_copy(send_ref.at[me, :, cols], recv[c].at[me], flocal.at[c])
        copies = [local]
        for k in sorted(range(1, n_feat), key=lambda k: min(k, n_feat - k)):
            peer = lax.rem(me + k, n_feat)
            copies.append(pltpu.make_async_remote_copy(
                src_ref=send_ref.at[peer, :, cols],
                dst_ref=recv[c].at[me],
                send_sem=fsend.at[c, k],
                recv_sem=frecv.at[c, k],
                device_id={"feat": peer},
                device_id_type=MESH,
            ))
        return copies

    def reduce_last(c):
        h = slots // 2
        cols = pl.ds(c * w, w)
        cp0 = pltpu.make_async_remote_copy(
            src_ref=gbuf.at[1 - core], dst_ref=st0.at[c], send_sem=send0.at[c],
            recv_sem=recv0.at[c], device_id={"tok": core_peer}, device_id_type=MESH,
        )
        cp0.start()
        cp0.wait()
        s1buf[...] = gbuf[core] + st0[c]
        a_y = []
        for o in range(1, n_y):
            dy = lax.rem(y + o, n_y)
            cp = pltpu.make_async_remote_copy(
                src_ref=s1buf.at[dy, :, pl.ds(0, h)], dst_ref=st1.at[c, y, :, pl.ds(0, h)],
                send_sem=send1.at[c, o], recv_sem=recv1.at[c, o],
                device_id={"tok": x * 2 * n_y + dy * 2 + core}, device_id_type=MESH,
            )
            cp.start()
            a_y.append(cp)
        b_x = pltpu.make_async_remote_copy(
            src_ref=s1buf.at[:, 1 - x, pl.ds(h, slots - h)], dst_ref=bxbuf,
            send_sem=bsem.at[0], recv_sem=bsem.at[1], device_id={"tok": x_peer}, device_id_type=MESH,
        )
        b_x.start()
        b_x.wait()
        bsum[...] = s1buf[:, x, h:] + bxbuf[...]
        b_y = []
        for o in range(1, n_y):
            dy = lax.rem(y + o, n_y)
            cp = pltpu.make_async_remote_copy(
                src_ref=bsum.at[dy], dst_ref=bybuf.at[y],
                send_sem=bysend.at[o], recv_sem=byrecv.at[o],
                device_id={"tok": x * 2 * n_y + dy * 2 + core}, device_id_type=MESH,
            )
            cp.start()
            b_y.append(cp)
        for cp in a_y:
            cp.wait()
        acc = s1buf[y, :, :h]
        for o in range(1, n_y):
            acc = acc + st1[c, lax.rem(y + o, n_y), :, :h]
        s2buf[:, :h] = acc
        a_x = pltpu.make_async_remote_copy(
            src_ref=s2buf.at[1 - x, pl.ds(0, h)], dst_ref=st2.at[c, pl.ds(0, h)],
            send_sem=send2.at[c], recv_sem=recv2.at[c], device_id={"tok": x_peer}, device_id_type=MESH,
        )
        a_x.start()
        for cp in b_y:
            cp.wait()
        accb = bsum[y]
        for o in range(1, n_y):
            accb = accb + bybuf[lax.rem(y + o, n_y)]
        out_ref[h:, :, cols] = accb
        a_x.wait()
        out_ref[:h, :, cols] = s2buf[x, :h] + st2[c, :h]

    in_flight = []
    for c in range(min(2, chunks)):
        in_flight.append(feat_copies(c))
        for cp in in_flight[-1]:
            cp.start()
    for c in range(chunks):
        for cp in in_flight[c]:
            cp.wait()
        if c + 2 < chunks:
            in_flight.append(feat_copies(c + 2))
            for cp in in_flight[-1]:
                cp.start()

        def gram_one(k, carry):
            q = recv[c][holder_ref[k]]
            p = act_ref[rowblk_ref[k]]
            g = lax.dot_general(
                p, q, (((0,), (0,)), ((), ())), preferred_element_type=jnp.float32
            ) * scale
            for xx in range(2):
                for yy in range(n_y):
                    for cc in range(2):
                        r0 = ((xx * n_y + yy) * 2 + cc) * piece
                        gbuf[cc, yy, xx, k] = g[r0:r0 + piece, :]
            return carry

        lax.fori_loop(0, slots, gram_one, 0)

        if c == chunks - 1 and slots > 1:
            reduce_last(c)
            continue

        cp0 = pltpu.make_async_remote_copy(
            src_ref=gbuf.at[1 - core],
            dst_ref=st0.at[c],
            send_sem=send0.at[c],
            recv_sem=recv0.at[c],
            device_id={"tok": core_peer},
            device_id_type=MESH,
        )
        cp0.start()
        cp0.wait()
        s1buf[...] = gbuf[core] + st0[c]

        copies1 = []
        for o in range(1, n_y):
            dy = lax.rem(y + o, n_y)
            cp = pltpu.make_async_remote_copy(
                src_ref=s1buf.at[dy],
                dst_ref=st1.at[c, y],
                send_sem=send1.at[c, o],
                recv_sem=recv1.at[c, o],
                device_id={"tok": x * 2 * n_y + dy * 2 + core},
                device_id_type=MESH,
            )
            cp.start()
            copies1.append(cp)
        for cp in copies1:
            cp.wait()
        acc = s1buf[y]
        for o in range(1, n_y):
            acc = acc + st1[c, lax.rem(y + o, n_y)]
        s2buf[...] = acc

        cp2 = pltpu.make_async_remote_copy(
            src_ref=s2buf.at[1 - x],
            dst_ref=st2.at[c],
            send_sem=send2.at[c],
            recv_sem=recv2.at[c],
            device_id={"tok": x_peer},
            device_id_type=MESH,
        )
        cp2.start()
        cp2.wait()
        out_ref[:, :, pl.ds(c * w, w)] = s2buf[x] + st2[c]


def fused(holder, rowblk, picked, activations, n_feat, n_tok, scale):
    slots = holder.shape[0]
    tokens, width = activations.shape[0], BLK
    panel_blocks = activations.shape[1] // BLK
    w = width // CHUNKS
    n_y = n_tok // 4
    piece = width // n_tok
    kernel = functools.partial(fused_kernel, n_feat, n_tok, CHUNKS, scale)
    blk = (slots, piece, w)
    return pl.pallas_call(
        kernel,
        out_shape=jax.ShapeDtypeStruct((slots, piece, width), jnp.float32),
        in_specs=[
            pl.BlockSpec(memory_space=pltpu.SMEM),
            pl.BlockSpec(memory_space=pltpu.SMEM),
            pl.BlockSpec(memory_space=pltpu.SMEM),
            pl.BlockSpec(memory_space=pl.ANY),
        ],
        out_specs=pl.BlockSpec(memory_space=pltpu.VMEM),
        scratch_shapes=[pltpu.VMEM((n_feat, tokens, w), activations.dtype) for _ in range(CHUNKS)] + [
            pltpu.VMEM((panel_blocks, tokens, width), activations.dtype),
            pltpu.VMEM((n_feat, tokens, width), activations.dtype),
            pltpu.VMEM((2, n_y, 2) + blk, jnp.float32),
            pltpu.VMEM((CHUNKS, n_y, 2) + blk, jnp.float32),
            pltpu.VMEM((n_y, 2) + blk, jnp.float32),
            pltpu.VMEM((CHUNKS, n_y, 2) + blk, jnp.float32),
            pltpu.VMEM((2,) + blk, jnp.float32),
            pltpu.VMEM((CHUNKS,) + blk, jnp.float32),
            pltpu.SemaphoreType.DMA((panel_blocks,)),
            pltpu.SemaphoreType.DMA((CHUNKS, n_feat)),
            pltpu.SemaphoreType.DMA((CHUNKS, n_feat)),
            pltpu.SemaphoreType.DMA((CHUNKS,)),
            pltpu.SemaphoreType.DMA((CHUNKS,)),
            pltpu.SemaphoreType.DMA((CHUNKS,)),
            pltpu.SemaphoreType.DMA((CHUNKS, n_y)),
            pltpu.SemaphoreType.DMA((CHUNKS, n_y)),
            pltpu.SemaphoreType.DMA((CHUNKS,)),
            pltpu.SemaphoreType.DMA((CHUNKS,)),
            pltpu.VMEM((n_y, slots - slots // 2, piece, w), jnp.float32),
            pltpu.VMEM((n_y, slots - slots // 2, piece, w), jnp.float32),
            pltpu.VMEM((n_y, slots - slots // 2, piece, w), jnp.float32),
            pltpu.SemaphoreType.DMA((2,)),
            pltpu.SemaphoreType.DMA((n_y,)),
            pltpu.SemaphoreType.DMA((n_y,)),
        ],
        compiler_params=pltpu.CompilerParams(
            collective_id=0, has_side_effects=True, vmem_limit_bytes=60 * 1024 * 1024
        ),
    )(holder, rowblk, picked, activations)


def body(activations, pattern, block_slot):
    tok_rows, width = activations.shape
    feat_count = lax.axis_size("feat")
    tok_count = lax.axis_size("tok")
    my_index = lax.axis_index("feat")
    panel_blocks = width // BLK
    list_length = pattern.shape[0]
    per_device = list_length // feat_count
    scale = 1.0 / (tok_rows * tok_count)
    ordered = jnp.zeros_like(pattern).at[block_slot].set(pattern)
    pairs = ordered.reshape(feat_count, per_device, 2)
    holder = pairs[:, :, 1] // panel_blocks
    local_column = pairs[:, :, 1] % panel_blocks
    picked = jnp.sum(jnp.where(holder == my_index, local_column, 0), axis=1)
    my_pairs = lax.dynamic_index_in_dim(pairs, my_index, 0, keepdims=False)
    my_holder = my_pairs[:, 1] // panel_blocks
    rowblk = my_pairs[:, 0] % panel_blocks
    out = fused(my_holder, rowblk, picked, activations, feat_count, tok_count, scale)
    return out.transpose(1, 0, 2)


def solution(mesh):
    placed = (P("tok", "feat"), P(), P())
    return jax.shard_map(
        body, mesh=mesh, in_specs=placed, out_specs=P("tok", "feat", None), check_vma=False
    )
```

```python
import functools

import jax
import jax.numpy as jnp
from jax import lax
from jax.experimental import pallas as pl
from jax.experimental.pallas import tpu as pltpu
from jax.sharding import PartitionSpec as P

BLK = 512
CHUNKS = 4
MESH = pl.DeviceIdType.MESH


def fused_kernel(n_feat, n_tok, chunks, scale,
                 holder_ref, rowblk_ref, picked_ref, act_hbm, out_ref, *scratch):
    recv = scratch[:chunks]
    (act_ref, send_ref, gbuf, st0, s1buf, st1, s2buf, st2, panel_sem,
     fsend, frecv, flocal, send0, recv0, send1, recv1, send2, recv2,
     bxbuf, bsum, bybuf, bsem, bysend, byrecv) = scratch[chunks:]
    slots = holder_ref.shape[0]
    tokens, width = send_ref.shape[1], send_ref.shape[2]
    panel_blocks = act_ref.shape[0]
    w = width // chunks
    n_y = n_tok // 4
    piece = width // n_tok
    me = lax.axis_index("feat")
    t = lax.axis_index("tok")
    x = t // (2 * n_y)
    y = (t // 2) % n_y
    core = t % 2
    core_peer = t + 1 - 2 * core
    x_peer = t + (1 - 2 * x) * 2 * n_y

    barrier = pltpu.get_barrier_semaphore()
    for k in range(1, n_feat):
        pl.semaphore_signal(barrier, 1, device_id={"feat": lax.rem(me + k, n_feat)}, device_id_type=MESH)
    for o in range(1, n_y):
        dest = x * 2 * n_y + lax.rem(y + o, n_y) * 2 + core
        pl.semaphore_signal(barrier, 1, device_id={"tok": dest}, device_id_type=MESH)
    pl.semaphore_signal(barrier, 1, device_id={"tok": core_peer}, device_id_type=MESH)
    pl.semaphore_signal(barrier, 1, device_id={"tok": x_peer}, device_id_type=MESH)

    panel = [
        pltpu.make_async_copy(act_hbm.at[:, pl.ds(b * width, width)], act_ref.at[b], panel_sem.at[b])
        for b in range(panel_blocks)
    ]
    for cp in panel:
        cp.start()
    for cp in panel:
        cp.wait()
    for p in range(n_feat):
        send_ref[p] = act_ref[picked_ref[p]]

    pl.semaphore_wait(barrier, n_feat - 1 + n_y - 1 + 2)

    def feat_copies(c):
        cols = pl.ds(c * w, w)
        local = pltpu.make_async_copy(send_ref.at[me, :, cols], recv[c].at[me], flocal.at[c])
        copies = [local]
        for k in sorted(range(1, n_feat), key=lambda k: min(k, n_feat - k)):
            peer = lax.rem(me + k, n_feat)
            copies.append(pltpu.make_async_remote_copy(
                src_ref=send_ref.at[peer, :, cols],
                dst_ref=recv[c].at[me],
                send_sem=fsend.at[c, k],
                recv_sem=frecv.at[c, k],
                device_id={"feat": peer},
                device_id_type=MESH,
            ))
        return copies

    def reduce_last(c):
        h = (slots * 5) // 12
        cols = pl.ds(c * w, w)
        cp0 = pltpu.make_async_remote_copy(
            src_ref=gbuf.at[1 - core], dst_ref=st0.at[c], send_sem=send0.at[c],
            recv_sem=recv0.at[c], device_id={"tok": core_peer}, device_id_type=MESH,
        )
        cp0.start()
        cp0.wait()
        s1buf[...] = gbuf[core] + st0[c]
        a_y = []
        for o in range(1, n_y):
            dy = lax.rem(y + o, n_y)
            cp = pltpu.make_async_remote_copy(
                src_ref=s1buf.at[dy, :, pl.ds(0, h)], dst_ref=st1.at[c, y, :, pl.ds(0, h)],
                send_sem=send1.at[c, o], recv_sem=recv1.at[c, o],
                device_id={"tok": x * 2 * n_y + dy * 2 + core}, device_id_type=MESH,
            )
            cp.start()
            a_y.append(cp)
        b_x = pltpu.make_async_remote_copy(
            src_ref=s1buf.at[:, 1 - x, pl.ds(h, slots - h)], dst_ref=bxbuf,
            send_sem=bsem.at[0], recv_sem=bsem.at[1], device_id={"tok": x_peer}, device_id_type=MESH,
        )
        b_x.start()
        b_x.wait()
        bsum[...] = s1buf[:, x, h:] + bxbuf[...]
        b_y = []
        for o in range(1, n_y):
            dy = lax.rem(y + o, n_y)
            cp = pltpu.make_async_remote_copy(
                src_ref=bsum.at[dy], dst_ref=bybuf.at[y],
                send_sem=bysend.at[o], recv_sem=byrecv.at[o],
                device_id={"tok": x * 2 * n_y + dy * 2 + core}, device_id_type=MESH,
            )
            cp.start()
            b_y.append(cp)
        for cp in a_y:
            cp.wait()
        acc = s1buf[y, :, :h]
        for o in range(1, n_y):
            acc = acc + st1[c, lax.rem(y + o, n_y), :, :h]
        s2buf[:, :h] = acc
        a_x = pltpu.make_async_remote_copy(
            src_ref=s2buf.at[1 - x, pl.ds(0, h)], dst_ref=st2.at[c, pl.ds(0, h)],
            send_sem=send2.at[c], recv_sem=recv2.at[c], device_id={"tok": x_peer}, device_id_type=MESH,
        )
        a_x.start()
        for cp in b_y:
            cp.wait()
        accb = bsum[y]
        for o in range(1, n_y):
            accb = accb + bybuf[lax.rem(y + o, n_y)]
        out_ref[h:, :, cols] = accb
        a_x.wait()
        out_ref[:h, :, cols] = s2buf[x, :h] + st2[c, :h]

    in_flight = []
    for c in range(min(2, chunks)):
        in_flight.append(feat_copies(c))
        for cp in in_flight[-1]:
            cp.start()
    for c in range(chunks):
        for cp in in_flight[c]:
            cp.wait()
        if c + 2 < chunks:
            in_flight.append(feat_copies(c + 2))
            for cp in in_flight[-1]:
                cp.start()

        def gram_one(k, carry):
            q = recv[c][holder_ref[k]]
            p = act_ref[rowblk_ref[k]]
            g = lax.dot_general(
                p, q, (((0,), (0,)), ((), ())), preferred_element_type=jnp.float32
            ) * scale
            for xx in range(2):
                for yy in range(n_y):
                    for cc in range(2):
                        r0 = ((xx * n_y + yy) * 2 + cc) * piece
                        gbuf[cc, yy, xx, k] = g[r0:r0 + piece, :]
            return carry

        lax.fori_loop(0, slots, gram_one, 0)

        if c == chunks - 1 and slots > 1:
            reduce_last(c)
            continue

        cp0 = pltpu.make_async_remote_copy(
            src_ref=gbuf.at[1 - core],
            dst_ref=st0.at[c],
            send_sem=send0.at[c],
            recv_sem=recv0.at[c],
            device_id={"tok": core_peer},
            device_id_type=MESH,
        )
        cp0.start()
        cp0.wait()
        s1buf[...] = gbuf[core] + st0[c]

        copies1 = []
        for o in range(1, n_y):
            dy = lax.rem(y + o, n_y)
            cp = pltpu.make_async_remote_copy(
                src_ref=s1buf.at[dy],
                dst_ref=st1.at[c, y],
                send_sem=send1.at[c, o],
                recv_sem=recv1.at[c, o],
                device_id={"tok": x * 2 * n_y + dy * 2 + core},
                device_id_type=MESH,
            )
            cp.start()
            copies1.append(cp)
        for cp in copies1:
            cp.wait()
        acc = s1buf[y]
        for o in range(1, n_y):
            acc = acc + st1[c, lax.rem(y + o, n_y)]
        s2buf[...] = acc

        cp2 = pltpu.make_async_remote_copy(
            src_ref=s2buf.at[1 - x],
            dst_ref=st2.at[c],
            send_sem=send2.at[c],
            recv_sem=recv2.at[c],
            device_id={"tok": x_peer},
            device_id_type=MESH,
        )
        cp2.start()
        cp2.wait()
        out_ref[:, :, pl.ds(c * w, w)] = s2buf[x] + st2[c]


def fused(holder, rowblk, picked, activations, n_feat, n_tok, scale):
    slots = holder.shape[0]
    tokens, width = activations.shape[0], BLK
    panel_blocks = activations.shape[1] // BLK
    w = width // CHUNKS
    n_y = n_tok // 4
    piece = width // n_tok
    kernel = functools.partial(fused_kernel, n_feat, n_tok, CHUNKS, scale)
    blk = (slots, piece, w)
    return pl.pallas_call(
        kernel,
        out_shape=jax.ShapeDtypeStruct((slots, piece, width), jnp.float32),
        in_specs=[
            pl.BlockSpec(memory_space=pltpu.SMEM),
            pl.BlockSpec(memory_space=pltpu.SMEM),
            pl.BlockSpec(memory_space=pltpu.SMEM),
            pl.BlockSpec(memory_space=pl.ANY),
        ],
        out_specs=pl.BlockSpec(memory_space=pltpu.VMEM),
        scratch_shapes=[pltpu.VMEM((n_feat, tokens, w), activations.dtype) for _ in range(CHUNKS)] + [
            pltpu.VMEM((panel_blocks, tokens, width), activations.dtype),
            pltpu.VMEM((n_feat, tokens, width), activations.dtype),
            pltpu.VMEM((2, n_y, 2) + blk, jnp.float32),
            pltpu.VMEM((CHUNKS, n_y, 2) + blk, jnp.float32),
            pltpu.VMEM((n_y, 2) + blk, jnp.float32),
            pltpu.VMEM((CHUNKS, n_y, 2) + blk, jnp.float32),
            pltpu.VMEM((2,) + blk, jnp.float32),
            pltpu.VMEM((CHUNKS,) + blk, jnp.float32),
            pltpu.SemaphoreType.DMA((panel_blocks,)),
            pltpu.SemaphoreType.DMA((CHUNKS, n_feat)),
            pltpu.SemaphoreType.DMA((CHUNKS, n_feat)),
            pltpu.SemaphoreType.DMA((CHUNKS,)),
            pltpu.SemaphoreType.DMA((CHUNKS,)),
            pltpu.SemaphoreType.DMA((CHUNKS,)),
            pltpu.SemaphoreType.DMA((CHUNKS, n_y)),
            pltpu.SemaphoreType.DMA((CHUNKS, n_y)),
            pltpu.SemaphoreType.DMA((CHUNKS,)),
            pltpu.SemaphoreType.DMA((CHUNKS,)),
            pltpu.VMEM((n_y, slots - (slots * 5) // 12, piece, w), jnp.float32),
            pltpu.VMEM((n_y, slots - (slots * 5) // 12, piece, w), jnp.float32),
            pltpu.VMEM((n_y, slots - (slots * 5) // 12, piece, w), jnp.float32),
            pltpu.SemaphoreType.DMA((2,)),
            pltpu.SemaphoreType.DMA((n_y,)),
            pltpu.SemaphoreType.DMA((n_y,)),
        ],
        compiler_params=pltpu.CompilerParams(
            collective_id=0, has_side_effects=True, vmem_limit_bytes=60 * 1024 * 1024
        ),
    )(holder, rowblk, picked, activations)


def body(activations, pattern, block_slot):
    tok_rows, width = activations.shape
    feat_count = lax.axis_size("feat")
    tok_count = lax.axis_size("tok")
    my_index = lax.axis_index("feat")
    panel_blocks = width // BLK
    list_length = pattern.shape[0]
    per_device = list_length // feat_count
    scale = 1.0 / (tok_rows * tok_count)
    ordered = jnp.zeros_like(pattern).at[block_slot].set(pattern)
    pairs = ordered.reshape(feat_count, per_device, 2)
    holder = pairs[:, :, 1] // panel_blocks
    local_column = pairs[:, :, 1] % panel_blocks
    picked = jnp.sum(jnp.where(holder == my_index, local_column, 0), axis=1)
    my_pairs = lax.dynamic_index_in_dim(pairs, my_index, 0, keepdims=False)
    my_holder = my_pairs[:, 1] // panel_blocks
    rowblk = my_pairs[:, 0] % panel_blocks
    out = fused(my_holder, rowblk, picked, activations, feat_count, tok_count, scale)
    return out.transpose(1, 0, 2)


def solution(mesh):
    placed = (P("tok", "feat"), P(), P())
    return jax.shard_map(
        body, mesh=mesh, in_specs=placed, out_specs=P("tok", "feat", None), check_vma=False
    )
```

```python
import functools

import jax
import jax.numpy as jnp
from jax import lax
from jax.experimental import pallas as pl
from jax.experimental.pallas import tpu as pltpu
from jax.sharding import PartitionSpec as P

BLK = 512
CHUNKS = 4
MESH = pl.DeviceIdType.MESH


def fused_kernel(n_feat, n_tok, chunks, scale,
                 holder_ref, rowblk_ref, picked_ref, act_hbm, out_ref, *scratch):
    recv = scratch[:chunks]
    (act_ref, send_ref, gbuf, st0, s1buf, st1, s2buf, st2, panel_sem,
     fsend, frecv, flocal, send0, recv0, send1, recv1, send2, recv2,
     bxbuf, bsum, bybuf, bsem, bysend, byrecv) = scratch[chunks:]
    slots = holder_ref.shape[0]
    tokens, width = send_ref.shape[1], send_ref.shape[2]
    panel_blocks = act_ref.shape[0]
    w = width // chunks
    n_y = n_tok // 4
    piece = width // n_tok
    me = lax.axis_index("feat")
    t = lax.axis_index("tok")
    x = t // (2 * n_y)
    y = (t // 2) % n_y
    core = t % 2
    core_peer = t + 1 - 2 * core
    x_peer = t + (1 - 2 * x) * 2 * n_y

    barrier = pltpu.get_barrier_semaphore()
    for k in range(1, n_feat):
        pl.semaphore_signal(barrier, 1, device_id={"feat": lax.rem(me + k, n_feat)}, device_id_type=MESH)
    for o in range(1, n_y):
        dest = x * 2 * n_y + lax.rem(y + o, n_y) * 2 + core
        pl.semaphore_signal(barrier, 1, device_id={"tok": dest}, device_id_type=MESH)
    pl.semaphore_signal(barrier, 1, device_id={"tok": core_peer}, device_id_type=MESH)
    pl.semaphore_signal(barrier, 1, device_id={"tok": x_peer}, device_id_type=MESH)

    panel = [
        pltpu.make_async_copy(act_hbm.at[:, pl.ds(b * width, width)], act_ref.at[b], panel_sem.at[b])
        for b in range(panel_blocks)
    ]
    for cp in panel:
        cp.start()
    for cp in panel:
        cp.wait()
    for p in range(n_feat):
        send_ref[p] = act_ref[picked_ref[p]]

    pl.semaphore_wait(barrier, n_feat - 1 + n_y - 1 + 2)

    def feat_copies(c):
        cols = pl.ds(c * w, w)
        local = pltpu.make_async_copy(send_ref.at[me, :, cols], recv[c].at[me], flocal.at[c])
        copies = [local]
        for k in sorted(range(1, n_feat), key=lambda k: min(k, n_feat - k)):
            peer = lax.rem(me + k, n_feat)
            copies.append(pltpu.make_async_remote_copy(
                src_ref=send_ref.at[peer, :, cols],
                dst_ref=recv[c].at[me],
                send_sem=fsend.at[c, k],
                recv_sem=frecv.at[c, k],
                device_id={"feat": peer},
                device_id_type=MESH,
            ))
        return copies

    def reduce_last(c):
        h = (slots * 7) // 12
        cols = pl.ds(c * w, w)
        cp0 = pltpu.make_async_remote_copy(
            src_ref=gbuf.at[1 - core], dst_ref=st0.at[c], send_sem=send0.at[c],
            recv_sem=recv0.at[c], device_id={"tok": core_peer}, device_id_type=MESH,
        )
        cp0.start()
        cp0.wait()
        s1buf[...] = gbuf[core] + st0[c]
        a_y = []
        for o in range(1, n_y):
            dy = lax.rem(y + o, n_y)
            cp = pltpu.make_async_remote_copy(
                src_ref=s1buf.at[dy, :, pl.ds(0, h)], dst_ref=st1.at[c, y, :, pl.ds(0, h)],
                send_sem=send1.at[c, o], recv_sem=recv1.at[c, o],
                device_id={"tok": x * 2 * n_y + dy * 2 + core}, device_id_type=MESH,
            )
            cp.start()
            a_y.append(cp)
        b_x = pltpu.make_async_remote_copy(
            src_ref=s1buf.at[:, 1 - x, pl.ds(h, slots - h)], dst_ref=bxbuf,
            send_sem=bsem.at[0], recv_sem=bsem.at[1], device_id={"tok": x_peer}, device_id_type=MESH,
        )
        b_x.start()
        b_x.wait()
        bsum[...] = s1buf[:, x, h:] + bxbuf[...]
        b_y = []
        for o in range(1, n_y):
            dy = lax.rem(y + o, n_y)
            cp = pltpu.make_async_remote_copy(
                src_ref=bsum.at[dy], dst_ref=bybuf.at[y],
                send_sem=bysend.at[o], recv_sem=byrecv.at[o],
                device_id={"tok": x * 2 * n_y + dy * 2 + core}, device_id_type=MESH,
            )
            cp.start()
            b_y.append(cp)
        for cp in a_y:
            cp.wait()
        acc = s1buf[y, :, :h]
        for o in range(1, n_y):
            acc = acc + st1[c, lax.rem(y + o, n_y), :, :h]
        s2buf[:, :h] = acc
        a_x = pltpu.make_async_remote_copy(
            src_ref=s2buf.at[1 - x, pl.ds(0, h)], dst_ref=st2.at[c, pl.ds(0, h)],
            send_sem=send2.at[c], recv_sem=recv2.at[c], device_id={"tok": x_peer}, device_id_type=MESH,
        )
        a_x.start()
        for cp in b_y:
            cp.wait()
        accb = bsum[y]
        for o in range(1, n_y):
            accb = accb + bybuf[lax.rem(y + o, n_y)]
        out_ref[h:, :, cols] = accb
        a_x.wait()
        out_ref[:h, :, cols] = s2buf[x, :h] + st2[c, :h]

    in_flight = []
    for c in range(min(2, chunks)):
        in_flight.append(feat_copies(c))
        for cp in in_flight[-1]:
            cp.start()
    for c in range(chunks):
        for cp in in_flight[c]:
            cp.wait()
        if c + 2 < chunks:
            in_flight.append(feat_copies(c + 2))
            for cp in in_flight[-1]:
                cp.start()

        def gram_one(k, carry):
            q = recv[c][holder_ref[k]]
            p = act_ref[rowblk_ref[k]]
            g = lax.dot_general(
                p, q, (((0,), (0,)), ((), ())), preferred_element_type=jnp.float32
            ) * scale
            for xx in range(2):
                for yy in range(n_y):
                    for cc in range(2):
                        r0 = ((xx * n_y + yy) * 2 + cc) * piece
                        gbuf[cc, yy, xx, k] = g[r0:r0 + piece, :]
            return carry

        lax.fori_loop(0, slots, gram_one, 0)

        if c == chunks - 1 and slots > 1:
            reduce_last(c)
            continue

        cp0 = pltpu.make_async_remote_copy(
            src_ref=gbuf.at[1 - core],
            dst_ref=st0.at[c],
            send_sem=send0.at[c],
            recv_sem=recv0.at[c],
            device_id={"tok": core_peer},
            device_id_type=MESH,
        )
        cp0.start()
        cp0.wait()
        s1buf[...] = gbuf[core] + st0[c]

        copies1 = []
        for o in range(1, n_y):
            dy = lax.rem(y + o, n_y)
            cp = pltpu.make_async_remote_copy(
                src_ref=s1buf.at[dy],
                dst_ref=st1.at[c, y],
                send_sem=send1.at[c, o],
                recv_sem=recv1.at[c, o],
                device_id={"tok": x * 2 * n_y + dy * 2 + core},
                device_id_type=MESH,
            )
            cp.start()
            copies1.append(cp)
        for cp in copies1:
            cp.wait()
        acc = s1buf[y]
        for o in range(1, n_y):
            acc = acc + st1[c, lax.rem(y + o, n_y)]
        s2buf[...] = acc

        cp2 = pltpu.make_async_remote_copy(
            src_ref=s2buf.at[1 - x],
            dst_ref=st2.at[c],
            send_sem=send2.at[c],
            recv_sem=recv2.at[c],
            device_id={"tok": x_peer},
            device_id_type=MESH,
        )
        cp2.start()
        cp2.wait()
        out_ref[:, :, pl.ds(c * w, w)] = s2buf[x] + st2[c]


def fused(holder, rowblk, picked, activations, n_feat, n_tok, scale):
    slots = holder.shape[0]
    tokens, width = activations.shape[0], BLK
    panel_blocks = activations.shape[1] // BLK
    w = width // CHUNKS
    n_y = n_tok // 4
    piece = width // n_tok
    kernel = functools.partial(fused_kernel, n_feat, n_tok, CHUNKS, scale)
    blk = (slots, piece, w)
    return pl.pallas_call(
        kernel,
        out_shape=jax.ShapeDtypeStruct((slots, piece, width), jnp.float32),
        in_specs=[
            pl.BlockSpec(memory_space=pltpu.SMEM),
            pl.BlockSpec(memory_space=pltpu.SMEM),
            pl.BlockSpec(memory_space=pltpu.SMEM),
            pl.BlockSpec(memory_space=pl.ANY),
        ],
        out_specs=pl.BlockSpec(memory_space=pltpu.VMEM),
        scratch_shapes=[pltpu.VMEM((n_feat, tokens, w), activations.dtype) for _ in range(CHUNKS)] + [
            pltpu.VMEM((panel_blocks, tokens, width), activations.dtype),
            pltpu.VMEM((n_feat, tokens, width), activations.dtype),
            pltpu.VMEM((2, n_y, 2) + blk, jnp.float32),
            pltpu.VMEM((CHUNKS, n_y, 2) + blk, jnp.float32),
            pltpu.VMEM((n_y, 2) + blk, jnp.float32),
            pltpu.VMEM((CHUNKS, n_y, 2) + blk, jnp.float32),
            pltpu.VMEM((2,) + blk, jnp.float32),
            pltpu.VMEM((CHUNKS,) + blk, jnp.float32),
            pltpu.SemaphoreType.DMA((panel_blocks,)),
            pltpu.SemaphoreType.DMA((CHUNKS, n_feat)),
            pltpu.SemaphoreType.DMA((CHUNKS, n_feat)),
            pltpu.SemaphoreType.DMA((CHUNKS,)),
            pltpu.SemaphoreType.DMA((CHUNKS,)),
            pltpu.SemaphoreType.DMA((CHUNKS,)),
            pltpu.SemaphoreType.DMA((CHUNKS, n_y)),
            pltpu.SemaphoreType.DMA((CHUNKS, n_y)),
            pltpu.SemaphoreType.DMA((CHUNKS,)),
            pltpu.SemaphoreType.DMA((CHUNKS,)),
            pltpu.VMEM((n_y, slots - (slots * 7) // 12, piece, w), jnp.float32),
            pltpu.VMEM((n_y, slots - (slots * 7) // 12, piece, w), jnp.float32),
            pltpu.VMEM((n_y, slots - (slots * 7) // 12, piece, w), jnp.float32),
            pltpu.SemaphoreType.DMA((2,)),
            pltpu.SemaphoreType.DMA((n_y,)),
            pltpu.SemaphoreType.DMA((n_y,)),
        ],
        compiler_params=pltpu.CompilerParams(
            collective_id=0, has_side_effects=True, vmem_limit_bytes=60 * 1024 * 1024
        ),
    )(holder, rowblk, picked, activations)


def body(activations, pattern, block_slot):
    tok_rows, width = activations.shape
    feat_count = lax.axis_size("feat")
    tok_count = lax.axis_size("tok")
    my_index = lax.axis_index("feat")
    panel_blocks = width // BLK
    list_length = pattern.shape[0]
    per_device = list_length // feat_count
    scale = 1.0 / (tok_rows * tok_count)
    ordered = jnp.zeros_like(pattern).at[block_slot].set(pattern)
    pairs = ordered.reshape(feat_count, per_device, 2)
    holder = pairs[:, :, 1] // panel_blocks
    local_column = pairs[:, :, 1] % panel_blocks
    picked = jnp.sum(jnp.where(holder == my_index, local_column, 0), axis=1)
    my_pairs = lax.dynamic_index_in_dim(pairs, my_index, 0, keepdims=False)
    my_holder = my_pairs[:, 1] // panel_blocks
    rowblk = my_pairs[:, 0] % panel_blocks
    out = fused(my_holder, rowblk, picked, activations, feat_count, tok_count, scale)
    return out.transpose(1, 0, 2)


def solution(mesh):
    placed = (P("tok", "feat"), P(), P())
    return jax.shard_map(
        body, mesh=mesh, in_specs=placed, out_specs=P("tok", "feat", None), check_vma=False
    )
```

```python
import functools

import jax
import jax.numpy as jnp
from jax import lax
from jax.experimental import pallas as pl
from jax.experimental.pallas import tpu as pltpu
from jax.sharding import PartitionSpec as P

BLK = 512
CHUNKS = 4
MESH = pl.DeviceIdType.MESH


def fused_kernel(n_feat, n_tok, chunks, scale,
                 holder_ref, rowblk_ref, picked_ref, act_hbm, out_ref, *scratch):
    recv = scratch[:chunks]
    (act_ref, send_ref, gbuf, st0, s1buf, st1, s2buf, st2, panel_sem,
     fsend, frecv, flocal, send0, recv0, send1, recv1, send2, recv2,
     bxbuf, bsum, bybuf, bsem, bysend, byrecv) = scratch[chunks:]
    slots = holder_ref.shape[0]
    tokens, width = send_ref.shape[1], send_ref.shape[2]
    panel_blocks = act_ref.shape[0]
    w = width // chunks
    n_y = n_tok // 4
    piece = width // n_tok
    me = lax.axis_index("feat")
    t = lax.axis_index("tok")
    x = t // (2 * n_y)
    y = (t // 2) % n_y
    core = t % 2
    core_peer = t + 1 - 2 * core
    x_peer = t + (1 - 2 * x) * 2 * n_y

    barrier = pltpu.get_barrier_semaphore()
    for k in range(1, n_feat):
        pl.semaphore_signal(barrier, 1, device_id={"feat": lax.rem(me + k, n_feat)}, device_id_type=MESH)
    for o in range(1, n_y):
        dest = x * 2 * n_y + lax.rem(y + o, n_y) * 2 + core
        pl.semaphore_signal(barrier, 1, device_id={"tok": dest}, device_id_type=MESH)
    pl.semaphore_signal(barrier, 1, device_id={"tok": core_peer}, device_id_type=MESH)
    pl.semaphore_signal(barrier, 1, device_id={"tok": x_peer}, device_id_type=MESH)

    panel = [
        pltpu.make_async_copy(act_hbm.at[:, pl.ds(b * width, width)], act_ref.at[b], panel_sem.at[b])
        for b in range(panel_blocks)
    ]
    for cp in panel:
        cp.start()
    for cp in panel:
        cp.wait()
    for p in range(n_feat):
        send_ref[p] = act_ref[picked_ref[p]]

    pl.semaphore_wait(barrier, n_feat - 1 + n_y - 1 + 2)

    def feat_copies(c):
        cols = pl.ds(c * w, w)
        local = pltpu.make_async_copy(send_ref.at[me, :, cols], recv[c].at[me], flocal.at[c])
        copies = [local]
        for k in sorted(range(1, n_feat), key=lambda k: min(k, n_feat - k)):
            peer = lax.rem(me + k, n_feat)
            copies.append(pltpu.make_async_remote_copy(
                src_ref=send_ref.at[peer, :, cols],
                dst_ref=recv[c].at[me],
                send_sem=fsend.at[c, k],
                recv_sem=frecv.at[c, k],
                device_id={"feat": peer},
                device_id_type=MESH,
            ))
        return copies

    def reduce_last(c):
        h = (slots * 7) // 12
        cols = pl.ds(c * w, w)
        cp0 = pltpu.make_async_remote_copy(
            src_ref=gbuf.at[1 - core], dst_ref=st0.at[c], send_sem=send0.at[c],
            recv_sem=recv0.at[c], device_id={"tok": core_peer}, device_id_type=MESH,
        )
        cp0.start()
        cp0.wait()
        s1buf[...] = gbuf[core] + st0[c]
        a_y = []
        for o in range(1, n_y):
            dy = lax.rem(y + o, n_y)
            cp = pltpu.make_async_remote_copy(
                src_ref=s1buf.at[dy, :, pl.ds(0, h)], dst_ref=st1.at[c, y, :, pl.ds(0, h)],
                send_sem=send1.at[c, o], recv_sem=recv1.at[c, o],
                device_id={"tok": x * 2 * n_y + dy * 2 + core}, device_id_type=MESH,
            )
            cp.start()
            a_y.append(cp)
        b_x = pltpu.make_async_remote_copy(
            src_ref=s1buf.at[:, 1 - x, pl.ds(h, slots - h)], dst_ref=bxbuf,
            send_sem=bsem.at[0], recv_sem=bsem.at[1], device_id={"tok": x_peer}, device_id_type=MESH,
        )
        b_x.start()
        b_x.wait()
        bsum[...] = s1buf[:, x, h:] + bxbuf[...]
        b_y = []
        for o in range(1, n_y):
            dy = lax.rem(y + o, n_y)
            cp = pltpu.make_async_remote_copy(
                src_ref=bsum.at[dy], dst_ref=bybuf.at[y],
                send_sem=bysend.at[o], recv_sem=byrecv.at[o],
                device_id={"tok": x * 2 * n_y + dy * 2 + core}, device_id_type=MESH,
            )
            cp.start()
            b_y.append(cp)
        for cp in a_y:
            cp.wait()
        acc = s1buf[y, :, :h]
        for o in range(1, n_y):
            acc = acc + st1[c, lax.rem(y + o, n_y), :, :h]
        s2buf[:, :h] = acc
        a_x = pltpu.make_async_remote_copy(
            src_ref=s2buf.at[1 - x, pl.ds(0, h)], dst_ref=st2.at[c, pl.ds(0, h)],
            send_sem=send2.at[c], recv_sem=recv2.at[c], device_id={"tok": x_peer}, device_id_type=MESH,
        )
        a_x.start()
        for cp in b_y:
            cp.wait()
        accb = bsum[y]
        for o in range(1, n_y):
            accb = accb + bybuf[lax.rem(y + o, n_y)]
        out_ref[h:, :, cols] = accb
        a_x.wait()
        out_ref[:h, :, cols] = s2buf[x, :h] + st2[c, :h]

    in_flight = []
    for c in range(min(3, chunks)):
        in_flight.append(feat_copies(c))
        for cp in in_flight[-1]:
            cp.start()
    for c in range(chunks):
        for cp in in_flight[c]:
            cp.wait()
        if c + 3 < chunks:
            in_flight.append(feat_copies(c + 3))
            for cp in in_flight[-1]:
                cp.start()

        def gram_one(k, carry):
            q = recv[c][holder_ref[k]]
            p = act_ref[rowblk_ref[k]]
            g = lax.dot_general(
                p, q, (((0,), (0,)), ((), ())), preferred_element_type=jnp.float32
            ) * scale
            for xx in range(2):
                for yy in range(n_y):
                    for cc in range(2):
                        r0 = ((xx * n_y + yy) * 2 + cc) * piece
                        gbuf[cc, yy, xx, k] = g[r0:r0 + piece, :]
            return carry

        lax.fori_loop(0, slots, gram_one, 0)

        if c == chunks - 1 and slots > 1:
            reduce_last(c)
            continue

        cp0 = pltpu.make_async_remote_copy(
            src_ref=gbuf.at[1 - core],
            dst_ref=st0.at[c],
            send_sem=send0.at[c],
            recv_sem=recv0.at[c],
            device_id={"tok": core_peer},
            device_id_type=MESH,
        )
        cp0.start()
        cp0.wait()
        s1buf[...] = gbuf[core] + st0[c]

        copies1 = []
        for o in range(1, n_y):
            dy = lax.rem(y + o, n_y)
            cp = pltpu.make_async_remote_copy(
                src_ref=s1buf.at[dy],
                dst_ref=st1.at[c, y],
                send_sem=send1.at[c, o],
                recv_sem=recv1.at[c, o],
                device_id={"tok": x * 2 * n_y + dy * 2 + core},
                device_id_type=MESH,
            )
            cp.start()
            copies1.append(cp)
        for cp in copies1:
            cp.wait()
        acc = s1buf[y]
        for o in range(1, n_y):
            acc = acc + st1[c, lax.rem(y + o, n_y)]
        s2buf[...] = acc

        cp2 = pltpu.make_async_remote_copy(
            src_ref=s2buf.at[1 - x],
            dst_ref=st2.at[c],
            send_sem=send2.at[c],
            recv_sem=recv2.at[c],
            device_id={"tok": x_peer},
            device_id_type=MESH,
        )
        cp2.start()
        cp2.wait()
        out_ref[:, :, pl.ds(c * w, w)] = s2buf[x] + st2[c]


def fused(holder, rowblk, picked, activations, n_feat, n_tok, scale):
    slots = holder.shape[0]
    tokens, width = activations.shape[0], BLK
    panel_blocks = activations.shape[1] // BLK
    w = width // CHUNKS
    n_y = n_tok // 4
    piece = width // n_tok
    kernel = functools.partial(fused_kernel, n_feat, n_tok, CHUNKS, scale)
    blk = (slots, piece, w)
    return pl.pallas_call(
        kernel,
        out_shape=jax.ShapeDtypeStruct((slots, piece, width), jnp.float32),
        in_specs=[
            pl.BlockSpec(memory_space=pltpu.SMEM),
            pl.BlockSpec(memory_space=pltpu.SMEM),
            pl.BlockSpec(memory_space=pltpu.SMEM),
            pl.BlockSpec(memory_space=pl.ANY),
        ],
        out_specs=pl.BlockSpec(memory_space=pltpu.VMEM),
        scratch_shapes=[pltpu.VMEM((n_feat, tokens, w), activations.dtype) for _ in range(CHUNKS)] + [
            pltpu.VMEM((panel_blocks, tokens, width), activations.dtype),
            pltpu.VMEM((n_feat, tokens, width), activations.dtype),
            pltpu.VMEM((2, n_y, 2) + blk, jnp.float32),
            pltpu.VMEM((CHUNKS, n_y, 2) + blk, jnp.float32),
            pltpu.VMEM((n_y, 2) + blk, jnp.float32),
            pltpu.VMEM((CHUNKS, n_y, 2) + blk, jnp.float32),
            pltpu.VMEM((2,) + blk, jnp.float32),
            pltpu.VMEM((CHUNKS,) + blk, jnp.float32),
            pltpu.SemaphoreType.DMA((panel_blocks,)),
            pltpu.SemaphoreType.DMA((CHUNKS, n_feat)),
            pltpu.SemaphoreType.DMA((CHUNKS, n_feat)),
            pltpu.SemaphoreType.DMA((CHUNKS,)),
            pltpu.SemaphoreType.DMA((CHUNKS,)),
            pltpu.SemaphoreType.DMA((CHUNKS,)),
            pltpu.SemaphoreType.DMA((CHUNKS, n_y)),
            pltpu.SemaphoreType.DMA((CHUNKS, n_y)),
            pltpu.SemaphoreType.DMA((CHUNKS,)),
            pltpu.SemaphoreType.DMA((CHUNKS,)),
            pltpu.VMEM((n_y, slots - (slots * 7) // 12, piece, w), jnp.float32),
            pltpu.VMEM((n_y, slots - (slots * 7) // 12, piece, w), jnp.float32),
            pltpu.VMEM((n_y, slots - (slots * 7) // 12, piece, w), jnp.float32),
            pltpu.SemaphoreType.DMA((2,)),
            pltpu.SemaphoreType.DMA((n_y,)),
            pltpu.SemaphoreType.DMA((n_y,)),
        ],
        compiler_params=pltpu.CompilerParams(
            collective_id=0, has_side_effects=True, vmem_limit_bytes=60 * 1024 * 1024
        ),
    )(holder, rowblk, picked, activations)


def body(activations, pattern, block_slot):
    tok_rows, width = activations.shape
    feat_count = lax.axis_size("feat")
    tok_count = lax.axis_size("tok")
    my_index = lax.axis_index("feat")
    panel_blocks = width // BLK
    list_length = pattern.shape[0]
    per_device = list_length // feat_count
    scale = 1.0 / (tok_rows * tok_count)
    ordered = jnp.zeros_like(pattern).at[block_slot].set(pattern)
    pairs = ordered.reshape(feat_count, per_device, 2)
    holder = pairs[:, :, 1] // panel_blocks
    local_column = pairs[:, :, 1] % panel_blocks
    picked = jnp.sum(jnp.where(holder == my_index, local_column, 0), axis=1)
    my_pairs = lax.dynamic_index_in_dim(pairs, my_index, 0, keepdims=False)
    my_holder = my_pairs[:, 1] // panel_blocks
    rowblk = my_pairs[:, 0] % panel_blocks
    out = fused(my_holder, rowblk, picked, activations, feat_count, tok_count, scale)
    return out.transpose(1, 0, 2)


def solution(mesh):
    placed = (P("tok", "feat"), P(), P())
    return jax.shard_map(
        body, mesh=mesh, in_specs=placed, out_specs=P("tok", "feat", None), check_vma=False
    )
```

```python
import functools

import jax
import jax.numpy as jnp
from jax import lax
from jax.experimental import pallas as pl
from jax.experimental.pallas import tpu as pltpu
from jax.sharding import PartitionSpec as P

BLK = 512
CHUNKS = 4
MESH = pl.DeviceIdType.MESH


def fused_kernel(n_feat, n_tok, chunks, scale,
                 holder_ref, rowblk_ref, picked_ref, act_hbm, out_ref, *scratch):
    recv = scratch[:chunks]
    (act_ref, send_ref, gbuf, st0, s1buf, st1, s2buf, st2, panel_sem,
     fsend, frecv, flocal, send0, recv0, send1, recv1, send2, recv2,
     bxbuf, bsum, bybuf, bsem, bysend, byrecv) = scratch[chunks:]
    slots = holder_ref.shape[0]
    tokens, width = send_ref.shape[1], send_ref.shape[2]
    panel_blocks = act_ref.shape[0]
    w = width // chunks
    n_y = n_tok // 4
    piece = width // n_tok
    me = lax.axis_index("feat")
    t = lax.axis_index("tok")
    x = t // (2 * n_y)
    y = (t // 2) % n_y
    core = t % 2
    core_peer = t + 1 - 2 * core
    x_peer = t + (1 - 2 * x) * 2 * n_y

    barrier = pltpu.get_barrier_semaphore()
    for k in range(1, n_feat):
        pl.semaphore_signal(barrier, 1, device_id={"feat": lax.rem(me + k, n_feat)}, device_id_type=MESH)
    for o in range(1, n_y):
        dest = x * 2 * n_y + lax.rem(y + o, n_y) * 2 + core
        pl.semaphore_signal(barrier, 1, device_id={"tok": dest}, device_id_type=MESH)
    pl.semaphore_signal(barrier, 1, device_id={"tok": core_peer}, device_id_type=MESH)
    pl.semaphore_signal(barrier, 1, device_id={"tok": x_peer}, device_id_type=MESH)

    panel = [
        pltpu.make_async_copy(act_hbm.at[:, pl.ds(b * width, width)], act_ref.at[b], panel_sem.at[b])
        for b in range(panel_blocks)
    ]
    for cp in panel:
        cp.start()
    for cp in panel:
        cp.wait()
    for p in range(n_feat):
        send_ref[p] = act_ref[picked_ref[p]]

    pl.semaphore_wait(barrier, n_feat - 1 + n_y - 1 + 2)

    def feat_copies(c):
        cols = pl.ds(c * w, w)
        local = pltpu.make_async_copy(send_ref.at[me, :, cols], recv[c].at[me], flocal.at[c])
        copies = [local]
        for k in sorted(range(1, n_feat), key=lambda k: min(k, n_feat - k)):
            peer = lax.rem(me + k, n_feat)
            copies.append(pltpu.make_async_remote_copy(
                src_ref=send_ref.at[peer, :, cols],
                dst_ref=recv[c].at[me],
                send_sem=fsend.at[c, k],
                recv_sem=frecv.at[c, k],
                device_id={"feat": peer},
                device_id_type=MESH,
            ))
        return copies

    def reduce_last(c, gram_one):
        h = (slots * 7) // 12
        cols = pl.ds(c * w, w)
        cp0a = pltpu.make_async_remote_copy(
            src_ref=gbuf.at[1 - core, :, :, pl.ds(0, h)], dst_ref=st0.at[c, :, :, pl.ds(0, h)],
            send_sem=send0.at[c], recv_sem=recv0.at[c], device_id={"tok": core_peer}, device_id_type=MESH,
        )
        cp0b = pltpu.make_async_remote_copy(
            src_ref=gbuf.at[1 - core, :, :, pl.ds(h, slots - h)],
            dst_ref=st0.at[c, :, :, pl.ds(h, slots - h)],
            send_sem=bsem.at[2], recv_sem=bsem.at[3], device_id={"tok": core_peer}, device_id_type=MESH,
        )
        lax.fori_loop(0, h, gram_one, 0)
        cp0a.start()
        lax.fori_loop(h, slots, gram_one, 0)
        cp0b.start()
        cp0a.wait()
        s1buf[:, :, :h] = gbuf[core, :, :, :h] + st0[c, :, :, :h]
        a_y = []
        for o in range(1, n_y):
            dy = lax.rem(y + o, n_y)
            cp = pltpu.make_async_remote_copy(
                src_ref=s1buf.at[dy, :, pl.ds(0, h)], dst_ref=st1.at[c, y, :, pl.ds(0, h)],
                send_sem=send1.at[c, o], recv_sem=recv1.at[c, o],
                device_id={"tok": x * 2 * n_y + dy * 2 + core}, device_id_type=MESH,
            )
            cp.start()
            a_y.append(cp)
        cp0b.wait()
        s1buf[:, :, h:] = gbuf[core, :, :, h:] + st0[c, :, :, h:]
        b_x = pltpu.make_async_remote_copy(
            src_ref=s1buf.at[:, 1 - x, pl.ds(h, slots - h)], dst_ref=bxbuf,
            send_sem=bsem.at[0], recv_sem=bsem.at[1], device_id={"tok": x_peer}, device_id_type=MESH,
        )
        b_x.start()
        b_x.wait()
        bsum[...] = s1buf[:, x, h:] + bxbuf[...]
        b_y = []
        for o in range(1, n_y):
            dy = lax.rem(y + o, n_y)
            cp = pltpu.make_async_remote_copy(
                src_ref=bsum.at[dy], dst_ref=bybuf.at[y],
                send_sem=bysend.at[o], recv_sem=byrecv.at[o],
                device_id={"tok": x * 2 * n_y + dy * 2 + core}, device_id_type=MESH,
            )
            cp.start()
            b_y.append(cp)
        for cp in a_y:
            cp.wait()
        acc = s1buf[y, :, :h]
        for o in range(1, n_y):
            acc = acc + st1[c, lax.rem(y + o, n_y), :, :h]
        s2buf[:, :h] = acc
        a_x = pltpu.make_async_remote_copy(
            src_ref=s2buf.at[1 - x, pl.ds(0, h)], dst_ref=st2.at[c, pl.ds(0, h)],
            send_sem=send2.at[c], recv_sem=recv2.at[c], device_id={"tok": x_peer}, device_id_type=MESH,
        )
        a_x.start()
        for cp in b_y:
            cp.wait()
        accb = bsum[y]
        for o in range(1, n_y):
            accb = accb + bybuf[lax.rem(y + o, n_y)]
        out_ref[h:, :, cols] = accb
        a_x.wait()
        out_ref[:h, :, cols] = s2buf[x, :h] + st2[c, :h]

    in_flight = []
    for c in range(min(2, chunks)):
        in_flight.append(feat_copies(c))
        for cp in in_flight[-1]:
            cp.start()
    for c in range(chunks):
        for cp in in_flight[c]:
            cp.wait()
        if c + 2 < chunks:
            in_flight.append(feat_copies(c + 2))
            for cp in in_flight[-1]:
                cp.start()

        def gram_one(k, carry):
            q = recv[c][holder_ref[k]]
            p = act_ref[rowblk_ref[k]]
            g = lax.dot_general(
                p, q, (((0,), (0,)), ((), ())), preferred_element_type=jnp.float32
            ) * scale
            for xx in range(2):
                for yy in range(n_y):
                    for cc in range(2):
                        r0 = ((xx * n_y + yy) * 2 + cc) * piece
                        gbuf[cc, yy, xx, k] = g[r0:r0 + piece, :]
            return carry

        if c == chunks - 1 and slots > 1:
            reduce_last(c, gram_one)
            continue

        lax.fori_loop(0, slots, gram_one, 0)

        cp0 = pltpu.make_async_remote_copy(
            src_ref=gbuf.at[1 - core],
            dst_ref=st0.at[c],
            send_sem=send0.at[c],
            recv_sem=recv0.at[c],
            device_id={"tok": core_peer},
            device_id_type=MESH,
        )
        cp0.start()
        cp0.wait()
        s1buf[...] = gbuf[core] + st0[c]

        copies1 = []
        for o in range(1, n_y):
            dy = lax.rem(y + o, n_y)
            cp = pltpu.make_async_remote_copy(
                src_ref=s1buf.at[dy],
                dst_ref=st1.at[c, y],
                send_sem=send1.at[c, o],
                recv_sem=recv1.at[c, o],
                device_id={"tok": x * 2 * n_y + dy * 2 + core},
                device_id_type=MESH,
            )
            cp.start()
            copies1.append(cp)
        for cp in copies1:
            cp.wait()
        acc = s1buf[y]
        for o in range(1, n_y):
            acc = acc + st1[c, lax.rem(y + o, n_y)]
        s2buf[...] = acc

        cp2 = pltpu.make_async_remote_copy(
            src_ref=s2buf.at[1 - x],
            dst_ref=st2.at[c],
            send_sem=send2.at[c],
            recv_sem=recv2.at[c],
            device_id={"tok": x_peer},
            device_id_type=MESH,
        )
        cp2.start()
        cp2.wait()
        out_ref[:, :, pl.ds(c * w, w)] = s2buf[x] + st2[c]


def fused(holder, rowblk, picked, activations, n_feat, n_tok, scale):
    slots = holder.shape[0]
    tokens, width = activations.shape[0], BLK
    panel_blocks = activations.shape[1] // BLK
    w = width // CHUNKS
    n_y = n_tok // 4
    piece = width // n_tok
    kernel = functools.partial(fused_kernel, n_feat, n_tok, CHUNKS, scale)
    blk = (slots, piece, w)
    return pl.pallas_call(
        kernel,
        out_shape=jax.ShapeDtypeStruct((slots, piece, width), jnp.float32),
        in_specs=[
            pl.BlockSpec(memory_space=pltpu.SMEM),
            pl.BlockSpec(memory_space=pltpu.SMEM),
            pl.BlockSpec(memory_space=pltpu.SMEM),
            pl.BlockSpec(memory_space=pl.ANY),
        ],
        out_specs=pl.BlockSpec(memory_space=pltpu.VMEM),
        scratch_shapes=[pltpu.VMEM((n_feat, tokens, w), activations.dtype) for _ in range(CHUNKS)] + [
            pltpu.VMEM((panel_blocks, tokens, width), activations.dtype),
            pltpu.VMEM((n_feat, tokens, width), activations.dtype),
            pltpu.VMEM((2, n_y, 2) + blk, jnp.float32),
            pltpu.VMEM((CHUNKS, n_y, 2) + blk, jnp.float32),
            pltpu.VMEM((n_y, 2) + blk, jnp.float32),
            pltpu.VMEM((CHUNKS, n_y, 2) + blk, jnp.float32),
            pltpu.VMEM((2,) + blk, jnp.float32),
            pltpu.VMEM((CHUNKS,) + blk, jnp.float32),
            pltpu.SemaphoreType.DMA((panel_blocks,)),
            pltpu.SemaphoreType.DMA((CHUNKS, n_feat)),
            pltpu.SemaphoreType.DMA((CHUNKS, n_feat)),
            pltpu.SemaphoreType.DMA((CHUNKS,)),
            pltpu.SemaphoreType.DMA((CHUNKS,)),
            pltpu.SemaphoreType.DMA((CHUNKS,)),
            pltpu.SemaphoreType.DMA((CHUNKS, n_y)),
            pltpu.SemaphoreType.DMA((CHUNKS, n_y)),
            pltpu.SemaphoreType.DMA((CHUNKS,)),
            pltpu.SemaphoreType.DMA((CHUNKS,)),
            pltpu.VMEM((n_y, slots - (slots * 7) // 12, piece, w), jnp.float32),
            pltpu.VMEM((n_y, slots - (slots * 7) // 12, piece, w), jnp.float32),
            pltpu.VMEM((n_y, slots - (slots * 7) // 12, piece, w), jnp.float32),
            pltpu.SemaphoreType.DMA((4,)),
            pltpu.SemaphoreType.DMA((n_y,)),
            pltpu.SemaphoreType.DMA((n_y,)),
        ],
        compiler_params=pltpu.CompilerParams(
            collective_id=0, has_side_effects=True, vmem_limit_bytes=60 * 1024 * 1024
        ),
    )(holder, rowblk, picked, activations)


def body(activations, pattern, block_slot):
    tok_rows, width = activations.shape
    feat_count = lax.axis_size("feat")
    tok_count = lax.axis_size("tok")
    my_index = lax.axis_index("feat")
    panel_blocks = width // BLK
    list_length = pattern.shape[0]
    per_device = list_length // feat_count
    scale = 1.0 / (tok_rows * tok_count)
    ordered = jnp.zeros_like(pattern).at[block_slot].set(pattern)
    pairs = ordered.reshape(feat_count, per_device, 2)
    holder = pairs[:, :, 1] // panel_blocks
    local_column = pairs[:, :, 1] % panel_blocks
    picked = jnp.sum(jnp.where(holder == my_index, local_column, 0), axis=1)
    my_pairs = lax.dynamic_index_in_dim(pairs, my_index, 0, keepdims=False)
    my_holder = my_pairs[:, 1] // panel_blocks
    rowblk = my_pairs[:, 0] % panel_blocks
    out = fused(my_holder, rowblk, picked, activations, feat_count, tok_count, scale)
    return out.transpose(1, 0, 2)


def solution(mesh):
    placed = (P("tok", "feat"), P(), P())
    return jax.shard_map(
        body, mesh=mesh, in_specs=placed, out_specs=P("tok", "feat", None), check_vma=False
    )
```

```python
import functools

import jax
import jax.numpy as jnp
from jax import lax
from jax.experimental import pallas as pl
from jax.experimental.pallas import tpu as pltpu
from jax.sharding import PartitionSpec as P

BLK = 512
CHUNKS = 4
MESH = pl.DeviceIdType.MESH


def fused_kernel(n_feat, n_tok, chunks, scale,
                 holder_ref, rowblk_ref, picked_ref, act_hbm, out_ref, *scratch):
    recv = scratch[:chunks]
    (act_ref, send_ref, gbuf, st0, s1buf, st1, s2buf, st2, panel_sem,
     fsend, frecv, flocal, send0, recv0, send1, recv1, send2, recv2,
     bxbuf, bsum, bybuf, bsem, bysend, byrecv) = scratch[chunks:]
    slots = holder_ref.shape[0]
    tokens, width = send_ref.shape[1], send_ref.shape[2]
    panel_blocks = act_ref.shape[0]
    w = width // chunks
    n_y = n_tok // 4
    piece = width // n_tok
    me = lax.axis_index("feat")
    t = lax.axis_index("tok")
    x = t // (2 * n_y)
    y = (t // 2) % n_y
    core = t % 2
    core_peer = t + 1 - 2 * core
    x_peer = t + (1 - 2 * x) * 2 * n_y

    barrier = pltpu.get_barrier_semaphore()
    for k in range(1, n_feat):
        pl.semaphore_signal(barrier, 1, device_id={"feat": lax.rem(me + k, n_feat)}, device_id_type=MESH)
    for o in range(1, n_y):
        dest = x * 2 * n_y + lax.rem(y + o, n_y) * 2 + core
        pl.semaphore_signal(barrier, 1, device_id={"tok": dest}, device_id_type=MESH)
    pl.semaphore_signal(barrier, 1, device_id={"tok": core_peer}, device_id_type=MESH)
    pl.semaphore_signal(barrier, 1, device_id={"tok": x_peer}, device_id_type=MESH)

    panel = [
        pltpu.make_async_copy(act_hbm.at[:, pl.ds(b * width, width)], act_ref.at[b], panel_sem.at[b])
        for b in range(panel_blocks)
    ]
    for cp in panel:
        cp.start()
    for cp in panel:
        cp.wait()
    for p in range(n_feat):
        send_ref[p] = act_ref[picked_ref[p]]

    pl.semaphore_wait(barrier, n_feat - 1 + n_y - 1 + 2)

    def feat_copies(c):
        cols = pl.ds(c * w, w)
        local = pltpu.make_async_copy(send_ref.at[me, :, cols], recv[c].at[me], flocal.at[c])
        copies = [local]
        for k in sorted(range(1, n_feat), key=lambda k: min(k, n_feat - k)):
            peer = lax.rem(me + k, n_feat)
            copies.append(pltpu.make_async_remote_copy(
                src_ref=send_ref.at[peer, :, cols],
                dst_ref=recv[c].at[me],
                send_sem=fsend.at[c, k],
                recv_sem=frecv.at[c, k],
                device_id={"feat": peer},
                device_id_type=MESH,
            ))
        return copies

    def reduce_last(c, gram_one):
        h = (slots * 8) // 12
        cols = pl.ds(c * w, w)
        cp0a = pltpu.make_async_remote_copy(
            src_ref=gbuf.at[1 - core, :, :, pl.ds(0, h)], dst_ref=st0.at[c, :, :, pl.ds(0, h)],
            send_sem=send0.at[c], recv_sem=recv0.at[c], device_id={"tok": core_peer}, device_id_type=MESH,
        )
        cp0b = pltpu.make_async_remote_copy(
            src_ref=gbuf.at[1 - core, :, :, pl.ds(h, slots - h)],
            dst_ref=st0.at[c, :, :, pl.ds(h, slots - h)],
            send_sem=bsem.at[2], recv_sem=bsem.at[3], device_id={"tok": core_peer}, device_id_type=MESH,
        )
        lax.fori_loop(0, h, gram_one, 0)
        cp0a.start()
        lax.fori_loop(h, slots, gram_one, 0)
        cp0b.start()
        cp0a.wait()
        s1buf[:, :, :h] = gbuf[core, :, :, :h] + st0[c, :, :, :h]
        a_y = []
        for o in range(1, n_y):
            dy = lax.rem(y + o, n_y)
            cp = pltpu.make_async_remote_copy(
                src_ref=s1buf.at[dy, :, pl.ds(0, h)], dst_ref=st1.at[c, y, :, pl.ds(0, h)],
                send_sem=send1.at[c, o], recv_sem=recv1.at[c, o],
                device_id={"tok": x * 2 * n_y + dy * 2 + core}, device_id_type=MESH,
            )
            cp.start()
            a_y.append(cp)
        cp0b.wait()
        s1buf[:, :, h:] = gbuf[core, :, :, h:] + st0[c, :, :, h:]
        b_x = pltpu.make_async_remote_copy(
            src_ref=s1buf.at[:, 1 - x, pl.ds(h, slots - h)], dst_ref=bxbuf,
            send_sem=bsem.at[0], recv_sem=bsem.at[1], device_id={"tok": x_peer}, device_id_type=MESH,
        )
        b_x.start()
        b_x.wait()
        bsum[...] = s1buf[:, x, h:] + bxbuf[...]
        b_y = []
        for o in range(1, n_y):
            dy = lax.rem(y + o, n_y)
            cp = pltpu.make_async_remote_copy(
                src_ref=bsum.at[dy], dst_ref=bybuf.at[y],
                send_sem=bysend.at[o], recv_sem=byrecv.at[o],
                device_id={"tok": x * 2 * n_y + dy * 2 + core}, device_id_type=MESH,
            )
            cp.start()
            b_y.append(cp)
        for cp in a_y:
            cp.wait()
        acc = s1buf[y, :, :h]
        for o in range(1, n_y):
            acc = acc + st1[c, lax.rem(y + o, n_y), :, :h]
        s2buf[:, :h] = acc
        a_x = pltpu.make_async_remote_copy(
            src_ref=s2buf.at[1 - x, pl.ds(0, h)], dst_ref=st2.at[c, pl.ds(0, h)],
            send_sem=send2.at[c], recv_sem=recv2.at[c], device_id={"tok": x_peer}, device_id_type=MESH,
        )
        a_x.start()
        for cp in b_y:
            cp.wait()
        accb = bsum[y]
        for o in range(1, n_y):
            accb = accb + bybuf[lax.rem(y + o, n_y)]
        out_ref[h:, :, cols] = accb
        a_x.wait()
        out_ref[:h, :, cols] = s2buf[x, :h] + st2[c, :h]

    in_flight = []
    for c in range(min(2, chunks)):
        in_flight.append(feat_copies(c))
        for cp in in_flight[-1]:
            cp.start()
    for c in range(chunks):
        for cp in in_flight[c]:
            cp.wait()
        if c + 2 < chunks:
            in_flight.append(feat_copies(c + 2))
            for cp in in_flight[-1]:
                cp.start()

        def gram_one(k, carry):
            q = recv[c][holder_ref[k]]
            p = act_ref[rowblk_ref[k]]
            g = lax.dot_general(
                p, q, (((0,), (0,)), ((), ())), preferred_element_type=jnp.float32
            ) * scale
            for xx in range(2):
                for yy in range(n_y):
                    for cc in range(2):
                        r0 = ((xx * n_y + yy) * 2 + cc) * piece
                        gbuf[cc, yy, xx, k] = g[r0:r0 + piece, :]
            return carry

        if c == chunks - 1 and slots > 1:
            reduce_last(c, gram_one)
            continue

        lax.fori_loop(0, slots, gram_one, 0)

        cp0 = pltpu.make_async_remote_copy(
            src_ref=gbuf.at[1 - core],
            dst_ref=st0.at[c],
            send_sem=send0.at[c],
            recv_sem=recv0.at[c],
            device_id={"tok": core_peer},
            device_id_type=MESH,
        )
        cp0.start()
        cp0.wait()
        s1buf[...] = gbuf[core] + st0[c]

        copies1 = []
        for o in range(1, n_y):
            dy = lax.rem(y + o, n_y)
            cp = pltpu.make_async_remote_copy(
                src_ref=s1buf.at[dy],
                dst_ref=st1.at[c, y],
                send_sem=send1.at[c, o],
                recv_sem=recv1.at[c, o],
                device_id={"tok": x * 2 * n_y + dy * 2 + core},
                device_id_type=MESH,
            )
            cp.start()
            copies1.append(cp)
        for cp in copies1:
            cp.wait()
        acc = s1buf[y]
        for o in range(1, n_y):
            acc = acc + st1[c, lax.rem(y + o, n_y)]
        s2buf[...] = acc

        cp2 = pltpu.make_async_remote_copy(
            src_ref=s2buf.at[1 - x],
            dst_ref=st2.at[c],
            send_sem=send2.at[c],
            recv_sem=recv2.at[c],
            device_id={"tok": x_peer},
            device_id_type=MESH,
        )
        cp2.start()
        cp2.wait()
        out_ref[:, :, pl.ds(c * w, w)] = s2buf[x] + st2[c]


def fused(holder, rowblk, picked, activations, n_feat, n_tok, scale):
    slots = holder.shape[0]
    tokens, width = activations.shape[0], BLK
    panel_blocks = activations.shape[1] // BLK
    w = width // CHUNKS
    n_y = n_tok // 4
    piece = width // n_tok
    kernel = functools.partial(fused_kernel, n_feat, n_tok, CHUNKS, scale)
    blk = (slots, piece, w)
    return pl.pallas_call(
        kernel,
        out_shape=jax.ShapeDtypeStruct((slots, piece, width), jnp.float32),
        in_specs=[
            pl.BlockSpec(memory_space=pltpu.SMEM),
            pl.BlockSpec(memory_space=pltpu.SMEM),
            pl.BlockSpec(memory_space=pltpu.SMEM),
            pl.BlockSpec(memory_space=pl.ANY),
        ],
        out_specs=pl.BlockSpec(memory_space=pltpu.VMEM),
        scratch_shapes=[pltpu.VMEM((n_feat, tokens, w), activations.dtype) for _ in range(CHUNKS)] + [
            pltpu.VMEM((panel_blocks, tokens, width), activations.dtype),
            pltpu.VMEM((n_feat, tokens, width), activations.dtype),
            pltpu.VMEM((2, n_y, 2) + blk, jnp.float32),
            pltpu.VMEM((CHUNKS, n_y, 2) + blk, jnp.float32),
            pltpu.VMEM((n_y, 2) + blk, jnp.float32),
            pltpu.VMEM((CHUNKS, n_y, 2) + blk, jnp.float32),
            pltpu.VMEM((2,) + blk, jnp.float32),
            pltpu.VMEM((CHUNKS,) + blk, jnp.float32),
            pltpu.SemaphoreType.DMA((panel_blocks,)),
            pltpu.SemaphoreType.DMA((CHUNKS, n_feat)),
            pltpu.SemaphoreType.DMA((CHUNKS, n_feat)),
            pltpu.SemaphoreType.DMA((CHUNKS,)),
            pltpu.SemaphoreType.DMA((CHUNKS,)),
            pltpu.SemaphoreType.DMA((CHUNKS,)),
            pltpu.SemaphoreType.DMA((CHUNKS, n_y)),
            pltpu.SemaphoreType.DMA((CHUNKS, n_y)),
            pltpu.SemaphoreType.DMA((CHUNKS,)),
            pltpu.SemaphoreType.DMA((CHUNKS,)),
            pltpu.VMEM((n_y, slots - (slots * 8) // 12, piece, w), jnp.float32),
            pltpu.VMEM((n_y, slots - (slots * 8) // 12, piece, w), jnp.float32),
            pltpu.VMEM((n_y, slots - (slots * 8) // 12, piece, w), jnp.float32),
            pltpu.SemaphoreType.DMA((4,)),
            pltpu.SemaphoreType.DMA((n_y,)),
            pltpu.SemaphoreType.DMA((n_y,)),
        ],
        compiler_params=pltpu.CompilerParams(
            collective_id=0, has_side_effects=True, vmem_limit_bytes=60 * 1024 * 1024
        ),
    )(holder, rowblk, picked, activations)


def body(activations, pattern, block_slot):
    tok_rows, width = activations.shape
    feat_count = lax.axis_size("feat")
    tok_count = lax.axis_size("tok")
    my_index = lax.axis_index("feat")
    panel_blocks = width // BLK
    list_length = pattern.shape[0]
    per_device = list_length // feat_count
    scale = 1.0 / (tok_rows * tok_count)
    ordered = jnp.zeros_like(pattern).at[block_slot].set(pattern)
    pairs = ordered.reshape(feat_count, per_device, 2)
    holder = pairs[:, :, 1] // panel_blocks
    local_column = pairs[:, :, 1] % panel_blocks
    picked = jnp.sum(jnp.where(holder == my_index, local_column, 0), axis=1)
    my_pairs = lax.dynamic_index_in_dim(pairs, my_index, 0, keepdims=False)
    my_holder = my_pairs[:, 1] // panel_blocks
    rowblk = my_pairs[:, 0] % panel_blocks
    out = fused(my_holder, rowblk, picked, activations, feat_count, tok_count, scale)
    return out.transpose(1, 0, 2)


def solution(mesh):
    placed = (P("tok", "feat"), P(), P())
    return jax.shard_map(
        body, mesh=mesh, in_specs=placed, out_specs=P("tok", "feat", None), check_vma=False
    )
```

```python
import functools

import jax
import jax.numpy as jnp
from jax import lax
from jax.experimental import pallas as pl
from jax.experimental.pallas import tpu as pltpu
from jax.sharding import PartitionSpec as P

BLK = 512
CHUNKS = 4
MESH = pl.DeviceIdType.MESH


def fused_kernel(n_feat, n_tok, chunks, scale,
                 holder_ref, rowblk_ref, picked_ref, act_hbm, out_ref, *scratch):
    recv = scratch[:chunks]
    (act_ref, send_ref, gbuf, st0, s1buf, st1, s2buf, st2, panel_sem,
     fsend, frecv, flocal, send0, recv0, send1, recv1, send2, recv2,
     bxbuf, bsum, bybuf, bsem, bysend, byrecv) = scratch[chunks:]
    slots = holder_ref.shape[0]
    tokens, width = send_ref.shape[1], send_ref.shape[2]
    panel_blocks = act_ref.shape[0]
    w = width // chunks
    n_y = n_tok // 4
    piece = width // n_tok
    me = lax.axis_index("feat")
    t = lax.axis_index("tok")
    x = t // (2 * n_y)
    y = (t // 2) % n_y
    core = t % 2
    core_peer = t + 1 - 2 * core
    x_peer = t + (1 - 2 * x) * 2 * n_y

    barrier = pltpu.get_barrier_semaphore()
    for k in range(1, n_feat):
        pl.semaphore_signal(barrier, 1, device_id={"feat": lax.rem(me + k, n_feat)}, device_id_type=MESH)
    for o in range(1, n_y):
        dest = x * 2 * n_y + lax.rem(y + o, n_y) * 2 + core
        pl.semaphore_signal(barrier, 1, device_id={"tok": dest}, device_id_type=MESH)
    pl.semaphore_signal(barrier, 1, device_id={"tok": core_peer}, device_id_type=MESH)
    pl.semaphore_signal(barrier, 1, device_id={"tok": x_peer}, device_id_type=MESH)

    panel = [
        pltpu.make_async_copy(act_hbm.at[:, pl.ds(b * width, width)], act_ref.at[b], panel_sem.at[b])
        for b in range(panel_blocks)
    ]
    for cp in panel:
        cp.start()
    for cp in panel:
        cp.wait()
    for p in range(n_feat):
        send_ref[p] = act_ref[picked_ref[p]]

    pl.semaphore_wait(barrier, n_feat - 1 + n_y - 1 + 2)

    def feat_copies(c):
        cols = pl.ds(c * w, w)
        local = pltpu.make_async_copy(send_ref.at[me, :, cols], recv[c].at[me], flocal.at[c])
        copies = [local]
        for k in sorted(range(1, n_feat), key=lambda k: min(k, n_feat - k)):
            peer = lax.rem(me + k, n_feat)
            copies.append(pltpu.make_async_remote_copy(
                src_ref=send_ref.at[peer, :, cols],
                dst_ref=recv[c].at[me],
                send_sem=fsend.at[c, k],
                recv_sem=frecv.at[c, k],
                device_id={"feat": peer},
                device_id_type=MESH,
            ))
        return copies

    def reduce_last(c, gram_one):
        h = slots // 2
        cols = pl.ds(c * w, w)
        cp0a = pltpu.make_async_remote_copy(
            src_ref=gbuf.at[1 - core, :, :, pl.ds(0, h)], dst_ref=st0.at[c, :, :, pl.ds(0, h)],
            send_sem=send0.at[c], recv_sem=recv0.at[c], device_id={"tok": core_peer}, device_id_type=MESH,
        )
        cp0b = pltpu.make_async_remote_copy(
            src_ref=gbuf.at[1 - core, :, :, pl.ds(h, slots - h)],
            dst_ref=st0.at[c, :, :, pl.ds(h, slots - h)],
            send_sem=bsem.at[2], recv_sem=bsem.at[3], device_id={"tok": core_peer}, device_id_type=MESH,
        )
        lax.fori_loop(0, h, gram_one, 0)
        cp0a.start()
        lax.fori_loop(h, slots, gram_one, 0)
        cp0b.start()
        cp0a.wait()
        s1buf[:, :, :h] = gbuf[core, :, :, :h] + st0[c, :, :, :h]
        a_y = []
        for o in range(1, n_y):
            dy = lax.rem(y + o, n_y)
            cp = pltpu.make_async_remote_copy(
                src_ref=s1buf.at[dy, :, pl.ds(0, h)], dst_ref=st1.at[c, y, :, pl.ds(0, h)],
                send_sem=send1.at[c, o], recv_sem=recv1.at[c, o],
                device_id={"tok": x * 2 * n_y + dy * 2 + core}, device_id_type=MESH,
            )
            cp.start()
            a_y.append(cp)
        cp0b.wait()
        s1buf[:, :, h:] = gbuf[core, :, :, h:] + st0[c, :, :, h:]
        b_x = pltpu.make_async_remote_copy(
            src_ref=s1buf.at[:, 1 - x, pl.ds(h, slots - h)], dst_ref=bxbuf,
            send_sem=bsem.at[0], recv_sem=bsem.at[1], device_id={"tok": x_peer}, device_id_type=MESH,
        )
        b_x.start()
        b_x.wait()
        bsum[...] = s1buf[:, x, h:] + bxbuf[...]
        b_y = []
        for o in range(1, n_y):
            dy = lax.rem(y + o, n_y)
            cp = pltpu.make_async_remote_copy(
                src_ref=bsum.at[dy], dst_ref=bybuf.at[y],
                send_sem=bysend.at[o], recv_sem=byrecv.at[o],
                device_id={"tok": x * 2 * n_y + dy * 2 + core}, device_id_type=MESH,
            )
            cp.start()
            b_y.append(cp)
        for cp in a_y:
            cp.wait()
        acc = s1buf[y, :, :h]
        for o in range(1, n_y):
            acc = acc + st1[c, lax.rem(y + o, n_y), :, :h]
        s2buf[:, :h] = acc
        a_x = pltpu.make_async_remote_copy(
            src_ref=s2buf.at[1 - x, pl.ds(0, h)], dst_ref=st2.at[c, pl.ds(0, h)],
            send_sem=send2.at[c], recv_sem=recv2.at[c], device_id={"tok": x_peer}, device_id_type=MESH,
        )
        a_x.start()
        for cp in b_y:
            cp.wait()
        accb = bsum[y]
        for o in range(1, n_y):
            accb = accb + bybuf[lax.rem(y + o, n_y)]
        out_ref[h:, :, cols] = accb
        a_x.wait()
        out_ref[:h, :, cols] = s2buf[x, :h] + st2[c, :h]

    in_flight = []
    for c in range(min(2, chunks)):
        in_flight.append(feat_copies(c))
        for cp in in_flight[-1]:
            cp.start()
    for c in range(chunks):
        for cp in in_flight[c]:
            cp.wait()
        if c + 2 < chunks:
            in_flight.append(feat_copies(c + 2))
            for cp in in_flight[-1]:
                cp.start()

        def gram_one(k, carry):
            q = recv[c][holder_ref[k]]
            p = act_ref[rowblk_ref[k]]
            g = lax.dot_general(
                p, q, (((0,), (0,)), ((), ())), preferred_element_type=jnp.float32
            ) * scale
            for xx in range(2):
                for yy in range(n_y):
                    for cc in range(2):
                        r0 = ((xx * n_y + yy) * 2 + cc) * piece
                        gbuf[cc, yy, xx, k] = g[r0:r0 + piece, :]
            return carry

        if c == chunks - 1 and slots > 1:
            reduce_last(c, gram_one)
            continue

        lax.fori_loop(0, slots, gram_one, 0)

        cp0 = pltpu.make_async_remote_copy(
            src_ref=gbuf.at[1 - core],
            dst_ref=st0.at[c],
            send_sem=send0.at[c],
            recv_sem=recv0.at[c],
            device_id={"tok": core_peer},
            device_id_type=MESH,
        )
        cp0.start()
        cp0.wait()
        s1buf[...] = gbuf[core] + st0[c]

        copies1 = []
        for o in range(1, n_y):
            dy = lax.rem(y + o, n_y)
            cp = pltpu.make_async_remote_copy(
                src_ref=s1buf.at[dy],
                dst_ref=st1.at[c, y],
                send_sem=send1.at[c, o],
                recv_sem=recv1.at[c, o],
                device_id={"tok": x * 2 * n_y + dy * 2 + core},
                device_id_type=MESH,
            )
            cp.start()
            copies1.append(cp)
        for cp in copies1:
            cp.wait()
        acc = s1buf[y]
        for o in range(1, n_y):
            acc = acc + st1[c, lax.rem(y + o, n_y)]
        s2buf[...] = acc

        cp2 = pltpu.make_async_remote_copy(
            src_ref=s2buf.at[1 - x],
            dst_ref=st2.at[c],
            send_sem=send2.at[c],
            recv_sem=recv2.at[c],
            device_id={"tok": x_peer},
            device_id_type=MESH,
        )
        cp2.start()
        cp2.wait()
        out_ref[:, :, pl.ds(c * w, w)] = s2buf[x] + st2[c]


def fused(holder, rowblk, picked, activations, n_feat, n_tok, scale):
    slots = holder.shape[0]
    tokens, width = activations.shape[0], BLK
    panel_blocks = activations.shape[1] // BLK
    w = width // CHUNKS
    n_y = n_tok // 4
    piece = width // n_tok
    kernel = functools.partial(fused_kernel, n_feat, n_tok, CHUNKS, scale)
    blk = (slots, piece, w)
    return pl.pallas_call(
        kernel,
        out_shape=jax.ShapeDtypeStruct((slots, piece, width), jnp.float32),
        in_specs=[
            pl.BlockSpec(memory_space=pltpu.SMEM),
            pl.BlockSpec(memory_space=pltpu.SMEM),
            pl.BlockSpec(memory_space=pltpu.SMEM),
            pl.BlockSpec(memory_space=pl.ANY),
        ],
        out_specs=pl.BlockSpec(memory_space=pltpu.VMEM),
        scratch_shapes=[pltpu.VMEM((n_feat, tokens, w), activations.dtype) for _ in range(CHUNKS)] + [
            pltpu.VMEM((panel_blocks, tokens, width), activations.dtype),
            pltpu.VMEM((n_feat, tokens, width), activations.dtype),
            pltpu.VMEM((2, n_y, 2) + blk, jnp.float32),
            pltpu.VMEM((CHUNKS, n_y, 2) + blk, jnp.float32),
            pltpu.VMEM((n_y, 2) + blk, jnp.float32),
            pltpu.VMEM((CHUNKS, n_y, 2) + blk, jnp.float32),
            pltpu.VMEM((2,) + blk, jnp.float32),
            pltpu.VMEM((CHUNKS,) + blk, jnp.float32),
            pltpu.SemaphoreType.DMA((panel_blocks,)),
            pltpu.SemaphoreType.DMA((CHUNKS, n_feat)),
            pltpu.SemaphoreType.DMA((CHUNKS, n_feat)),
            pltpu.SemaphoreType.DMA((CHUNKS,)),
            pltpu.SemaphoreType.DMA((CHUNKS,)),
            pltpu.SemaphoreType.DMA((CHUNKS,)),
            pltpu.SemaphoreType.DMA((CHUNKS, n_y)),
            pltpu.SemaphoreType.DMA((CHUNKS, n_y)),
            pltpu.SemaphoreType.DMA((CHUNKS,)),
            pltpu.SemaphoreType.DMA((CHUNKS,)),
            pltpu.VMEM((n_y, slots - slots // 2, piece, w), jnp.float32),
            pltpu.VMEM((n_y, slots - slots // 2, piece, w), jnp.float32),
            pltpu.VMEM((n_y, slots - slots // 2, piece, w), jnp.float32),
            pltpu.SemaphoreType.DMA((4,)),
            pltpu.SemaphoreType.DMA((n_y,)),
            pltpu.SemaphoreType.DMA((n_y,)),
        ],
        compiler_params=pltpu.CompilerParams(
            collective_id=0, has_side_effects=True, vmem_limit_bytes=60 * 1024 * 1024
        ),
    )(holder, rowblk, picked, activations)


def body(activations, pattern, block_slot):
    tok_rows, width = activations.shape
    feat_count = lax.axis_size("feat")
    tok_count = lax.axis_size("tok")
    my_index = lax.axis_index("feat")
    panel_blocks = width // BLK
    list_length = pattern.shape[0]
    per_device = list_length // feat_count
    scale = 1.0 / (tok_rows * tok_count)
    ordered = jnp.zeros_like(pattern).at[block_slot].set(pattern)
    pairs = ordered.reshape(feat_count, per_device, 2)
    holder = pairs[:, :, 1] // panel_blocks
    local_column = pairs[:, :, 1] % panel_blocks
    picked = jnp.sum(jnp.where(holder == my_index, local_column, 0), axis=1)
    my_pairs = lax.dynamic_index_in_dim(pairs, my_index, 0, keepdims=False)
    my_holder = my_pairs[:, 1] // panel_blocks
    rowblk = my_pairs[:, 0] % panel_blocks
    out = fused(my_holder, rowblk, picked, activations, feat_count, tok_count, scale)
    return out.transpose(1, 0, 2)


def solution(mesh):
    placed = (P("tok", "feat"), P(), P())
    return jax.shard_map(
        body, mesh=mesh, in_specs=placed, out_specs=P("tok", "feat", None), check_vma=False
    )
```

```python
import functools

import jax
import jax.numpy as jnp
from jax import lax
from jax.experimental import pallas as pl
from jax.experimental.pallas import tpu as pltpu
from jax.sharding import PartitionSpec as P

BLK = 512
CHUNKS = 4
MESH = pl.DeviceIdType.MESH


def fused_kernel(n_feat, n_tok, chunks, scale,
                 holder_ref, rowblk_ref, picked_ref, act_hbm, out_ref, *scratch):
    recv = scratch[:chunks]
    (act_ref, send_ref, gbuf, st0, s1buf, st1, s2buf, st2, panel_sem,
     fsend, frecv, flocal, send0, recv0, send1, recv1, send2, recv2,
     bxbuf, bsum, bybuf, bsem, bysend, byrecv) = scratch[chunks:]
    slots = holder_ref.shape[0]
    tokens, width = send_ref.shape[1], send_ref.shape[2]
    panel_blocks = act_ref.shape[0]
    w = width // chunks
    n_y = n_tok // 4
    piece = width // n_tok
    me = lax.axis_index("feat")
    t = lax.axis_index("tok")
    x = t // (2 * n_y)
    y = (t // 2) % n_y
    core = t % 2
    core_peer = t + 1 - 2 * core
    x_peer = t + (1 - 2 * x) * 2 * n_y

    barrier = pltpu.get_barrier_semaphore()
    for k in range(1, n_feat):
        pl.semaphore_signal(barrier, 1, device_id={"feat": lax.rem(me + k, n_feat)}, device_id_type=MESH)
    for o in range(1, n_y):
        dest = x * 2 * n_y + lax.rem(y + o, n_y) * 2 + core
        pl.semaphore_signal(barrier, 1, device_id={"tok": dest}, device_id_type=MESH)
    pl.semaphore_signal(barrier, 1, device_id={"tok": core_peer}, device_id_type=MESH)
    pl.semaphore_signal(barrier, 1, device_id={"tok": x_peer}, device_id_type=MESH)

    panel = [
        pltpu.make_async_copy(act_hbm.at[:, pl.ds(b * width, width)], act_ref.at[b], panel_sem.at[b])
        for b in range(panel_blocks)
    ]
    for cp in panel:
        cp.start()
    for cp in panel:
        cp.wait()
    for p in range(n_feat):
        send_ref[p] = act_ref[picked_ref[p]]

    pl.semaphore_wait(barrier, n_feat - 1 + n_y - 1 + 2)

    def feat_copies(c):
        cols = pl.ds(c * w, w)
        local = pltpu.make_async_copy(send_ref.at[me, :, cols], recv[c].at[me], flocal.at[c])
        copies = [local]
        for k in sorted(range(1, n_feat), key=lambda k: min(k, n_feat - k)):
            peer = lax.rem(me + k, n_feat)
            copies.append(pltpu.make_async_remote_copy(
                src_ref=send_ref.at[peer, :, cols],
                dst_ref=recv[c].at[me],
                send_sem=fsend.at[c, k],
                recv_sem=frecv.at[c, k],
                device_id={"feat": peer},
                device_id_type=MESH,
            ))
        return copies

    def reduce_last(c, gram_one):
        h = (slots * 7) // 12
        cols = pl.ds(c * w, w)
        cp0a = pltpu.make_async_remote_copy(
            src_ref=gbuf.at[1 - core, :, :, pl.ds(0, h)], dst_ref=st0.at[c, :, :, pl.ds(0, h)],
            send_sem=send0.at[c], recv_sem=recv0.at[c], device_id={"tok": core_peer}, device_id_type=MESH,
        )
        cp0b = pltpu.make_async_remote_copy(
            src_ref=gbuf.at[1 - core, :, :, pl.ds(h, slots - h)],
            dst_ref=st0.at[c, :, :, pl.ds(h, slots - h)],
            send_sem=bsem.at[2], recv_sem=bsem.at[3], device_id={"tok": core_peer}, device_id_type=MESH,
        )
        lax.fori_loop(0, h, gram_one, 0)
        cp0a.start()
        lax.fori_loop(h, slots, gram_one, 0)
        cp0b.start()
        cp0a.wait()
        s1buf[:, :, :h] = gbuf[core, :, :, :h] + st0[c, :, :, :h]
        a_y = []
        for o in sorted(range(1, n_y), key=lambda o: min(o, n_y - o)):
            dy = lax.rem(y + o, n_y)
            cp = pltpu.make_async_remote_copy(
                src_ref=s1buf.at[dy, :, pl.ds(0, h)], dst_ref=st1.at[c, y, :, pl.ds(0, h)],
                send_sem=send1.at[c, o], recv_sem=recv1.at[c, o],
                device_id={"tok": x * 2 * n_y + dy * 2 + core}, device_id_type=MESH,
            )
            cp.start()
            a_y.append(cp)
        cp0b.wait()
        s1buf[:, :, h:] = gbuf[core, :, :, h:] + st0[c, :, :, h:]
        b_x = pltpu.make_async_remote_copy(
            src_ref=s1buf.at[:, 1 - x, pl.ds(h, slots - h)], dst_ref=bxbuf,
            send_sem=bsem.at[0], recv_sem=bsem.at[1], device_id={"tok": x_peer}, device_id_type=MESH,
        )
        b_x.start()
        b_x.wait()
        bsum[...] = s1buf[:, x, h:] + bxbuf[...]
        b_y = []
        for o in sorted(range(1, n_y), key=lambda o: min(o, n_y - o)):
            dy = lax.rem(y + o, n_y)
            cp = pltpu.make_async_remote_copy(
                src_ref=bsum.at[dy], dst_ref=bybuf.at[y],
                send_sem=bysend.at[o], recv_sem=byrecv.at[o],
                device_id={"tok": x * 2 * n_y + dy * 2 + core}, device_id_type=MESH,
            )
            cp.start()
            b_y.append(cp)
        for cp in a_y:
            cp.wait()
        acc = s1buf[y, :, :h]
        for o in range(1, n_y):
            acc = acc + st1[c, lax.rem(y + o, n_y), :, :h]
        s2buf[:, :h] = acc
        a_x = pltpu.make_async_remote_copy(
            src_ref=s2buf.at[1 - x, pl.ds(0, h)], dst_ref=st2.at[c, pl.ds(0, h)],
            send_sem=send2.at[c], recv_sem=recv2.at[c], device_id={"tok": x_peer}, device_id_type=MESH,
        )
        a_x.start()
        for cp in b_y:
            cp.wait()
        accb = bsum[y]
        for o in range(1, n_y):
            accb = accb + bybuf[lax.rem(y + o, n_y)]
        out_ref[h:, :, cols] = accb
        a_x.wait()
        out_ref[:h, :, cols] = s2buf[x, :h] + st2[c, :h]

    in_flight = []
    for c in range(min(2, chunks)):
        in_flight.append(feat_copies(c))
        for cp in in_flight[-1]:
            cp.start()
    for c in range(chunks):
        for cp in in_flight[c]:
            cp.wait()
        if c + 2 < chunks:
            in_flight.append(feat_copies(c + 2))
            for cp in in_flight[-1]:
                cp.start()

        def gram_one(k, carry):
            q = recv[c][holder_ref[k]]
            p = act_ref[rowblk_ref[k]]
            g = lax.dot_general(
                p, q, (((0,), (0,)), ((), ())), preferred_element_type=jnp.float32
            ) * scale
            for xx in range(2):
                for yy in range(n_y):
                    for cc in range(2):
                        r0 = ((xx * n_y + yy) * 2 + cc) * piece
                        gbuf[cc, yy, xx, k] = g[r0:r0 + piece, :]
            return carry

        if c == chunks - 1 and slots > 1:
            reduce_last(c, gram_one)
            continue

        lax.fori_loop(0, slots, gram_one, 0)

        cp0 = pltpu.make_async_remote_copy(
            src_ref=gbuf.at[1 - core],
            dst_ref=st0.at[c],
            send_sem=send0.at[c],
            recv_sem=recv0.at[c],
            device_id={"tok": core_peer},
            device_id_type=MESH,
        )
        cp0.start()
        cp0.wait()
        s1buf[...] = gbuf[core] + st0[c]

        copies1 = []
        for o in sorted(range(1, n_y), key=lambda o: min(o, n_y - o)):
            dy = lax.rem(y + o, n_y)
            cp = pltpu.make_async_remote_copy(
                src_ref=s1buf.at[dy],
                dst_ref=st1.at[c, y],
                send_sem=send1.at[c, o],
                recv_sem=recv1.at[c, o],
                device_id={"tok": x * 2 * n_y + dy * 2 + core},
                device_id_type=MESH,
            )
            cp.start()
            copies1.append(cp)
        for cp in copies1:
            cp.wait()
        acc = s1buf[y]
        for o in range(1, n_y):
            acc = acc + st1[c, lax.rem(y + o, n_y)]
        s2buf[...] = acc

        cp2 = pltpu.make_async_remote_copy(
            src_ref=s2buf.at[1 - x],
            dst_ref=st2.at[c],
            send_sem=send2.at[c],
            recv_sem=recv2.at[c],
            device_id={"tok": x_peer},
            device_id_type=MESH,
        )
        cp2.start()
        cp2.wait()
        out_ref[:, :, pl.ds(c * w, w)] = s2buf[x] + st2[c]


def fused(holder, rowblk, picked, activations, n_feat, n_tok, scale):
    slots = holder.shape[0]
    tokens, width = activations.shape[0], BLK
    panel_blocks = activations.shape[1] // BLK
    w = width // CHUNKS
    n_y = n_tok // 4
    piece = width // n_tok
    kernel = functools.partial(fused_kernel, n_feat, n_tok, CHUNKS, scale)
    blk = (slots, piece, w)
    return pl.pallas_call(
        kernel,
        out_shape=jax.ShapeDtypeStruct((slots, piece, width), jnp.float32),
        in_specs=[
            pl.BlockSpec(memory_space=pltpu.SMEM),
            pl.BlockSpec(memory_space=pltpu.SMEM),
            pl.BlockSpec(memory_space=pltpu.SMEM),
            pl.BlockSpec(memory_space=pl.ANY),
        ],
        out_specs=pl.BlockSpec(memory_space=pltpu.VMEM),
        scratch_shapes=[pltpu.VMEM((n_feat, tokens, w), activations.dtype) for _ in range(CHUNKS)] + [
            pltpu.VMEM((panel_blocks, tokens, width), activations.dtype),
            pltpu.VMEM((n_feat, tokens, width), activations.dtype),
            pltpu.VMEM((2, n_y, 2) + blk, jnp.float32),
            pltpu.VMEM((CHUNKS, n_y, 2) + blk, jnp.float32),
            pltpu.VMEM((n_y, 2) + blk, jnp.float32),
            pltpu.VMEM((CHUNKS, n_y, 2) + blk, jnp.float32),
            pltpu.VMEM((2,) + blk, jnp.float32),
            pltpu.VMEM((CHUNKS,) + blk, jnp.float32),
            pltpu.SemaphoreType.DMA((panel_blocks,)),
            pltpu.SemaphoreType.DMA((CHUNKS, n_feat)),
            pltpu.SemaphoreType.DMA((CHUNKS, n_feat)),
            pltpu.SemaphoreType.DMA((CHUNKS,)),
            pltpu.SemaphoreType.DMA((CHUNKS,)),
            pltpu.SemaphoreType.DMA((CHUNKS,)),
            pltpu.SemaphoreType.DMA((CHUNKS, n_y)),
            pltpu.SemaphoreType.DMA((CHUNKS, n_y)),
            pltpu.SemaphoreType.DMA((CHUNKS,)),
            pltpu.SemaphoreType.DMA((CHUNKS,)),
            pltpu.VMEM((n_y, slots - (slots * 7) // 12, piece, w), jnp.float32),
            pltpu.VMEM((n_y, slots - (slots * 7) // 12, piece, w), jnp.float32),
            pltpu.VMEM((n_y, slots - (slots * 7) // 12, piece, w), jnp.float32),
            pltpu.SemaphoreType.DMA((4,)),
            pltpu.SemaphoreType.DMA((n_y,)),
            pltpu.SemaphoreType.DMA((n_y,)),
        ],
        compiler_params=pltpu.CompilerParams(
            collective_id=0, has_side_effects=True, vmem_limit_bytes=60 * 1024 * 1024
        ),
    )(holder, rowblk, picked, activations)


def body(activations, pattern, block_slot):
    tok_rows, width = activations.shape
    feat_count = lax.axis_size("feat")
    tok_count = lax.axis_size("tok")
    my_index = lax.axis_index("feat")
    panel_blocks = width // BLK
    list_length = pattern.shape[0]
    per_device = list_length // feat_count
    scale = 1.0 / (tok_rows * tok_count)
    ordered = jnp.zeros_like(pattern).at[block_slot].set(pattern)
    pairs = ordered.reshape(feat_count, per_device, 2)
    holder = pairs[:, :, 1] // panel_blocks
    local_column = pairs[:, :, 1] % panel_blocks
    picked = jnp.sum(jnp.where(holder == my_index, local_column, 0), axis=1)
    my_pairs = lax.dynamic_index_in_dim(pairs, my_index, 0, keepdims=False)
    my_holder = my_pairs[:, 1] // panel_blocks
    rowblk = my_pairs[:, 0] % panel_blocks
    out = fused(my_holder, rowblk, picked, activations, feat_count, tok_count, scale)
    return out.transpose(1, 0, 2)


def solution(mesh):
    placed = (P("tok", "feat"), P(), P())
    return jax.shard_map(
        body, mesh=mesh, in_specs=placed, out_specs=P("tok", "feat", None), check_vma=False
    )
```

```python
import functools

import jax
import jax.numpy as jnp
from jax import lax
from jax.experimental import pallas as pl
from jax.experimental.pallas import tpu as pltpu
from jax.sharding import PartitionSpec as P

BLK = 512
CHUNKS = 4
MESH = pl.DeviceIdType.MESH


def fused_kernel(n_feat, n_tok, chunks, scale,
                 holder_ref, rowblk_ref, picked_ref, act_hbm, out_ref, *scratch):
    recv = scratch[:chunks]
    (act_ref, send_ref, gbuf, st0, s1buf, st1, s2buf, st2, panel_sem,
     fsend, frecv, flocal, send0, recv0, send1, recv1, send2, recv2,
     bxbuf, bsum, bybuf, bsem, bysend, byrecv) = scratch[chunks:]
    slots = holder_ref.shape[0]
    tokens, width = send_ref.shape[1], send_ref.shape[2]
    panel_blocks = act_ref.shape[0]
    w = width // chunks
    n_y = n_tok // 4
    piece = width // n_tok
    me = lax.axis_index("feat")
    t = lax.axis_index("tok")
    x = t // (2 * n_y)
    y = (t // 2) % n_y
    core = t % 2
    core_peer = t + 1 - 2 * core
    x_peer = t + (1 - 2 * x) * 2 * n_y

    barrier = pltpu.get_barrier_semaphore()
    for k in range(1, n_feat):
        pl.semaphore_signal(barrier, 1, device_id={"feat": lax.rem(me + k, n_feat)}, device_id_type=MESH)
    for o in range(1, n_y):
        dest = x * 2 * n_y + lax.rem(y + o, n_y) * 2 + core
        pl.semaphore_signal(barrier, 1, device_id={"tok": dest}, device_id_type=MESH)
    pl.semaphore_signal(barrier, 1, device_id={"tok": core_peer}, device_id_type=MESH)
    pl.semaphore_signal(barrier, 1, device_id={"tok": x_peer}, device_id_type=MESH)

    panel = [
        pltpu.make_async_copy(act_hbm.at[:, pl.ds(b * width, width)], act_ref.at[b], panel_sem.at[b])
        for b in range(panel_blocks)
    ]
    for cp in panel:
        cp.start()
    for cp in panel:
        cp.wait()
    for p in range(n_feat):
        send_ref[p] = act_ref[picked_ref[p]]

    pl.semaphore_wait(barrier, n_feat - 1 + n_y - 1 + 2)

    def feat_copies(c):
        cols = pl.ds(c * w, w)
        local = pltpu.make_async_copy(send_ref.at[me, :, cols], recv[c].at[me], flocal.at[c])
        copies = []
        for k in sorted(range(1, n_feat), key=lambda k: min(k, n_feat - k)):
            peer = lax.rem(me + k, n_feat)
            copies.append(pltpu.make_async_remote_copy(
                src_ref=send_ref.at[peer, :, cols],
                dst_ref=recv[c].at[me],
                send_sem=fsend.at[c, k],
                recv_sem=frecv.at[c, k],
                device_id={"feat": peer},
                device_id_type=MESH,
            ))
        copies.append(local)
        return copies

    def reduce_last(c, gram_one):
        h = (slots * 7) // 12
        cols = pl.ds(c * w, w)
        cp0a = pltpu.make_async_remote_copy(
            src_ref=gbuf.at[1 - core, :, :, pl.ds(0, h)], dst_ref=st0.at[c, :, :, pl.ds(0, h)],
            send_sem=send0.at[c], recv_sem=recv0.at[c], device_id={"tok": core_peer}, device_id_type=MESH,
        )
        cp0b = pltpu.make_async_remote_copy(
            src_ref=gbuf.at[1 - core, :, :, pl.ds(h, slots - h)],
            dst_ref=st0.at[c, :, :, pl.ds(h, slots - h)],
            send_sem=bsem.at[2], recv_sem=bsem.at[3], device_id={"tok": core_peer}, device_id_type=MESH,
        )
        lax.fori_loop(0, h, gram_one, 0)
        cp0a.start()
        lax.fori_loop(h, slots, gram_one, 0)
        cp0b.start()
        cp0a.wait()
        s1buf[:, :, :h] = gbuf[core, :, :, :h] + st0[c, :, :, :h]
        a_y = []
        for o in range(1, n_y):
            dy = lax.rem(y + o, n_y)
            cp = pltpu.make_async_remote_copy(
                src_ref=s1buf.at[dy, :, pl.ds(0, h)], dst_ref=st1.at[c, y, :, pl.ds(0, h)],
                send_sem=send1.at[c, o], recv_sem=recv1.at[c, o],
                device_id={"tok": x * 2 * n_y + dy * 2 + core}, device_id_type=MESH,
            )
            cp.start()
            a_y.append(cp)
        cp0b.wait()
        s1buf[:, :, h:] = gbuf[core, :, :, h:] + st0[c, :, :, h:]
        b_x = pltpu.make_async_remote_copy(
            src_ref=s1buf.at[:, 1 - x, pl.ds(h, slots - h)], dst_ref=bxbuf,
            send_sem=bsem.at[0], recv_sem=bsem.at[1], device_id={"tok": x_peer}, device_id_type=MESH,
        )
        b_x.start()
        b_x.wait()
        bsum[...] = s1buf[:, x, h:] + bxbuf[...]
        b_y = []
        for o in range(1, n_y):
            dy = lax.rem(y + o, n_y)
            cp = pltpu.make_async_remote_copy(
                src_ref=bsum.at[dy], dst_ref=bybuf.at[y],
                send_sem=bysend.at[o], recv_sem=byrecv.at[o],
                device_id={"tok": x * 2 * n_y + dy * 2 + core}, device_id_type=MESH,
            )
            cp.start()
            b_y.append(cp)
        for cp in a_y:
            cp.wait()
        acc = s1buf[y, :, :h]
        for o in range(1, n_y):
            acc = acc + st1[c, lax.rem(y + o, n_y), :, :h]
        s2buf[:, :h] = acc
        a_x = pltpu.make_async_remote_copy(
            src_ref=s2buf.at[1 - x, pl.ds(0, h)], dst_ref=st2.at[c, pl.ds(0, h)],
            send_sem=send2.at[c], recv_sem=recv2.at[c], device_id={"tok": x_peer}, device_id_type=MESH,
        )
        a_x.start()
        for cp in b_y:
            cp.wait()
        accb = bsum[y]
        for o in range(1, n_y):
            accb = accb + bybuf[lax.rem(y + o, n_y)]
        out_ref[h:, :, cols] = accb
        a_x.wait()
        out_ref[:h, :, cols] = s2buf[x, :h] + st2[c, :h]

    in_flight = []
    for c in range(min(2, chunks)):
        in_flight.append(feat_copies(c))
        for cp in in_flight[-1]:
            cp.start()
    for c in range(chunks):
        for cp in in_flight[c]:
            cp.wait()
        if c + 2 < chunks:
            in_flight.append(feat_copies(c + 2))
            for cp in in_flight[-1]:
                cp.start()

        def gram_one(k, carry):
            q = recv[c][holder_ref[k]]
            p = act_ref[rowblk_ref[k]]
            g = lax.dot_general(
                p, q, (((0,), (0,)), ((), ())), preferred_element_type=jnp.float32
            ) * scale
            for xx in range(2):
                for yy in range(n_y):
                    for cc in range(2):
                        r0 = ((xx * n_y + yy) * 2 + cc) * piece
                        gbuf[cc, yy, xx, k] = g[r0:r0 + piece, :]
            return carry

        if c == chunks - 1 and slots > 1:
            reduce_last(c, gram_one)
            continue

        lax.fori_loop(0, slots, gram_one, 0)

        cp0 = pltpu.make_async_remote_copy(
            src_ref=gbuf.at[1 - core],
            dst_ref=st0.at[c],
            send_sem=send0.at[c],
            recv_sem=recv0.at[c],
            device_id={"tok": core_peer},
            device_id_type=MESH,
        )
        cp0.start()
        cp0.wait()
        s1buf[...] = gbuf[core] + st0[c]

        copies1 = []
        for o in range(1, n_y):
            dy = lax.rem(y + o, n_y)
            cp = pltpu.make_async_remote_copy(
                src_ref=s1buf.at[dy],
                dst_ref=st1.at[c, y],
                send_sem=send1.at[c, o],
                recv_sem=recv1.at[c, o],
                device_id={"tok": x * 2 * n_y + dy * 2 + core},
                device_id_type=MESH,
            )
            cp.start()
            copies1.append(cp)
        for cp in copies1:
            cp.wait()
        acc = s1buf[y]
        for o in range(1, n_y):
            acc = acc + st1[c, lax.rem(y + o, n_y)]
        s2buf[...] = acc

        cp2 = pltpu.make_async_remote_copy(
            src_ref=s2buf.at[1 - x],
            dst_ref=st2.at[c],
            send_sem=send2.at[c],
            recv_sem=recv2.at[c],
            device_id={"tok": x_peer},
            device_id_type=MESH,
        )
        cp2.start()
        cp2.wait()
        out_ref[:, :, pl.ds(c * w, w)] = s2buf[x] + st2[c]


def fused(holder, rowblk, picked, activations, n_feat, n_tok, scale):
    slots = holder.shape[0]
    tokens, width = activations.shape[0], BLK
    panel_blocks = activations.shape[1] // BLK
    w = width // CHUNKS
    n_y = n_tok // 4
    piece = width // n_tok
    kernel = functools.partial(fused_kernel, n_feat, n_tok, CHUNKS, scale)
    blk = (slots, piece, w)
    return pl.pallas_call(
        kernel,
        out_shape=jax.ShapeDtypeStruct((slots, piece, width), jnp.float32),
        in_specs=[
            pl.BlockSpec(memory_space=pltpu.SMEM),
            pl.BlockSpec(memory_space=pltpu.SMEM),
            pl.BlockSpec(memory_space=pltpu.SMEM),
            pl.BlockSpec(memory_space=pl.ANY),
        ],
        out_specs=pl.BlockSpec(memory_space=pltpu.VMEM),
        scratch_shapes=[pltpu.VMEM((n_feat, tokens, w), activations.dtype) for _ in range(CHUNKS)] + [
            pltpu.VMEM((panel_blocks, tokens, width), activations.dtype),
            pltpu.VMEM((n_feat, tokens, width), activations.dtype),
            pltpu.VMEM((2, n_y, 2) + blk, jnp.float32),
            pltpu.VMEM((CHUNKS, n_y, 2) + blk, jnp.float32),
            pltpu.VMEM((n_y, 2) + blk, jnp.float32),
            pltpu.VMEM((CHUNKS, n_y, 2) + blk, jnp.float32),
            pltpu.VMEM((2,) + blk, jnp.float32),
            pltpu.VMEM((CHUNKS,) + blk, jnp.float32),
            pltpu.SemaphoreType.DMA((panel_blocks,)),
            pltpu.SemaphoreType.DMA((CHUNKS, n_feat)),
            pltpu.SemaphoreType.DMA((CHUNKS, n_feat)),
            pltpu.SemaphoreType.DMA((CHUNKS,)),
            pltpu.SemaphoreType.DMA((CHUNKS,)),
            pltpu.SemaphoreType.DMA((CHUNKS,)),
            pltpu.SemaphoreType.DMA((CHUNKS, n_y)),
            pltpu.SemaphoreType.DMA((CHUNKS, n_y)),
            pltpu.SemaphoreType.DMA((CHUNKS,)),
            pltpu.SemaphoreType.DMA((CHUNKS,)),
            pltpu.VMEM((n_y, slots - (slots * 7) // 12, piece, w), jnp.float32),
            pltpu.VMEM((n_y, slots - (slots * 7) // 12, piece, w), jnp.float32),
            pltpu.VMEM((n_y, slots - (slots * 7) // 12, piece, w), jnp.float32),
            pltpu.SemaphoreType.DMA((4,)),
            pltpu.SemaphoreType.DMA((n_y,)),
            pltpu.SemaphoreType.DMA((n_y,)),
        ],
        compiler_params=pltpu.CompilerParams(
            collective_id=0, has_side_effects=True, vmem_limit_bytes=60 * 1024 * 1024
        ),
    )(holder, rowblk, picked, activations)


def body(activations, pattern, block_slot):
    tok_rows, width = activations.shape
    feat_count = lax.axis_size("feat")
    tok_count = lax.axis_size("tok")
    my_index = lax.axis_index("feat")
    panel_blocks = width // BLK
    list_length = pattern.shape[0]
    per_device = list_length // feat_count
    scale = 1.0 / (tok_rows * tok_count)
    ordered = jnp.zeros_like(pattern).at[block_slot].set(pattern)
    pairs = ordered.reshape(feat_count, per_device, 2)
    holder = pairs[:, :, 1] // panel_blocks
    local_column = pairs[:, :, 1] % panel_blocks
    picked = jnp.sum(jnp.where(holder == my_index, local_column, 0), axis=1)
    my_pairs = lax.dynamic_index_in_dim(pairs, my_index, 0, keepdims=False)
    my_holder = my_pairs[:, 1] // panel_blocks
    rowblk = my_pairs[:, 0] % panel_blocks
    out = fused(my_holder, rowblk, picked, activations, feat_count, tok_count, scale)
    return out.transpose(1, 0, 2)


def solution(mesh):
    placed = (P("tok", "feat"), P(), P())
    return jax.shard_map(
        body, mesh=mesh, in_specs=placed, out_specs=P("tok", "feat", None), check_vma=False
    )
```

```python
import functools

import jax
import jax.numpy as jnp
from jax import lax
from jax.experimental import pallas as pl
from jax.experimental.pallas import tpu as pltpu
from jax.sharding import PartitionSpec as P

BLK = 512
CHUNKS = 4
MESH = pl.DeviceIdType.MESH


def fused_kernel(n_feat, n_tok, chunks, scale,
                 holder_ref, rowblk_ref, picked_ref, act_hbm, out_ref, *scratch):
    recv = scratch[:chunks]
    (act_ref, send_ref, gbuf, st0, s1buf, st1, s2buf, st2, panel_sem,
     fsend, frecv, flocal, send0, recv0, send1, recv1, send2, recv2,
     bxbuf, bsum, bybuf, bsem, bysend, byrecv) = scratch[chunks:]
    slots = holder_ref.shape[0]
    tokens, width = send_ref.shape[1], send_ref.shape[2]
    panel_blocks = act_ref.shape[0]
    w = width // chunks
    n_y = n_tok // 4
    piece = width // n_tok
    me = lax.axis_index("feat")
    t = lax.axis_index("tok")
    x = t // (2 * n_y)
    y = (t // 2) % n_y
    core = t % 2
    core_peer = t + 1 - 2 * core
    x_peer = t + (1 - 2 * x) * 2 * n_y

    barrier = pltpu.get_barrier_semaphore()
    for k in range(1, n_feat):
        pl.semaphore_signal(barrier, 1, device_id={"feat": lax.rem(me + k, n_feat)}, device_id_type=MESH)
    for o in range(1, n_y):
        dest = x * 2 * n_y + lax.rem(y + o, n_y) * 2 + core
        pl.semaphore_signal(barrier, 1, device_id={"tok": dest}, device_id_type=MESH)
    pl.semaphore_signal(barrier, 1, device_id={"tok": core_peer}, device_id_type=MESH)
    pl.semaphore_signal(barrier, 1, device_id={"tok": x_peer}, device_id_type=MESH)

    panel = [
        pltpu.make_async_copy(act_hbm.at[:, pl.ds(b * width, width)], act_ref.at[b], panel_sem.at[b])
        for b in range(panel_blocks)
    ]
    for cp in panel:
        cp.start()
    for cp in panel:
        cp.wait()
    for p in range(n_feat):
        send_ref[p] = act_ref[picked_ref[p]]

    pl.semaphore_wait(barrier, n_feat - 1 + n_y - 1 + 2)

    def feat_copies(c):
        cols = pl.ds(c * w, w)
        local = pltpu.make_async_copy(send_ref.at[me, :, cols], recv[c].at[me], flocal.at[c])
        copies = [local]
        for k in sorted(range(1, n_feat), key=lambda k: min(k, n_feat - k) + 2 * (k % 2)):
            peer = lax.rem(me + k, n_feat)
            copies.append(pltpu.make_async_remote_copy(
                src_ref=send_ref.at[peer, :, cols],
                dst_ref=recv[c].at[me],
                send_sem=fsend.at[c, k],
                recv_sem=frecv.at[c, k],
                device_id={"feat": peer},
                device_id_type=MESH,
            ))
        return copies

    def reduce_last(c, gram_one):
        h = (slots * 7) // 12
        cols = pl.ds(c * w, w)
        cp0a = pltpu.make_async_remote_copy(
            src_ref=gbuf.at[1 - core, :, :, pl.ds(0, h)], dst_ref=st0.at[c, :, :, pl.ds(0, h)],
            send_sem=send0.at[c], recv_sem=recv0.at[c], device_id={"tok": core_peer}, device_id_type=MESH,
        )
        cp0b = pltpu.make_async_remote_copy(
            src_ref=gbuf.at[1 - core, :, :, pl.ds(h, slots - h)],
            dst_ref=st0.at[c, :, :, pl.ds(h, slots - h)],
            send_sem=bsem.at[2], recv_sem=bsem.at[3], device_id={"tok": core_peer}, device_id_type=MESH,
        )
        lax.fori_loop(0, h, gram_one, 0)
        cp0a.start()
        lax.fori_loop(h, slots, gram_one, 0)
        cp0b.start()
        cp0a.wait()
        s1buf[:, :, :h] = gbuf[core, :, :, :h] + st0[c, :, :, :h]
        a_y = []
        for o in range(1, n_y):
            dy = lax.rem(y + o, n_y)
            cp = pltpu.make_async_remote_copy(
                src_ref=s1buf.at[dy, :, pl.ds(0, h)], dst_ref=st1.at[c, y, :, pl.ds(0, h)],
                send_sem=send1.at[c, o], recv_sem=recv1.at[c, o],
                device_id={"tok": x * 2 * n_y + dy * 2 + core}, device_id_type=MESH,
            )
            cp.start()
            a_y.append(cp)
        cp0b.wait()
        s1buf[:, :, h:] = gbuf[core, :, :, h:] + st0[c, :, :, h:]
        b_x = pltpu.make_async_remote_copy(
            src_ref=s1buf.at[:, 1 - x, pl.ds(h, slots - h)], dst_ref=bxbuf,
            send_sem=bsem.at[0], recv_sem=bsem.at[1], device_id={"tok": x_peer}, device_id_type=MESH,
        )
        b_x.start()
        b_x.wait()
        bsum[...] = s1buf[:, x, h:] + bxbuf[...]
        b_y = []
        for o in range(1, n_y):
            dy = lax.rem(y + o, n_y)
            cp = pltpu.make_async_remote_copy(
                src_ref=bsum.at[dy], dst_ref=bybuf.at[y],
                send_sem=bysend.at[o], recv_sem=byrecv.at[o],
                device_id={"tok": x * 2 * n_y + dy * 2 + core}, device_id_type=MESH,
            )
            cp.start()
            b_y.append(cp)
        for cp in a_y:
            cp.wait()
        acc = s1buf[y, :, :h]
        for o in range(1, n_y):
            acc = acc + st1[c, lax.rem(y + o, n_y), :, :h]
        s2buf[:, :h] = acc
        a_x = pltpu.make_async_remote_copy(
            src_ref=s2buf.at[1 - x, pl.ds(0, h)], dst_ref=st2.at[c, pl.ds(0, h)],
            send_sem=send2.at[c], recv_sem=recv2.at[c], device_id={"tok": x_peer}, device_id_type=MESH,
        )
        a_x.start()
        for cp in b_y:
            cp.wait()
        accb = bsum[y]
        for o in range(1, n_y):
            accb = accb + bybuf[lax.rem(y + o, n_y)]
        out_ref[h:, :, cols] = accb
        a_x.wait()
        out_ref[:h, :, cols] = s2buf[x, :h] + st2[c, :h]

    in_flight = []
    for c in range(min(2, chunks)):
        in_flight.append(feat_copies(c))
        for cp in in_flight[-1]:
            cp.start()
    for c in range(chunks):
        for cp in in_flight[c]:
            cp.wait()
        if c + 2 < chunks:
            in_flight.append(feat_copies(c + 2))
            for cp in in_flight[-1]:
                cp.start()

        def gram_one(k, carry):
            q = recv[c][holder_ref[k]]
            p = act_ref[rowblk_ref[k]]
            g = lax.dot_general(
                p, q, (((0,), (0,)), ((), ())), preferred_element_type=jnp.float32
            ) * scale
            for xx in range(2):
                for yy in range(n_y):
                    for cc in range(2):
                        r0 = ((xx * n_y + yy) * 2 + cc) * piece
                        gbuf[cc, yy, xx, k] = g[r0:r0 + piece, :]
            return carry

        if c == chunks - 1 and slots > 1:
            reduce_last(c, gram_one)
            continue

        lax.fori_loop(0, slots, gram_one, 0)

        cp0 = pltpu.make_async_remote_copy(
            src_ref=gbuf.at[1 - core],
            dst_ref=st0.at[c],
            send_sem=send0.at[c],
            recv_sem=recv0.at[c],
            device_id={"tok": core_peer},
            device_id_type=MESH,
        )
        cp0.start()
        cp0.wait()
        s1buf[...] = gbuf[core] + st0[c]

        copies1 = []
        for o in range(1, n_y):
            dy = lax.rem(y + o, n_y)
            cp = pltpu.make_async_remote_copy(
                src_ref=s1buf.at[dy],
                dst_ref=st1.at[c, y],
                send_sem=send1.at[c, o],
                recv_sem=recv1.at[c, o],
                device_id={"tok": x * 2 * n_y + dy * 2 + core},
                device_id_type=MESH,
            )
            cp.start()
            copies1.append(cp)
        for cp in copies1:
            cp.wait()
        acc = s1buf[y]
        for o in range(1, n_y):
            acc = acc + st1[c, lax.rem(y + o, n_y)]
        s2buf[...] = acc

        cp2 = pltpu.make_async_remote_copy(
            src_ref=s2buf.at[1 - x],
            dst_ref=st2.at[c],
            send_sem=send2.at[c],
            recv_sem=recv2.at[c],
            device_id={"tok": x_peer},
            device_id_type=MESH,
        )
        cp2.start()
        cp2.wait()
        out_ref[:, :, pl.ds(c * w, w)] = s2buf[x] + st2[c]


def fused(holder, rowblk, picked, activations, n_feat, n_tok, scale):
    slots = holder.shape[0]
    tokens, width = activations.shape[0], BLK
    panel_blocks = activations.shape[1] // BLK
    w = width // CHUNKS
    n_y = n_tok // 4
    piece = width // n_tok
    kernel = functools.partial(fused_kernel, n_feat, n_tok, CHUNKS, scale)
    blk = (slots, piece, w)
    return pl.pallas_call(
        kernel,
        out_shape=jax.ShapeDtypeStruct((slots, piece, width), jnp.float32),
        in_specs=[
            pl.BlockSpec(memory_space=pltpu.SMEM),
            pl.BlockSpec(memory_space=pltpu.SMEM),
            pl.BlockSpec(memory_space=pltpu.SMEM),
            pl.BlockSpec(memory_space=pl.ANY),
        ],
        out_specs=pl.BlockSpec(memory_space=pltpu.VMEM),
        scratch_shapes=[pltpu.VMEM((n_feat, tokens, w), activations.dtype) for _ in range(CHUNKS)] + [
            pltpu.VMEM((panel_blocks, tokens, width), activations.dtype),
            pltpu.VMEM((n_feat, tokens, width), activations.dtype),
            pltpu.VMEM((2, n_y, 2) + blk, jnp.float32),
            pltpu.VMEM((CHUNKS, n_y, 2) + blk, jnp.float32),
            pltpu.VMEM((n_y, 2) + blk, jnp.float32),
            pltpu.VMEM((CHUNKS, n_y, 2) + blk, jnp.float32),
            pltpu.VMEM((2,) + blk, jnp.float32),
            pltpu.VMEM((CHUNKS,) + blk, jnp.float32),
            pltpu.SemaphoreType.DMA((panel_blocks,)),
            pltpu.SemaphoreType.DMA((CHUNKS, n_feat)),
            pltpu.SemaphoreType.DMA((CHUNKS, n_feat)),
            pltpu.SemaphoreType.DMA((CHUNKS,)),
            pltpu.SemaphoreType.DMA((CHUNKS,)),
            pltpu.SemaphoreType.DMA((CHUNKS,)),
            pltpu.SemaphoreType.DMA((CHUNKS, n_y)),
            pltpu.SemaphoreType.DMA((CHUNKS, n_y)),
            pltpu.SemaphoreType.DMA((CHUNKS,)),
            pltpu.SemaphoreType.DMA((CHUNKS,)),
            pltpu.VMEM((n_y, slots - (slots * 7) // 12, piece, w), jnp.float32),
            pltpu.VMEM((n_y, slots - (slots * 7) // 12, piece, w), jnp.float32),
            pltpu.VMEM((n_y, slots - (slots * 7) // 12, piece, w), jnp.float32),
            pltpu.SemaphoreType.DMA((4,)),
            pltpu.SemaphoreType.DMA((n_y,)),
            pltpu.SemaphoreType.DMA((n_y,)),
        ],
        compiler_params=pltpu.CompilerParams(
            collective_id=0, has_side_effects=True, vmem_limit_bytes=60 * 1024 * 1024
        ),
    )(holder, rowblk, picked, activations)


def body(activations, pattern, block_slot):
    tok_rows, width = activations.shape
    feat_count = lax.axis_size("feat")
    tok_count = lax.axis_size("tok")
    my_index = lax.axis_index("feat")
    panel_blocks = width // BLK
    list_length = pattern.shape[0]
    per_device = list_length // feat_count
    scale = 1.0 / (tok_rows * tok_count)
    ordered = jnp.zeros_like(pattern).at[block_slot].set(pattern)
    pairs = ordered.reshape(feat_count, per_device, 2)
    holder = pairs[:, :, 1] // panel_blocks
    local_column = pairs[:, :, 1] % panel_blocks
    picked = jnp.sum(jnp.where(holder == my_index, local_column, 0), axis=1)
    my_pairs = lax.dynamic_index_in_dim(pairs, my_index, 0, keepdims=False)
    my_holder = my_pairs[:, 1] // panel_blocks
    rowblk = my_pairs[:, 0] % panel_blocks
    out = fused(my_holder, rowblk, picked, activations, feat_count, tok_count, scale)
    return out.transpose(1, 0, 2)


def solution(mesh):
    placed = (P("tok", "feat"), P(), P())
    return jax.shard_map(
        body, mesh=mesh, in_specs=placed, out_specs=P("tok", "feat", None), check_vma=False
    )
```
